32 devices in a mesh: dp: 2 (over y), ctx: 4 (over x, core), tp: 4 (over z).
Axes of the slice: x: 2, y: 2, z: 4, core: 2. Of those that a mesh axis runs over, the one named last changes fastest.
Arguments:
- layer_input: bfloat16 [2, 2048, 1024], P('dp', 'ctx'), may hold values from -6 to 6
- cotangent: bfloat16 [2, 2048, 1024], P('dp', 'ctx'), may hold values from -6 to 6
- segment_ids: int32 [2, 2048], P('dp'), may hold values from 0 to 11, never falling along the last dimension, each value on 1 to 1536 neighbouring positions
- norm1_gain: bfloat16 [1024], P(('dp', 'ctx')), may hold values from 0.5 to 1.5
- norm1_bias: bfloat16 [1024], P(('dp', 'ctx')), may hold values from -3 to 3
- attend_weight: bfloat16 [1024, 3, 1024], P(('dp', 'ctx'), None, 'tp'), may hold values from -0.1875 to 0.1875
- attend_bias: bfloat16 [2, 1024], P(None, ('tp', 'dp', 'ctx')), may hold values from -3 to 3
- merge_weight: bfloat16 [1024, 1024], P('tp', ('dp', 'ctx')), may hold values from -0.75 to 0.75
- merge_bias: bfloat16 [1024], P(('dp', 'ctx')), may hold values from -3 to 3
- norm2_gain: bfloat16 [1024], P(('dp', 'ctx')), may hold values from 0.5 to 1.5
- norm2_bias: bfloat16 [1024], P(('dp', 'ctx')), may hold values from -3 to 3
- expand_weight: bfloat16 [1024, 4096], P(('dp', 'ctx'), 'tp'), may hold values from -0.1875 to 0.1875
- expand_bias: bfloat16 [4096], P(('tp', 'dp', 'ctx')), may hold values from -3 to 3
- shrink_weight: bfloat16 [4096, 1024], P('tp', ('dp', 'ctx')), may hold values from -0.09375 to 0.09375
- shrink_bias: bfloat16 [1024], P(('dp', 'ctx')), may hold values from -3 to 3
Outputs:
- layer_output: bfloat16 [2, 2048, 1024], P('dp', 'ctx')
- input_grad: bfloat16 [2, 2048, 1024], P('dp', 'ctx')
- grad_norm1_gain: float32 [1024], P(('dp', 'ctx'))
- grad_norm1_bias: float32 [1024], P(('dp', 'ctx'))
- grad_attend_weight: float32 [1024, 3, 1024], P(('dp', 'ctx'), None, 'tp')
- grad_attend_bias: float32 [2, 1024], P(None, ('tp', 'dp', 'ctx'))
- grad_merge_weight: float32 [1024, 1024], P('tp', ('dp', 'ctx'))
- grad_merge_bias: float32 [1024], P(('dp', 'ctx'))
- grad_norm2_gain: float32 [1024], P(('dp', 'ctx'))
- grad_norm2_bias: float32 [1024], P(('dp', 'ctx'))
- grad_expand_weight: float32 [1024, 4096], P(('dp', 'ctx'), 'tp')
- grad_expand_bias: float32 [4096], P(('tp', 'dp', 'ctx'))
- grad_shrink_weight: float32 [4096, 1024], P('tp', ('dp', 'ctx'))
- grad_shrink_bias: float32 [1024], P(('dp', 'ctx'))
The draws below stay inside these ranges and needn't reach their ends.
Inputs may be any that keep to these rules, and one draw needn't show every extreme that they name: `segment_ids`: within each sequence the segment number never falls; every number 0 to 11 occurs; each holds 1 to 1536 tokens and one holds exactly 1536; segment 0, at the start of a sequence, is padding.
All inputs are finite; a program needn't handle non-finite values.
Results may differ from the reference program's by a relative error of at most 0.02.
Values may be sent and summed in bfloat16 or wider, within the bound.
No kernel may reach another device: no remote copies, remote signals or barrier semaphores. Data moves between devices by JAX's collectives and lax.ppermute only.
A program may use at most 128 MiB of HBM per device.

```python
import math
import jax
import jax.numpy as jnp
import numpy as np
from jax import lax

D = 1024
H = 16
HD = 64
FF = 4096
SEQ_LEN = 2048
DOCS = 12
SEQS = 2


def draw_layer_input(key, part):
    noise_key, topic_key = jax.random.split(jax.random.fold_in(key, 7))
    pieces = 8
    noise = jax.random.normal(noise_key, (SEQS, SEQ_LEN, D), jnp.float32)
    topics = jax.random.normal(topic_key, (SEQS, pieces, 1, D), jnp.float32)
    drawn = noise.reshape(SEQS, pieces, SEQ_LEN // pieces, D) + topics
    return jnp.clip(drawn.reshape(SEQS, SEQ_LEN, D), -6.0, 6.0).astype(jnp.bfloat16)


def block_scale(rng, dims, cuts, smallest, top_value):
    level = 1.0
    for dim, blocks in cuts:
        heights = jax.random.uniform(jax.random.fold_in(jax.random.fold_in(rng, 6), dim), (blocks,), jnp.float32, smallest / len(cuts), top_value / len(cuts))
        level = level * jnp.repeat(jnp.exp(heights), dims[dim] // blocks).reshape((-1,) + (1,) * (len(dims) - 1 - dim))
    return level


def length_profile(count, total, reach, skew):
    portions = [(1 << 20) // math.isqrt(standing ** skew) + 1 for standing in range(2, count + 1)]
    rest, given = total - reach - (count - 1), [1] * (count - 1)
    while rest > 0:
        candidates = [i for i in range(count - 1) if given[i] < reach]
        whole, left = sum([portions[i] for i in candidates]), rest
        for i in candidates:
            extra = min(reach - given[i], max(1, left * portions[i] // whole), rest)
            given[i] = given[i] + extra
            rest = rest - extra
    return np.array([reach] + given)


def uneven(key, amount, total, bound, skew):
    if amount == 2:
        one = jax.random.randint(key, (), max(1, total - bound), min(bound, total - 1) + 1)
        return jnp.stack([one, total - one])
    tallies = jnp.asarray(length_profile(amount, total, bound, skew), jnp.int32)
    couples = (amount - 1) // 2
    donor, taker = tallies[1:1 + 2 * couples:2], tallies[2:2 + 2 * couples:2]
    margin = jnp.minimum(donor - 1, bound - taker)
    moved = jax.random.randint(jax.random.fold_in(key, 1), (couples,), 0, 1 << 20) % (margin + 1)
    tallies = tallies.at[1:1 + 2 * couples:2].set(donor - moved).at[2:2 + 2 * couples:2].set(taker + moved)
    return tallies[jax.random.permutation(jax.random.fold_in(key, 2), amount)]


def centred(own_key, shape, deviation, most, cuts=(), dtype=jnp.bfloat16):
    values = deviation * jax.random.normal(own_key, shape, jnp.float32)
    if cuts:
        values = values * block_scale(own_key, shape, cuts, -0.22, 0.18)
    return jnp.clip(values, -most, most).astype(dtype)


def setup_inputs(seed: int = 0) -> dict:
    seeds = jax.random.split(jax.random.key(seed), 16)
    return {
        "layer_input": draw_layer_input(jax.random.fold_in(seeds[15], 71), 0),
        "cotangent": centred(seeds[1], (SEQS, SEQ_LEN, D), 1.0, 6.0, ((0, 2), (1, 4))),
        "segment_ids": jax.vmap(lambda own: jnp.searchsorted(jnp.cumsum(uneven(own, DOCS, SEQ_LEN, 3 * SEQ_LEN // 4, 2)), jnp.arange(SEQ_LEN), side="right"))(jax.random.split(seeds[2], SEQS)).reshape((SEQS, SEQ_LEN)).astype(jnp.int32),
        "norm1_gain": jnp.clip(1.0 + 0.1 * jax.random.normal(seeds[3], (D,), jnp.float32), 0.5, 1.5).astype(jnp.bfloat16),
        "norm1_bias": centred(seeds[4], (D,), 0.5, 3.0, ((0, 8),)),
        "attend_weight": centred(seeds[5], (D, 3, D), D ** -0.5, 0.1875, ((0, 8), (2, 4))),
        "attend_bias": centred(seeds[6], (2, D), 0.5, 3.0, ((1, 32),)),
        "merge_weight": centred(seeds[7], (D, D), (D // 16) ** -0.5, 0.75, ((0, 4), (1, 8))),
        "merge_bias": centred(seeds[8], (D,), 0.5, 3.0, ((0, 8),)),
        "norm2_gain": jnp.clip(1.0 + 0.1 * jax.random.normal(seeds[9], (D,), jnp.float32), 0.5, 1.5).astype(jnp.bfloat16),
        "norm2_bias": centred(seeds[10], (D,), 0.5, 3.0, ((0, 8),)),
        "expand_weight": centred(seeds[11], (D, FF), D ** -0.5, 0.1875, ((0, 8), (1, 4))),
        "expand_bias": centred(seeds[12], (FF,), 0.5, 3.0, ((0, 32),)),
        "shrink_weight": centred(seeds[13], (FF, D), FF ** -0.5, 0.09375, ((0, 4), (1, 8))),
        "shrink_bias": centred(seeds[14], (D,), 0.5, 3.0, ((0, 8),)),
    }


@jax.custom_vjp
def low(v):
    return lax.optimization_barrier(v.astype(jnp.bfloat16)).astype(jnp.float32)

@jax.custom_vjp
def low_back(v):
    return v

def low_keep(v):
    return (low(v), None)

def low_pass(kept, grad):
    return (grad,)

def back_keep(v):
    return (v, None)

def back_low(kept, grad):
    return (low(grad),)
low.defvjp(low_keep, low_pass)
low_back.defvjp(back_keep, back_low)

def layer_norm(values, gain, bias):
    row_mean = lax.optimization_barrier(jnp.mean(values, axis=-1, keepdims=True))
    centered = values - row_mean
    row_var = lax.optimization_barrier(jnp.mean(centered * centered, axis=-1, keepdims=True))
    return centered * lax.rsqrt(row_var + 1e-05) * gain + bias

def gelu_tanh(values):
    return 0.5 * values * (1.0 + jnp.tanh(0.7978845608028654 * (values + 0.044715 * values * values * values)))

def matmul(left_operand, right_operand):
    return jnp.einsum('izj,jn->izn', left_operand, right_operand, precision=lax.Precision.HIGHEST)

def seq_forward(params, inputs, seg_block):
    norm1_gain, norm1_bias, attend_weight, attend_bias, merge_weight, merge_bias, norm2_gain, norm2_bias, expand_weight, expand_bias, shrink_weight, shrink_bias = params
    seq_count, length, model_width = inputs.shape
    normalized_input = low(layer_norm(inputs, norm1_gain, norm1_bias))
    query = low_back(low(matmul(normalized_input, attend_weight[:, 0]) + attend_bias[0]))
    key_vals = low_back(low(matmul(normalized_input, attend_weight[:, 1])))
    value = low_back(low(matmul(normalized_input, attend_weight[:, 2]) + attend_bias[1]))
    position = jnp.arange(length)
    allowed = (seg_block[:, :, None] == seg_block[:, None, :]) & (position[None, None, :] <= position[None, :, None])
    head_scale_factor = 1.0 / math.sqrt(HD)

    def split_heads(tensor):
        return jnp.moveaxis(tensor.reshape(seq_count, length, H, HD), 2, 0)

    def one_head(pieces):
        query_per_head, key_per_head, value_per_head = pieces
        unnormalized_scores = jnp.einsum('imy,iey->ime', query_per_head, key_per_head, precision=lax.Precision.HIGHEST) * head_scale_factor
        scores = jnp.where(allowed, low_back(unnormalized_scores), -1e+30)
        row_top = lax.optimization_barrier(jnp.max(scores, axis=-1, keepdims=True))
        exp_scores = jnp.exp(scores - row_top)
        softmax_probabilities = low(exp_scores / lax.optimization_barrier(jnp.sum(exp_scores, axis=-1, keepdims=True)))
        return jnp.einsum('jni,jir->jnr', softmax_probabilities, value_per_head, precision=lax.Precision.HIGHEST)
    head_out = lax.map(jax.checkpoint(one_head), (split_heads(query), split_heads(key_vals), split_heads(value)))
    mixed_out = low_back(low(jnp.moveaxis(head_out, 0, 2).reshape(seq_count, length, model_width)))
    attn_out = low_back(matmul(mixed_out, merge_weight))
    hidden = inputs + attn_out + merge_bias
    normed2 = low(layer_norm(hidden, norm2_gain, norm2_bias))
    pre_act = low_back(matmul(normed2, expand_weight) + expand_bias)
    activation = low(gelu_tanh(pre_act))
    mlp_out = low_back(matmul(activation, shrink_weight))
    return hidden + mlp_out + shrink_bias

def reference(layer_input, cotangent, segment_ids, norm1_gain, norm1_bias, attend_weight, attend_bias, merge_weight, merge_bias, norm2_gain, norm2_bias, expand_weight, expand_bias, shrink_weight, shrink_bias):
    params = tuple((array.astype(jnp.float32) for array in (norm1_gain, norm1_bias, attend_weight, attend_bias, merge_weight, merge_bias, norm2_gain, norm2_bias, expand_weight, expand_bias, shrink_weight, shrink_bias)))
    group_size = math.gcd(SEQS, max(1, 4096 // SEQ_LEN))
    num_steps = SEQS // group_size
    keep_mask = (segment_ids > 0).astype(jnp.float32)
    grad_out = cotangent.astype(jnp.float32) * keep_mask[:, :, None]
    inputs_all = layer_input.astype(jnp.float32).reshape(num_steps, group_size, SEQ_LEN, D)
    grads_all = grad_out.reshape(num_steps, group_size, SEQ_LEN, D)
    segs_all = segment_ids.reshape(num_steps, group_size, SEQ_LEN)

    def scan_step(totals, pieces):
        inputs, grad_block, seg_block = pieces
        result, pull_back = jax.vjp(lambda prm, val: seq_forward(prm, val, seg_block), params, inputs)
        grad_params, grad_inputs = pull_back(grad_block)
        totals = jax.tree.map(lambda left_operand, right_operand: left_operand + right_operand, totals, grad_params)
        return (totals, (result, grad_inputs))
    zero_grads = jax.tree.map(jnp.zeros_like, params)
    totals, (results, grad_inputs) = lax.scan(scan_step, zero_grads, (inputs_all, grads_all, segs_all))
    layer_output = results.reshape(SEQS, SEQ_LEN, D).astype(jnp.bfloat16)
    input_grad = grad_inputs.reshape(SEQS, SEQ_LEN, D).astype(jnp.bfloat16)
    return (layer_output, input_grad, totals[0], totals[1], totals[2], totals[3], totals[4], totals[5], totals[6], totals[7], totals[8], totals[9], totals[10], totals[11])
```

```python
import functools
import math

import jax
import jax.numpy as jnp
from jax import lax
from jax.experimental import pallas as pl
from jax.experimental.pallas import tpu as pltpu
from jax.sharding import PartitionSpec as P

HD = 64
NEG = -1e30
F32 = jnp.float32
BF16 = jnp.bfloat16


def dot(left, right, left_dim, right_dim):
    return lax.dot_general(
        left, right, (((left_dim,), (right_dim,)), ((), ())), preferred_element_type=F32
    )


def fwd_kernel(heads,tq,tk,nchunk,q_len, ctx_ref, los_ref, lo_ref, q_ref, *refs):
    kv_refs=refs[:nchunk]
    mixed_ref,lse_ref,qm_ref,acc_ref,m_ref,l_ref=refs[nchunk:]
    width=heads*HD
    ctx=ctx_ref[0]
    lane=lax.broadcasted_iota(jnp.int32,(tq,width),1)
    for qi in range(q_len//tq):
        rows=slice(qi*tq,(qi+1)*tq)
        qv=q_ref[rows,:]*BF16(0.125)
        for h in range(heads):
            qm_ref[h]=jnp.where((lane>=h*HD)&(lane<(h+1)*HD),qv,jnp.zeros_like(qv))
        acc_ref[...]=jnp.zeros_like(acc_ref)
        m_ref[...]=jnp.full(m_ref.shape,NEG,F32)
        l_ref[...]=jnp.zeros_like(l_ref)
        qbase=ctx*q_len+qi*tq
        qpos=qbase+lax.broadcasted_iota(jnp.int32,(1,tq),1)
        lo=lo_ref[0:1,rows]
        lo_first=los_ref[qi]
        for c in range(nchunk):
            kv=kv_refs[c]
            cbase=(ctx^c)*q_len
            def step(ki,carry,kv=kv,cbase=cbase):
                kb=cbase+ki*tk
                @pl.when((kb<=qbase+tq-1)&(kb+tk-1>=lo_first))
                def _():
                    krows=pl.ds(pl.multiple_of(ki*tk,tk),tk)
                    k=kv[krows,0:width]
                    vt=kv[krows,width:2*width].T
                    kpos=kb+lax.broadcasted_iota(jnp.int32,(tk,1),0)
                    ok=(kpos>=lo)&(kpos<=qpos)
                    for h in range(heads):
                        s=dot(k,qm_ref[h],1,1)
                        s=jnp.where(ok,s,NEG)
                        m0=m_ref[h:h+1,:]
                        m1=jnp.maximum(m0,jnp.max(s,axis=0,keepdims=True))
                        p=jnp.exp(s-m1)
                        al=jnp.exp(m0-m1)
                        l_ref[h:h+1,:]=l_ref[h:h+1,:]*al+jnp.sum(p,axis=0,keepdims=True)
                        m_ref[h:h+1,:]=m1
                        hs=slice(h*HD,(h+1)*HD)
                        acc_ref[hs,:]=acc_ref[hs,:]*al+dot(vt[hs,:],p.astype(BF16),1,0)
                return carry
            lax.fori_loop(0,q_len//tk,step,0)
        lse_ref[:,rows]=m_ref[0:heads,:]+jnp.log(l_ref[0:heads,:])
        for h in range(heads):
            hs=slice(h*HD,(h+1)*HD)
            acc_ref[hs,:]=acc_ref[hs,:]/l_ref[h:h+1,:]
        mixed_ref[rows,:]=acc_ref[...].T.astype(BF16)

def attn_fwd(ctx,los,lo,q,kvs,heads,tq=256,tk=256):
    q_len,width=q.shape
    n=len(kvs)
    return pl.pallas_call(
        functools.partial(fwd_kernel,heads,tq,tk,n,q_len),
        out_shape=(jax.ShapeDtypeStruct((q_len,width),BF16),jax.ShapeDtypeStruct((heads,q_len),F32)),
        in_specs=[pl.BlockSpec(memory_space=pltpu.SMEM)]*2+[pl.BlockSpec(memory_space=pltpu.VMEM)]*(2+n),
        out_specs=(pl.BlockSpec(memory_space=pltpu.VMEM),)*2,
        scratch_shapes=[pltpu.VMEM((heads,tq,width),BF16),pltpu.VMEM((width,tq),F32),
                        pltpu.VMEM((8,tq),F32),pltpu.VMEM((8,tq),F32)],
        compiler_params=pltpu.CompilerParams(vmem_limit_bytes=40<<20),
        cost_estimate=pl.CostEstimate(flops=4*q_len*q_len*n*width,bytes_accessed=(2+2*n)*q_len*width*2,transcendentals=heads*q_len*q_len*n),
        name="attention_forward",
    )(ctx,los,lo,q,*kvs)

def bwd_kernel(heads,tq,tk,nchunk,q_len,nz, ctx_ref,z_ref,los_ref,lo_ref,lse_ref,q_ref,mixed_ref,*refs):
    kv_refs=refs[:nchunk]
    gm_refs=refs[nchunk:nchunk+nz]
    dq_ref=refs[nchunk+nz]
    dkv_refs=refs[nchunk+nz+1:nchunk+nz+1+nchunk]
    qm_ref,gom_ref,delta_ref,dqt_ref,go_ref=refs[nchunk+nz+1+nchunk:]
    width=heads*HD
    ctx=ctx_ref[0]
    z=z_ref[0]
    zb=q_len//nz
    for o in range(nz):
        go_ref[pl.ds(pl.multiple_of((z^o)*zb,zb),zb),:]=gm_refs[o][...]
    lane=lax.broadcasted_iota(jnp.int32,(tq,width),1)
    nq=q_len//tq
    hsel=(lax.broadcasted_iota(jnp.int32,(8,width),1)//HD==lax.broadcasted_iota(jnp.int32,(8,width),0)).astype(F32)
    for qi in range(nq):
        rows=slice(qi*tq,(qi+1)*tq)
        qv=q_ref[rows,:]*BF16(0.125)
        gv=go_ref[rows,:]
        for h in range(heads):
            sel=(lane>=h*HD)&(lane<(h+1)*HD)
            qm_ref[h,rows,:]=jnp.where(sel,qv,jnp.zeros_like(qv))
            gom_ref[h,rows,:]=jnp.where(sel,gv,jnp.zeros_like(gv))
        prod=(gv.astype(F32)*mixed_ref[rows,:].astype(F32)).T
        for h in range(heads):
            delta_ref[h:h+1,rows]=jnp.sum(prod[h*HD:(h+1)*HD,:],axis=0,keepdims=True)
    dqt_ref[...]=jnp.zeros_like(dqt_ref)
    for c in range(nchunk):
        kv=kv_refs[c]
        dkv=dkv_refs[c]
        cbase=(ctx^c)*q_len
        def step(ki,carry,kv=kv,dkv=dkv,cbase=cbase):
            kb=cbase+ki*tk
            krows=pl.ds(pl.multiple_of(ki*tk,tk),tk)
            live=[(kb<=ctx*q_len+(qi+1)*tq-1)&(kb+tk-1>=los_ref[qi]) for qi in range(nq)]
            anylive=functools.reduce(jnp.logical_or,live)
            @pl.when(jnp.logical_not(anylive))
            def _():
                dkv[krows,:]=jnp.zeros((tk,2*width),BF16)
            @pl.when(anylive)
            def _():
                def inner(acck_ref,accv_ref):
                    acck_ref[...]=jnp.zeros_like(acck_ref)
                    accv_ref[...]=jnp.zeros_like(accv_ref)
                    k=kv[krows,0:width]
                    v=kv[krows,width:2*width]
                    kt=k.T
                    kpos=kb+lax.broadcasted_iota(jnp.int32,(tk,1),0)
                    for qi in range(nq):
                        @pl.when(live[qi])
                        def _(qi=qi):
                            rows=slice(qi*tq,(qi+1)*tq)
                            qpos=ctx*q_len+qi*tq+lax.broadcasted_iota(jnp.int32,(1,tq),1)
                            ok=(kpos>=lo_ref[0:1,rows])&(kpos<=qpos)
                            dk=acck_ref[...]
                            dv=accv_ref[...]
                            for h in range(heads):
                                qh=qm_ref[h,rows,:]
                                gh=gom_ref[h,rows,:]
                                s=dot(k,qh,1,1)
                                p=jnp.where(ok,jnp.exp(s-lse_ref[h:h+1,rows]),0.0)
                                dp=dot(v,gh,1,1)
                                ds=(p*(dp-delta_ref[h:h+1,rows])).astype(BF16)
                                dv=dv+dot(p.astype(BF16),gh,1,0)
                                dk=dk+dot(ds,qh,1,0)
                                hs=slice(h*HD,(h+1)*HD)
                                dqt_ref[hs,rows]=dqt_ref[hs,rows]+dot(kt[hs,:],ds,1,0)
                            acck_ref[...]=dk
                            accv_ref[...]=dv
                    dkv[krows,0:width]=acck_ref[...].astype(BF16)
                    dkv[krows,width:2*width]=accv_ref[...].astype(BF16)
                pl.run_scoped(inner,pltpu.VMEM((tk,width),F32),pltpu.VMEM((tk,width),F32))
            return carry
        lax.fori_loop(0,q_len//tk,step,0)
    for qi in range(nq):
        rows=slice(qi*tq,(qi+1)*tq)
        dq_ref[rows,:]=(dqt_ref[:,rows].T*0.125).astype(BF16)

def attn_bwd(ctx,z,los,lo,lse,q,mixed,kvs,gms,heads,tq=256,tk=256):
    q_len,width=q.shape
    n=len(kvs); nz=len(gms)
    V=pl.BlockSpec(memory_space=pltpu.VMEM)
    S=pl.BlockSpec(memory_space=pltpu.SMEM)
    return pl.pallas_call(
        functools.partial(bwd_kernel,heads,tq,tk,n,q_len,nz),
        out_shape=(jax.ShapeDtypeStruct((q_len,width),BF16),)+(jax.ShapeDtypeStruct((q_len,2*width),BF16),)*n,
        in_specs=[S]*3+[V]*(4+n+nz),
        out_specs=(V,)*(1+n),
        scratch_shapes=[pltpu.VMEM((heads,q_len,width),BF16),pltpu.VMEM((heads,q_len,width),BF16),
                        pltpu.VMEM((8,q_len),F32),pltpu.VMEM((width,q_len),F32),pltpu.VMEM((q_len,width),BF16)],
        compiler_params=pltpu.CompilerParams(vmem_limit_bytes=48<<20),
        cost_estimate=pl.CostEstimate(flops=10*q_len*q_len*n*width,bytes_accessed=(4+4*n)*q_len*width*2,transcendentals=heads*q_len*q_len*n),
        name="attention_backward",
    )(ctx,z,los,lo,lse,q,mixed,*kvs,*gms)


def norm_stats(values):
    mean = jnp.mean(values, axis=-1, keepdims=True)
    centered = values - mean
    inv_std = lax.rsqrt(jnp.mean(centered * centered, axis=-1, keepdims=True) + 1e-05)
    return centered * inv_std, inv_std


def norm_backward(grad_out, normal, inv_std, gain):
    grad_normal = grad_out * gain
    centered = grad_normal - jnp.mean(grad_normal, axis=-1, keepdims=True)
    return inv_std * (
        centered - normal * jnp.mean(grad_normal * normal, axis=-1, keepdims=True)
    )


def gelu_tanh(values):
    return (
        0.5
        * values
        * (1.0 + jnp.tanh(0.7978845608028654 * (values + 0.044715 * values * values * values)))
    )


def column_kernel(order, width, back, index_ref, x_ref, out_ref):
    index = index_ref[0]
    for place, offset in enumerate(order):
        moved = pl.ds(pl.multiple_of((index ^ offset) * width, width), width)
        plain = slice(place * width, (place + 1) * width)
        if back:
            out_ref[:, moved] = x_ref[:, plain]
        else:
            out_ref[:, plain] = x_ref[:, moved]


def row_kernel(count, height, index_ref, *refs):
    index = index_ref[0]
    for offset in range(count):
        start = pl.multiple_of((index ^ offset) * height, height)
        refs[count][pl.ds(start, height), :] = refs[offset][...]


def place_rows(index, parts):
    count, (height, width) = len(parts), parts[0].shape
    return pl.pallas_call(
        functools.partial(row_kernel, count, height),
        out_shape=jax.ShapeDtypeStruct((count * height, width), parts[0].dtype),
        in_specs=[pl.BlockSpec(memory_space=pltpu.SMEM)]
        + [pl.BlockSpec(memory_space=pltpu.VMEM)] * count,
        out_specs=pl.BlockSpec(memory_space=pltpu.VMEM),
        cost_estimate=pl.CostEstimate(
            flops=0, transcendentals=0, bytes_accessed=4 * count * height * width
        ),
        name="place_rows",
    )(index, *parts)


def body(
    sizes,
    layer_input,
    cotangent,
    segment_ids,
    norm1_gain,
    norm1_bias,
    attend_weight,
    attend_bias,
    merge_weight,
    merge_bias,
    norm2_gain,
    norm2_bias,
    expand_weight,
    expand_bias,
    shrink_weight,
    shrink_bias,
):
    n_dp, n_ctx, n_tp = sizes
    group = n_dp * n_ctx
    order = list(range(0, group, 2)) + list(range(1, group, 2))
    half = group // 2
    ctx = lax.axis_index("ctx")
    tp = lax.axis_index("tp")
    me = lax.axis_index("dp") * n_ctx + ctx
    me_ref, ctx_ref, tp_ref = (jnp.reshape(v, (1,)).astype(jnp.int32) for v in (me, ctx, tp))
    blocks = jnp.array(order, jnp.int32) ^ me

    def plane_swap(value, offset):
        return lax.ppermute(value, ("dp", "ctx"), [(i, i ^ offset) for i in range(group)])

    def ctx_swap(value, offset):
        return lax.ppermute(value, "ctx", [(i, i ^ offset) for i in range(n_ctx)])

    def tp_swap(value, offset):
        return lax.ppermute(value, "tp", [(i, i ^ offset) for i in range(n_tp)])

    def plane_gather(value):
        if group > 8:
            every = lax.all_gather(value, ("dp", "ctx"), axis=0)
            return [lax.dynamic_index_in_dim(every, me ^ o, 0, False) for o in order]
        even = [value] + [plane_swap(value, o) for o in order[1:half]]
        return even + [ctx_swap(v, 1) for v in even]

    def plane_scatter(value):
        rows = value.shape[0] // group
        if group > 8:
            whole = jnp.reshape(value, (group, rows, value.shape[1]))
            place = jnp.argsort(blocks)
            whole = jnp.reshape(jnp.take(whole, place, axis=0), value.shape)
            return lax.psum_scatter(
                whole, ("dp", "ctx"), scatter_dimension=0, tiled=True
            ).astype(F32)
        near = value[: half * rows].astype(F32)
        pair = near + ctx_swap(value[half * rows :], 1).astype(F32)
        total = pair[:rows]
        sent = pair.astype(value.dtype)
        for place in range(1, half):
            part = sent[place * rows : (place + 1) * rows]
            total = total + plane_swap(part, order[place]).astype(F32)
        return total

    def tp_gather(value):
        return [value] + [tp_swap(value, o) for o in range(1, n_tp)]

    def tp_scatter(parts):
        total = parts[0].astype(F32)
        for o in range(1, n_tp):
            total = total + tp_swap(parts[o].astype(BF16), o).astype(F32)
        return total

    def columns(value, back=False):
        height, wide = value.shape
        width = wide // group
        if width % 128:
            source = jnp.argsort(blocks) if back else blocks
            return jnp.reshape(
                jnp.take(jnp.reshape(value, (height, group, width)), source, axis=1),
                value.shape,
            )
        return pl.pallas_call(
            functools.partial(column_kernel, order, width, back),
            out_shape=jax.ShapeDtypeStruct(value.shape, value.dtype),
            in_specs=[
                pl.BlockSpec(memory_space=pltpu.SMEM),
                pl.BlockSpec(memory_space=pltpu.VMEM),
            ],
            out_specs=pl.BlockSpec(memory_space=pltpu.VMEM),
            cost_estimate=pl.CostEstimate(
                flops=0, transcendentals=0, bytes_accessed=4 * height * wide
            ),
            name="order_columns",
        )(me_ref, value)

    def row_block(value, offset):
        height = value.shape[0] // n_tp
        return lax.dynamic_slice_in_dim(value, (tp ^ offset) * height, height, 0)

    assert layer_input.shape[0] == 1
    q_len, model_width = layer_input.shape[1:]
    length = segment_ids.shape[1]
    width = attend_weight.shape[2]
    heads = width // HD
    block = model_width // group
    row_count = q_len // n_tp
    bias_block = expand_bias.shape[0]
    head_block = attend_bias.shape[1]
    small_width = max(block, bias_block, 2 * head_block)
    select = (blocks[None, :] == jnp.arange(group)[:, None]).astype(F32)

    def small_row(value, wide):
        flat = jnp.reshape(value, (1, -1))
        return jnp.pad(flat, ((0, 0), (0, wide - flat.shape[1])))

    smalls = (
        norm1_gain,
        norm1_bias,
        merge_bias,
        norm2_gain,
        norm2_bias,
        shrink_bias,
        expand_bias,
        attend_bias,
    )
    pack = jnp.concatenate(
        [jnp.reshape(attend_weight, (block, 3 * width))]
        + [small_row(v, 3 * width) for v in smalls],
        axis=0,
    )
    first = plane_gather(pack)
    merge_rows = jnp.concatenate(tp_gather(merge_weight.T), axis=1)
    merge_full = jnp.concatenate(plane_gather(merge_rows), axis=0)
    dense = plane_gather(jnp.concatenate([expand_weight, shrink_weight.T], axis=0))
    expand_full = jnp.concatenate([v[:block] for v in dense], axis=0)
    shrink_full = jnp.concatenate([v[block:] for v in dense], axis=0)
    query_weight = jnp.concatenate([v[:block, :width] for v in first], axis=0)
    pair_weight = jnp.concatenate([v[:block, width:] for v in first], axis=0)
    table = jnp.stack([v[block : block + 8, :small_width] for v in first], axis=0).astype(F32)
    wide_rows = jnp.reshape(jnp.swapaxes(table[:, :6, :block], 0, 1), (6, model_width))
    gain_one, bias_one, merge_add, gain_two, bias_two, shrink_add = (
        wide_rows[i : i + 1] for i in range(6)
    )
    ordered = jnp.einsum("jo,orw->jrw", select, table[:, 6:], precision="highest")
    expand_add = jnp.reshape(ordered[:, 0, :bias_block], (1, -1))
    attend_add = jnp.reshape(
        jnp.swapaxes(jnp.reshape(ordered[:, 1, : 2 * head_block], (group, 2, head_block)), 0, 1),
        (2, width),
    )

    seg_all = segment_ids[0]
    seg_query = lax.dynamic_slice_in_dim(seg_all, ctx * q_len, q_len, 0)
    lows = jnp.sum(
        (seg_all[:, None] < seg_query[None, :]).astype(jnp.int32), axis=0, keepdims=True
    )
    tile = 256
    tile_lows = lows[0, ::tile]

    inputs = columns(layer_input[0])
    normal_one, _ = norm_stats(inputs.astype(F32))
    normed1 = (normal_one * gain_one + bias_one).astype(BF16)
    pair_bias = jnp.concatenate([jnp.zeros((1, width), F32), attend_add[1:2]], axis=1)
    pair = (dot(normed1, pair_weight, 1, 0) + pair_bias).astype(BF16)
    query = (dot(normed1, query_weight, 1, 0) + attend_add[0:1]).astype(BF16)
    near = [pair] + [ctx_swap(pair, o) for o in range(2, n_ctx, 2)]
    pairs = [None] * n_ctx
    for i, value in enumerate(near):
        pairs[2 * i] = value
        pairs[2 * i + 1] = ctx_swap(value, 1)
    mixed, lse = attn_fwd(ctx_ref, tile_lows, lows, query, pairs, heads, tile, tile)
    mixed_rows = jnp.concatenate(
        [row_block(mixed, 0)] + [tp_swap(row_block(mixed, o), o) for o in range(1, n_tp)],
        axis=1,
    )
    input_rows = row_block(inputs, 0).astype(F32)
    hidden = input_rows + dot(mixed_rows, merge_full, 1, 1) + merge_add

    normal_two, inv_two = norm_stats(hidden)
    normed2 = jnp.concatenate(
        tp_gather((normal_two * gain_two + bias_two).astype(BF16)), axis=0
    )
    pre_act = dot(normed2, expand_full, 1, 0) + expand_add
    act_value, gelu_pull = jax.vjp(gelu_tanh, pre_act)
    activation = act_value.astype(BF16)
    keep = (seg_query > 0).astype(BF16)
    grad_all = columns(cotangent[0]) * keep[:, None]
    grad_y = jnp.concatenate([row_block(grad_all, o) for o in range(n_tp)], axis=0)
    grad_act = dot(grad_y, shrink_full, 1, 0)
    grad_pre = gelu_pull(grad_act)[0].astype(BF16)
    part = dot(grad_pre, expand_full, 1, 1).astype(BF16)
    cut = [slice(o * row_count, (o + 1) * row_count) for o in range(n_tp)]
    grad_normed2 = tp_scatter([part[c] for c in cut])
    grad_rows = grad_y[:row_count].astype(F32)
    grad_hidden = grad_rows + norm_backward(grad_normed2, normal_two, inv_two, gain_two)
    grad_attn = grad_hidden.astype(BF16)
    grad_mixed = dot(grad_attn, merge_full, 1, 0).astype(BF16)
    grad_mixed_rows = [grad_mixed[:, :width]] + [
        tp_swap(grad_mixed[:, o * width : (o + 1) * width], o) for o in range(1, n_tp)
    ]
    grad_expand = plane_scatter(dot(normed2, grad_pre, 0, 0).astype(BF16))
    grad_shrink = plane_scatter(dot(grad_y, activation, 0, 0).astype(BF16)).T
    mlp_part = dot(activation, shrink_full, 1, 1).astype(BF16)
    mlp_out = tp_scatter([mlp_part[c] for c in cut])
    layer_rows = (hidden + mlp_out + shrink_add).astype(BF16)
    layer_output = place_rows(tp_ref, tp_gather(columns(layer_rows, True)))

    grad_merge = plane_scatter(dot(grad_attn, mixed_rows, 0, 0).astype(BF16)).astype(BF16)
    grad_merge = tp_scatter([grad_merge[:, o * width : (o + 1) * width] for o in range(n_tp)]).T

    grads = attn_bwd(
        ctx_ref, tp_ref, tile_lows, lows, lse, query, mixed, pairs, grad_mixed_rows, heads, tile, tile
    )
    grad_query, grad_pairs = grads[0], grads[1:]
    joined = [
        (grad_pairs[o].astype(F32) + ctx_swap(grad_pairs[o + 1], 1).astype(F32))
        for o in range(0, n_ctx, 2)
    ]
    grad_pair = joined[0]
    for i in range(1, n_ctx // 2):
        grad_pair = grad_pair + ctx_swap(joined[i].astype(BF16), 2 * i).astype(F32)
    grad_pair = grad_pair.astype(BF16)
    part = (dot(grad_query, query_weight, 1, 1) + dot(grad_pair, pair_weight, 1, 1)).astype(BF16)
    grad_normed1 = tp_scatter([row_block(part, o) for o in range(n_tp)])
    normal_rows, inv_rows = norm_stats(input_rows)
    input_grad = (
        grad_hidden + norm_backward(grad_normed1, normal_rows, inv_rows, gain_one)
    ).astype(BF16)
    input_grad = place_rows(tp_ref, tp_gather(columns(input_grad, True)))
    grad_proj = jnp.concatenate([grad_query, grad_pair], axis=1)
    grad_attend = plane_scatter(dot(normed1, grad_proj, 0, 0).astype(BF16))
    grad_attend = jnp.reshape(grad_attend, (block, 3, width))

    def token_sum(value):
        return jnp.sum(value, axis=0, keepdims=True)

    wide = jnp.concatenate(
        [
            token_sum(grad_normed1 * normal_rows),
            token_sum(grad_normed1),
            token_sum(grad_hidden),
            token_sum(grad_normed2 * normal_two),
            token_sum(grad_normed2),
            token_sum(grad_rows),
        ],
        axis=0,
    )
    wide = jnp.swapaxes(jnp.reshape(wide, (6, group, block)), 0, 1)
    wide = jnp.pad(wide, ((0, 0), (0, 0), (0, small_width - block)))
    expand_sum = jnp.reshape(token_sum(grad_pre.astype(F32)), (group, bias_block))
    expand_sum = jnp.pad(expand_sum, ((0, 0), (0, small_width - bias_block)))
    attend_sum = jnp.concatenate(
        [token_sum(grad_query.astype(F32)), token_sum(grad_pair[:, width:].astype(F32))], axis=0
    )
    attend_sum = jnp.swapaxes(jnp.reshape(attend_sum, (2, group, head_block)), 0, 1)
    attend_sum = jnp.reshape(attend_sum, (group, 2 * head_block))
    attend_sum = jnp.pad(attend_sum, ((0, 0), (0, small_width - 2 * head_block)))
    local = jnp.einsum(
        "jo,jrw->orw", select, jnp.stack([expand_sum, attend_sum], axis=1), precision="highest"
    )
    table = jnp.concatenate([wide, local], axis=1)
    table = plane_scatter(jnp.reshape(table, (group * 8, small_width)))
    over_tp = table
    for o in range(1, n_tp):
        over_tp = over_tp + tp_swap(table, o)
    return (
        layer_output[None],
        input_grad[None],
        over_tp[0, :block],
        over_tp[1, :block],
        grad_attend,
        jnp.reshape(table[7, : 2 * head_block], (2, head_block)),
        grad_merge,
        over_tp[2, :block],
        over_tp[3, :block],
        over_tp[4, :block],
        grad_expand,
        table[6, :bias_block],
        grad_shrink,
        over_tp[5, :block],
    )


def solution(mesh):
    sizes = (mesh.shape["dp"], mesh.shape["ctx"], mesh.shape["tp"])
    return jax.shard_map(
        functools.partial(body, sizes),
        mesh=mesh,
        in_specs=(
            P("dp", "ctx", None),
            P("dp", "ctx", None),
            P("dp", None),
            P(("dp", "ctx")),
            P(("dp", "ctx")),
            P(("dp", "ctx"), None, "tp"),
            P(None, ("tp", "dp", "ctx")),
            P("tp", ("dp", "ctx")),
            P(("dp", "ctx")),
            P(("dp", "ctx")),
            P(("dp", "ctx")),
            P(("dp", "ctx"), "tp"),
            P(("tp", "dp", "ctx")),
            P("tp", ("dp", "ctx")),
            P(("dp", "ctx")),
        ),
        out_specs=(
            P("dp", "ctx", None),
            P("dp", "ctx", None),
            P(("dp", "ctx")),
            P(("dp", "ctx")),
            P(("dp", "ctx"), None, "tp"),
            P(None, ("tp", "dp", "ctx")),
            P("tp", ("dp", "ctx")),
            P(("dp", "ctx")),
            P(("dp", "ctx")),
            P(("dp", "ctx")),
            P(("dp", "ctx"), "tp"),
            P(("tp", "dp", "ctx")),
            P("tp", ("dp", "ctx")),
            P(("dp", "ctx")),
        ),
        check_vma=False,
    )
```

```python
import functools

import jax
import jax.numpy as jnp
from jax import lax
from jax.experimental import pallas as pl
from jax.experimental.pallas import tpu as pltpu
from jax.sharding import PartitionSpec as P

HD = 64
NEG = -1e30
F32 = jnp.float32
BF16 = jnp.bfloat16


def dot(left, right, left_dim, right_dim):
    return lax.dot_general(
        left, right, (((left_dim,), (right_dim,)), ((), ())), preferred_element_type=F32
    )


def shape(dims, dtype):
    return jax.ShapeDtypeStruct(tuple(dims), dtype)


def call(kernel, name, scalars, ins, outs, scratch=(), flops=0):
    first = [] if scalars is None else [scalars]
    specs, arrays, moved = [], [], 0
    for value in ins:
        if isinstance(value, tuple):
            value, dims, index = value
            specs.append(pl.BlockSpec(dims, lambda i, index=index: index))
            moved += value.dtype.itemsize * functools.reduce(lambda a, b: a * b, dims)
        else:
            specs.append(pl.BlockSpec(memory_space=pltpu.VMEM))
            moved += value.size * value.dtype.itemsize
        arrays.append(value)
    moved += sum(v.size * v.dtype.itemsize for v in outs)
    return pl.pallas_call(
        kernel,
        grid=(1,),
        out_shape=tuple(outs),
        in_specs=[pl.BlockSpec(memory_space=pltpu.SMEM)] * len(first) + specs,
        out_specs=(pl.BlockSpec(memory_space=pltpu.VMEM),) * len(outs),
        scratch_shapes=list(scratch),
        compiler_params=pltpu.CompilerParams(vmem_limit_bytes=56 << 20),
        cost_estimate=pl.CostEstimate(
            flops=flops, transcendentals=0, bytes_accessed=moved
        ),
        name=name,
    )(*first, *arrays)


def lanes(index, offset, size):
    return pl.ds(pl.multiple_of((index ^ offset) * size, size), size)


def rows_of(refs, low, high):
    return jnp.concatenate([ref[low:high, :] for ref in refs], axis=0)


def pack_kernel(attend_ref, *refs):
    smalls, (pair_ref, out_ref) = refs[:-2], refs[-2:]
    parts, block, width = attend_ref.shape
    for c in range(parts):
        out_ref[:block, c * width : (c + 1) * width] = attend_ref[c]
    size = smalls[0].shape[1]
    last = jnp.concatenate([pair_ref[0:1, :], pair_ref[1:2, :]], axis=1).astype(F32)
    last = jnp.concatenate([last, jnp.zeros((1, size - last.shape[1]), F32)], axis=1)
    rows = jnp.concatenate([ref[...].astype(F32) for ref in smalls] + [last], axis=0)
    out_ref[block:, :size] = rows.astype(BF16)
    out_ref[block:, size:] = jnp.zeros((8, parts * width - size), BF16)


def turn_kernel(expand_ref, shrink_ref, *refs):
    parts, out_ref = refs[:-1], refs[-1]
    block = expand_ref.shape[0]
    out_ref[:block, :] = expand_ref[...]
    out_ref[block : 2 * block, :] = shrink_ref[...].T
    width = parts[0].shape[0]
    for o, ref in enumerate(parts):
        out_ref[2 * block :, o * width : (o + 1) * width] = ref[...].T


def decode(order, head_block, index, first, start, size, wide_ref, expand_ref, attend_ref):
    total = jnp.zeros(attend_ref.shape, F32)
    for place, offset in enumerate(order):
        rows = first[place][start : start + 8, :size].astype(F32)
        wide_ref[:, place * size : (place + 1) * size] = rows
        expand_ref[:, lanes(index, offset, size)] = rows[6:7, :]
        flat = jnp.concatenate([rows[7:8, :head_block], rows[7:8, head_block : 2 * head_block]], 0)
        flat = jnp.concatenate(
            [flat, jnp.zeros((2, attend_ref.shape[1] - head_block), F32)], axis=1
        )
        flat = jnp.concatenate([flat, jnp.zeros((6, attend_ref.shape[1]), F32)], axis=0)
        total = total + pltpu.roll(flat, (index ^ offset) * head_block, 1)[:2]
    attend_ref[...] = total


def grad_order_kernel(order, count, scalars, cot_ref, keep_ref, *outs):
    index, tp = scalars[0], scalars[2]
    height, wide = outs[0].shape
    size = wide // len(order)
    for o in range(count):
        rows = pl.ds(pl.multiple_of((tp ^ o) * height, height), height)
        keep = keep_ref[rows, 0:1]
        for place, offset in enumerate(order):
            outs[o][:, place * size : (place + 1) * size] = (
                cot_ref[rows, lanes(index, offset, size)] * keep
            )


def project_kernel(order, block, head_block, scalars, x_ref, *refs):
    count = len(order)
    weights, refs = refs[:count], refs[count:]
    given, outs = refs[:-7], refs[-7:]
    normed_ref, query_ref, pair_ref, rows_ref = outs[:4]
    wide_ref, expand_ref, attend_ref = outs[4:]
    index, tp = scalars[0], scalars[2]
    q_len, wide = x_ref.shape
    size = wide // count
    for source, target in zip(given, outs[4:]):
        target[...] = source[...]
    if not given:
        decode(order, head_block, index, weights, block, size, wide_ref, expand_ref, attend_ref)
    width = query_ref.shape[1]
    weight = rows_of(weights, 0, block)
    step = min(q_len, 256)
    bias = jnp.concatenate(
        [attend_ref[0:1, :], jnp.zeros((1, width), F32), attend_ref[1:2, :]], axis=1
    )
    for start in range(0, q_len, step):
        rows = slice(start, start + step)
        value = x_ref[rows, :].astype(F32)
        mean = jnp.mean(value, axis=-1, keepdims=True)
        centered = value - mean
        inv = lax.rsqrt(jnp.mean(centered * centered, axis=-1, keepdims=True) + 1e-05)
        for place, offset in enumerate(order):
            plain = slice(place * size, (place + 1) * size)
            part = x_ref[rows, lanes(index, offset, size)].astype(F32)
            part = (part - mean) * inv * wide_ref[0:1, plain] + wide_ref[1:2, plain]
            normed_ref[rows, plain] = part.astype(BF16)
        made = dot(normed_ref[rows, :], weight, 1, 0) + bias
        query_ref[rows, :] = made[:, :width].astype(BF16)
        pair_ref[rows, :] = made[:, width:].astype(BF16)
    height = rows_ref.shape[0]
    mine = pl.ds(pl.multiple_of(tp * height, height), height)
    for place, offset in enumerate(order):
        plain = slice(place * size, (place + 1) * size)
        rows_ref[:, plain] = x_ref[mine, lanes(index, offset, size)]


def attend_kernel(heads, tq, tk, n_chunk, n_tp, scalars, lo_ref, q_ref, *refs):
    kv_refs = refs[:n_chunk]
    outs, refs = refs[n_chunk : n_chunk + n_tp], refs[n_chunk + n_tp :]
    lse_ref, qm_ref, acc_ref, m_ref, l_ref, mixed_ref = refs
    q_len, width = q_ref.shape
    ctx = scalars[1]
    lane = lax.broadcasted_iota(jnp.int32, (tq, width), 1)
    for qi in range(q_len // tq):
        rows = slice(qi * tq, (qi + 1) * tq)
        qv = q_ref[rows, :] * BF16(0.125)
        for h in range(heads):
            mine = (lane >= h * HD) & (lane < (h + 1) * HD)
            qm_ref[h] = jnp.where(mine, qv, jnp.zeros_like(qv))
        acc_ref[...] = jnp.zeros_like(acc_ref)
        m_ref[...] = jnp.full(m_ref.shape, NEG, F32)
        l_ref[...] = jnp.zeros_like(l_ref)
        qbase = ctx * q_len + qi * tq
        qpos = qbase + lax.broadcasted_iota(jnp.int32, (1, tq), 1)
        lo = lo_ref[0:1, rows]
        lo_first = scalars[3 + qi]
        for c in range(n_chunk):
            kv = kv_refs[c]
            cbase = (ctx ^ c) * q_len

            def step(ki, carry, kv=kv, cbase=cbase):
                kb = cbase + ki * tk

                @pl.when((kb <= qbase + tq - 1) & (kb + tk - 1 >= lo_first))
                def _():
                    krows = pl.ds(pl.multiple_of(ki * tk, tk), tk)
                    k = kv[krows, 0:width]
                    vt = kv[krows, width : 2 * width].T
                    kpos = kb + lax.broadcasted_iota(jnp.int32, (tk, 1), 0)
                    ok = (kpos >= lo) & (kpos <= qpos)
                    for h in range(heads):
                        s = jnp.where(ok, dot(k, qm_ref[h], 1, 1), NEG)
                        m0 = m_ref[h : h + 1, :]
                        m1 = jnp.maximum(m0, jnp.max(s, axis=0, keepdims=True))
                        p = jnp.exp(s - m1)
                        al = jnp.exp(m0 - m1)
                        l_ref[h : h + 1, :] = l_ref[h : h + 1, :] * al + jnp.sum(
                            p, axis=0, keepdims=True
                        )
                        m_ref[h : h + 1, :] = m1
                        hs = slice(h * HD, (h + 1) * HD)
                        acc_ref[hs, :] = acc_ref[hs, :] * al + dot(
                            vt[hs, :], p.astype(BF16), 1, 0
                        )

                return carry

            lax.fori_loop(0, q_len // tk, step, 0)
        lse_ref[:, rows] = m_ref[0:heads, :] + jnp.log(l_ref[0:heads, :])
        for h in range(heads):
            hs = slice(h * HD, (h + 1) * HD)
            acc_ref[hs, :] = acc_ref[hs, :] / l_ref[h : h + 1, :]
        mixed_ref[rows, :] = acc_ref[...].T.astype(BF16)
    for o in range(n_tp):
        outs[o][...] = mixed_ref[lanes(scalars[2], o, q_len // n_tp), :]


def attend_back_kernel(heads, tq, tk, n_chunk, n_tp, scalars, lo_ref, lse_ref, q_ref, *refs):
    kv_refs, refs = refs[:n_chunk], refs[n_chunk:]
    mixed_refs, refs = refs[:n_tp], refs[n_tp:]
    gm_refs, refs = refs[:n_tp], refs[n_tp:]
    dq_ref, refs = refs[0], refs[1:]
    dkv_refs, refs = refs[:n_chunk], refs[n_chunk:]
    qm_ref, gom_ref, dqt_ref, acck_ref, accv_ref, go_ref, mixed_ref = refs
    q_len, width = q_ref.shape
    ctx, tp = scalars[1], scalars[2]
    for o in range(n_tp):
        go_ref[lanes(tp, o, q_len // n_tp), :] = gm_refs[o][...]
        mixed_ref[lanes(tp, o, q_len // n_tp), :] = mixed_refs[o][...]
    deltas = []
    for start in range(0, q_len, tq):
        rows = slice(start, start + tq)
        prod = (go_ref[rows, :].astype(F32) * mixed_ref[rows, :].astype(F32)).T
        sums = [
            jnp.sum(prod[h * HD : (h + 1) * HD, :], axis=0, keepdims=True) for h in range(heads)
        ]
        deltas.append(sums)
    lane = lax.broadcasted_iota(jnp.int32, (tq, width), 1)
    nq = q_len // tq
    for qi in range(nq):
        rows = slice(qi * tq, (qi + 1) * tq)
        qv = q_ref[rows, :] * BF16(0.125)
        gv = go_ref[rows, :]
        for h in range(heads):
            mine = (lane >= h * HD) & (lane < (h + 1) * HD)
            qm_ref[h, rows, :] = jnp.where(mine, qv, jnp.zeros_like(qv))
            gom_ref[h, rows, :] = jnp.where(mine, gv, jnp.zeros_like(gv))
    dqt_ref[...] = jnp.zeros_like(dqt_ref)
    for c in range(n_chunk):
        kv = kv_refs[c]
        dkv = dkv_refs[c]
        cbase = (ctx ^ c) * q_len

        def step(ki, carry, kv=kv, dkv=dkv, cbase=cbase):
            kb = cbase + ki * tk
            krows = pl.ds(pl.multiple_of(ki * tk, tk), tk)
            live = [
                (kb <= ctx * q_len + (qi + 1) * tq - 1) & (kb + tk - 1 >= scalars[3 + qi])
                for qi in range(nq)
            ]
            some = functools.reduce(jnp.logical_or, live)

            @pl.when(jnp.logical_not(some))
            def _():
                dkv[krows, :] = jnp.zeros((tk, 2 * width), BF16)

            @pl.when(some)
            def _():
                acck_ref[...] = jnp.zeros_like(acck_ref)
                accv_ref[...] = jnp.zeros_like(accv_ref)
                k = kv[krows, 0:width]
                v = kv[krows, width : 2 * width]
                kt = k.T
                kpos = kb + lax.broadcasted_iota(jnp.int32, (tk, 1), 0)
                for qi in range(nq):

                    @pl.when(live[qi])
                    def _(qi=qi):
                        rows = slice(qi * tq, (qi + 1) * tq)
                        qpos = (
                            ctx * q_len + qi * tq + lax.broadcasted_iota(jnp.int32, (1, tq), 1)
                        )
                        ok = (kpos >= lo_ref[0:1, rows]) & (kpos <= qpos)
                        dk = acck_ref[...]
                        dv = accv_ref[...]
                        for h in range(heads):
                            qh = qm_ref[h, rows, :]
                            gh = gom_ref[h, rows, :]
                            s = dot(k, qh, 1, 1)
                            p = jnp.where(ok, jnp.exp(s - lse_ref[h : h + 1, rows]), 0.0)
                            dp = dot(v, gh, 1, 1)
                            ds = (p * (dp - deltas[qi][h])).astype(BF16)
                            dv = dv + dot(p.astype(BF16), gh, 1, 0)
                            dk = dk + dot(ds, qh, 1, 0)
                            hs = slice(h * HD, (h + 1) * HD)
                            dqt_ref[hs, rows] = dqt_ref[hs, rows] + dot(kt[hs, :], ds, 1, 0)
                        acck_ref[...] = dk
                        accv_ref[...] = dv

                dkv[krows, 0:width] = acck_ref[...].astype(BF16)
                dkv[krows, width : 2 * width] = accv_ref[...].astype(BF16)

            return carry

        lax.fori_loop(0, q_len // tk, step, 0)
    for qi in range(nq):
        rows = slice(qi * tq, (qi + 1) * tq)
        dq_ref[rows, :] = (dqt_ref[:, rows].T * 0.125).astype(BF16)


def normal(value):
    mean = jnp.mean(value, axis=-1, keepdims=True)
    centered = value - mean
    inv = lax.rsqrt(jnp.mean(centered * centered, axis=-1, keepdims=True) + 1e-05)
    return centered * inv, inv


def normal_back(grad_out, norm, inv, gain):
    grad = grad_out * gain
    centered = grad - jnp.mean(grad, axis=-1, keepdims=True)
    return inv * (centered - norm * jnp.mean(grad * norm, axis=-1, keepdims=True))


def merge_kernel(n_tp, rows_ref, wide_ref, *refs):
    mixed, refs = refs[:n_tp], refs[n_tp:]
    weights, (hidden_ref, normed_ref) = refs[:-2], refs[-2:]
    values = jnp.concatenate([ref[...] for ref in mixed], axis=1)
    block = weights[0].shape[0]
    for place, ref in enumerate(weights):
        cols = slice(place * block, (place + 1) * block)
        made = dot(values, ref[...], 1, 1)
        hidden_ref[:, cols] = rows_ref[:, cols].astype(F32) + made + wide_ref[2:3, cols]
    norm, _ = normal(hidden_ref[...])
    normed_ref[...] = (norm * wide_ref[3:4, :] + wide_ref[4:5, :]).astype(BF16)


def dense_kernel(count, expand_ref, *refs):
    normed, refs = refs[:count], refs[count:]
    grads, refs = refs[:count], refs[count:]
    weights, outs = refs[: -4 * count - 1], refs[-4 * count - 1 :]
    acts, pres, normed_outs, mlp_outs = (outs[i * count : (i + 1) * count] for i in range(4))
    sum_ref = outs[-1]
    block = weights[0].shape[0] // 2
    height = normed[0].shape[0]
    hidden = expand_ref.shape[1]
    step = min(hidden, 512)
    value = jnp.concatenate([ref[...] for ref in normed], axis=0)
    grad = jnp.concatenate([ref[...] for ref in grads], axis=0)
    back = forth = None
    for start in range(0, hidden, step):
        cols = slice(start, start + step)
        expand = jnp.concatenate([ref[:block, cols] for ref in weights], axis=0)
        shrink = jnp.concatenate([ref[block:, cols] for ref in weights], axis=0)
        pre = dot(value, expand, 1, 0) + expand_ref[:, cols]
        square = pre * pre
        inner = jnp.tanh(0.7978845608028654 * (pre + 0.044715 * square * pre))
        act = (0.5 * pre * (1.0 + inner)).astype(BF16)
        slope = 0.5 * (1.0 + inner) + (0.5 * 0.7978845608028654) * pre * (
            1.0 - inner * inner
        ) * (1.0 + (3.0 * 0.044715) * square)
        low = (dot(grad, shrink, 1, 0) * slope).astype(BF16)
        sum_ref[:, cols] = jnp.sum(low.astype(F32), axis=0, keepdims=True)
        for i in range(count):
            rows = slice(i * height, (i + 1) * height)
            acts[i][:, cols] = act[rows]
            pres[i][:, cols] = low[rows]
        more = dot(low, expand, 1, 1)
        also = dot(act, shrink, 1, 1)
        back = more if back is None else back + more
        forth = also if forth is None else forth + also
    for i in range(count):
        rows = slice(i * height, (i + 1) * height)
        normed_outs[i][...] = back[rows].astype(BF16)
        mlp_outs[i][...] = forth[rows].astype(BF16)


def hidden_back_kernel(n_tp, grad_ref, hidden_ref, wide_ref, *refs):
    parts, refs = refs[:n_tp], refs[n_tp:]
    weights, outs = refs[: -3 - n_tp], refs[-3 - n_tp :]
    back_ref, low_ref, sums_ref = outs[:3]
    total = total_of(parts)
    norm, inv = normal(hidden_ref[...])
    grad = grad_ref[...].astype(F32)
    back = grad + normal_back(total, norm, inv, wide_ref[3:4, :])
    back_ref[...] = back
    low = back.astype(BF16)
    low_ref[...] = low
    width = outs[3].shape[1]
    for o in range(n_tp):
        cols = slice(o * width, (o + 1) * width)
        weight = jnp.concatenate([ref[:, cols] for ref in weights], axis=0)
        outs[3 + o][...] = dot(low, weight, 1, 0).astype(BF16)
    sums_ref[...] = jnp.concatenate(
        [jnp.sum(v, axis=0, keepdims=True) for v in (back, total * norm, total, grad)], axis=0
    )


def outer_kernel(order, spans, scalars, *refs):
    out_ref = refs[-1]
    tall = out_ref.shape[1] // len(spans)
    base = 0
    for many, more in spans:
        left, refs = refs[:many], refs[many:]
        right, refs = refs[:more], refs[more:]
        a = jnp.concatenate([ref[...] for ref in left], axis=0)
        b = jnp.concatenate([ref[...] for ref in right], axis=0)
        for place, offset in enumerate(order):
            made = dot(a[:, place * tall : (place + 1) * tall], b, 0, 0).astype(BF16)
            out_ref[scalars[0] ^ offset, base : base + tall, :] = made
        base += tall


def last_outer_kernel(order, n_tp, scalars, normed_ref, query_ref, pair_ref, grad_ref, *refs):
    mixed, out_ref = refs[:n_tp], refs[n_tp]
    tall = out_ref.shape[1]
    width = query_ref.shape[1]
    values = jnp.concatenate([ref[...] for ref in mixed], axis=1)
    for place, offset in enumerate(order):
        rows = slice(place * tall, (place + 1) * tall)
        target = scalars[0] ^ offset
        left = normed_ref[:, rows]
        out_ref[target, :, :width] = dot(left, query_ref[...], 0, 0).astype(BF16)
        out_ref[target, :, width : 3 * width] = dot(left, pair_ref[...], 0, 0).astype(BF16)
        out_ref[target, :, 3 * width :] = dot(grad_ref[:, rows], values, 0, 0).astype(BF16)


def join_kernel(left_ref, right_ref, out_ref):
    total = left_ref[...].astype(F32) + right_ref[...].astype(F32)
    out_ref[...] = total.astype(out_ref.dtype)


def sum_of(ref):
    total = ref[0].astype(F32)
    for i in range(1, ref.shape[0]):
        total = total + ref[i].astype(F32)
    return total


def dense_total_kernel(in_ref, expand_ref, shrink_ref):
    block = expand_ref.shape[0]
    expand_ref[...] = in_ref[:block, :].astype(F32)
    shrink_ref[...] = in_ref[block:, :].astype(F32).T


def last_total_kernel(in_ref, attend_ref, *outs):
    parts, _, width = attend_ref.shape
    for c in range(parts):
        attend_ref[c] = in_ref[:, c * width : (c + 1) * width].astype(F32)
    for o, ref in enumerate(outs):
        ref[...] = in_ref[:, (parts + o) * width : (parts + o + 1) * width]


def merge_turned_kernel(*refs):
    refs[-1][...] = total_of(refs[:-1]).T


def total_of(refs):
    total = refs[0][...].astype(F32)
    for ref in refs[1:]:
        total = total + ref[...].astype(F32)
    return total


def layer_kernel(order, scalars, hidden_ref, wide_ref, *refs):
    total = total_of(refs[:-1])
    out_ref = refs[-1]
    value = (hidden_ref[...] + total + wide_ref[5:6, :]).astype(BF16)
    size = value.shape[1] // len(order)
    for place, offset in enumerate(order):
        out_ref[:, lanes(scalars[0], offset, size)] = value[:, place * size : (place + 1) * size]


def input_kernel(order, scalars, rows_ref, back_ref, wide_ref, *refs):
    out_ref, sums_ref = refs[-2:]
    total = total_of(refs[:-2])
    norm, inv = normal(rows_ref[...].astype(F32))
    value = (back_ref[...] + normal_back(total, norm, inv, wide_ref[0:1, :])).astype(BF16)
    size = value.shape[1] // len(order)
    for place, offset in enumerate(order):
        out_ref[:, lanes(scalars[0], offset, size)] = value[:, place * size : (place + 1) * size]
    sums_ref[...] = jnp.concatenate(
        [jnp.sum(v, axis=0, keepdims=True) for v in (total * norm, total)], axis=0
    )


def place_kernel(count, scalars, *refs):
    height = refs[0].shape[0]
    for o in range(count):
        start = pl.multiple_of((scalars[2] ^ o) * height, height)
        refs[count][pl.ds(start, height), :] = refs[o][...]


def project_back_kernel(block, n_pair, n_tp, scalars, dq_ref, *refs):
    many = len(refs) - n_tp - 2
    outs = refs[many:]
    pair_ref, sums_ref = outs[n_tp:]
    pair = total_of(refs[:n_pair]).astype(BF16)
    weights = refs[n_pair:many]
    pair_ref[...] = pair
    width = dq_ref.shape[1]
    weight = rows_of(weights, 0, block)
    height = outs[0].shape[0]
    for o in range(n_tp):
        rows = pl.ds(pl.multiple_of((scalars[2] ^ o) * height, height), height)
        both = jnp.concatenate([dq_ref[rows, :], pair_ref[rows, :]], axis=1)
        outs[o][...] = dot(both, weight, 1, 1).astype(BF16)
    sums_ref[...] = jnp.concatenate(
        [
            jnp.sum(v, axis=0, keepdims=True)
            for v in (dq_ref[...].astype(F32), pair[:, width:].astype(F32))
        ],
        axis=0,
    )


def small_kernel(order, head_block, n_tp, scalars, two_ref, four_ref, attend_ref, *refs):
    index = scalars[0]
    out_ref = refs[-1]
    hidden = total_of(refs[:-1])
    size = out_ref.shape[2]
    attend = jnp.concatenate([attend_ref[...], jnp.zeros((6, attend_ref.shape[1]), F32)], axis=0)
    for place, offset in enumerate(order):
        cols = slice(place * size, (place + 1) * size)
        block = index ^ offset
        turned = pltpu.roll(attend, attend.shape[1] - block * head_block, 1)
        last = jnp.concatenate(
            [
                turned[0:1, :head_block],
                turned[1:2, :head_block],
                jnp.zeros((1, size - 2 * head_block), F32),
            ],
            axis=1,
        )
        mine = jnp.zeros((1, size), F32)
        for j in range(len(order)):
            mine = mine + jnp.where(block == j, hidden[:, j * size : (j + 1) * size], 0.0)
        made = jnp.concatenate([two_ref[:, cols], four_ref[:, cols], mine, last], axis=0)
        for o in range(n_tp):
            out_ref[block * n_tp + o] = made


def small_total_kernel(n_tp, scalars, in_ref, *outs):
    total = sum_of(in_ref)
    local = in_ref[scalars[2]]
    for i in range(1, in_ref.shape[0] // n_tp):
        local = local + in_ref[i * n_tp + scalars[2]]
    for i in range(6):
        outs[i][...] = total[i : i + 1, :]
    outs[6][...] = local[6:7, :]
    size = outs[7].shape[1]
    outs[7][...] = jnp.concatenate([local[7:8, :size], local[7:8, size : 2 * size]], axis=0)


def after(value, *others):
    return lax.optimization_barrier((value, *others))[0]


def body(
    sizes,
    layer_input,
    cotangent,
    segment_ids,
    norm1_gain,
    norm1_bias,
    attend_weight,
    attend_bias,
    merge_weight,
    merge_bias,
    norm2_gain,
    norm2_bias,
    expand_weight,
    expand_bias,
    shrink_weight,
    shrink_bias,
):
    n_dp, n_ctx, n_tp = sizes
    group = n_dp * n_ctx
    seqs, q_len, wide = layer_input.shape
    assert seqs == 1
    block = wide // group
    width = attend_weight.shape[2]
    heads = width // HD
    hidden_width = expand_weight.shape[1]
    height = q_len // n_tp
    bias_block = expand_bias.shape[0]
    head_block = attend_bias.shape[1]
    tile = min(256, q_len)
    direct = (n_dp, n_ctx) == (2, 4) and block % 128 == 0
    direct = direct and bias_block == block and 2 * head_block <= block
    order = [0, 2, 4, 6, 1, 3, 5, 7] if direct else [0]
    ctx = lax.axis_index("ctx")
    tp = lax.axis_index("tp")
    me = lax.axis_index("dp") * n_ctx + ctx if direct else 0 * ctx
    plane = ("dp", "ctx")

    def plane_swap(value, offset):
        return lax.ppermute(value, plane, [(i, i ^ offset) for i in range(group)])

    def ctx_swap(value, offset):
        return lax.ppermute(value, "ctx", [(i, i ^ offset) for i in range(n_ctx)])

    def tp_swap(value, offset):
        return lax.ppermute(value, "tp", [(i, i ^ offset) for i in range(n_tp)])

    def with_cores(even):
        return even + [ctx_swap(v, 1) for v in even]

    def tp_gather(value):
        return [value] + [tp_swap(value, o) for o in range(1, n_tp)]

    def tp_exchange(parts):
        return [parts[0]] + [tp_swap(parts[o], o) for o in range(1, n_tp)]

    smalls = (
        norm1_gain,
        norm1_bias,
        merge_bias,
        norm2_gain,
        norm2_bias,
        shrink_bias,
        expand_bias,
    )
    if direct:
        (pack,) = call(
            pack_kernel,
            "pack",
            None,
            [jnp.swapaxes(attend_weight, 0, 1)]
            + [jnp.reshape(v, (1, block)) for v in smalls]
            + [attend_bias],
            [shape((block + 8, 3 * width), BF16)],
        )
        first_x = plane_swap(pack, 2)
        first_y = plane_swap(pack, 4)
        merge_rows = tp_gather(after(merge_weight, pack))
        (rest,) = call(
            turn_kernel,
            "turn",
            None,
            [expand_weight, shrink_weight, *merge_rows],
            [shape((3 * block, wide), BF16)],
        )
        first_xy = plane_swap(first_x, 4)
        first = with_cores([pack, first_x, first_y, first_xy])
        rest_x = plane_swap(after(rest, first_x), 2)
        rest_y = plane_swap(after(rest, first_xy), 4)
        rest_xy = plane_swap(rest_x, 4)
        given = []
    else:

        def whole(value, axis):
            return lax.all_gather(value, plane, axis=axis, tiled=True)

        first = [jnp.reshape(whole(attend_weight, 0), (wide, 3 * width))]
        merge_rows = whole(jnp.concatenate(tp_gather(merge_weight.T), axis=1), 0)
        rest_all = [
            jnp.concatenate([whole(expand_weight, 0), whole(shrink_weight.T, 0), merge_rows], 0)
        ]
        wide_rows = whole(jnp.stack(smalls[:6]), 1).astype(F32)
        given = [
            jnp.pad(wide_rows, ((0, 2), (0, 0))),
            whole(expand_bias, 0).astype(F32)[None],
            whole(attend_bias, 1).astype(F32),
        ]
    span = block if direct else wide

    seg_all = segment_ids[0]
    seg_query = lax.dynamic_slice_in_dim(seg_all, ctx * q_len, q_len, 0)
    lows = jnp.sum(
        (seg_all[:, None] < seg_query[None, :]).astype(jnp.int32), axis=0, keepdims=True
    )
    place = jnp.stack([me, ctx, tp]).astype(jnp.int32)
    limits = jnp.concatenate([place, lows[0, ::tile]], axis=0)
    keep = jnp.broadcast_to((seg_query > 0).astype(BF16)[:, None], (q_len, 128))

    normed1, query, pair, input_rows, wide_rows, expand_add, attend_add = call(
        functools.partial(project_kernel, order, span, head_block),
        "project",
        place,
        [layer_input[0], *first, *given],
        [
            shape((q_len, wide), BF16),
            shape((q_len, width), BF16),
            shape((q_len, 2 * width), BF16),
            shape((height, wide), BF16),
            shape((8, wide), F32),
            shape((1, hidden_width), F32),
            shape((2, width), F32),
        ],
        flops=6 * q_len * wide * width,
    )
    near = [pair] + [ctx_swap(pair, o) for o in range(2, n_ctx, 2)]
    pairs = []
    for value in near:
        pairs += [value, ctx_swap(value, 1)]
    grad_rows = call(
        functools.partial(grad_order_kernel, order, n_tp),
        "order_grad",
        place,
        [after(cotangent[0], pair), keep],
        [shape((height, wide), BF16)] * n_tp,
    )
    pairs[-1] = after(pairs[-1], grad_rows[0], limits)
    out = call(
        functools.partial(attend_kernel, heads, tile, tile, n_ctx, n_tp),
        "attention",
        limits,
        [lows, query, *pairs],
        [shape((height, width), BF16)] * n_tp + [shape((heads, q_len), F32)],
        [
            pltpu.VMEM((heads, tile, width), BF16),
            pltpu.VMEM((width, tile), F32),
            pltpu.VMEM((8, tile), F32),
            pltpu.VMEM((8, tile), F32),
            pltpu.VMEM((q_len, width), BF16),
        ],
        flops=4 * q_len * q_len * n_ctx * width,
    )
    mixed, lse = out[:n_tp], out[n_tp]
    if direct:
        rest_all = with_cores([after(v, mixed[0]) for v in (rest, rest_x, rest_y, rest_xy)])
    merge_all = [(v, (span, wide), (2, 0)) for v in rest_all]
    dense_all = [(v, (2 * span, wide), (0, 0)) for v in rest_all]
    mixed_rows = tp_exchange(mixed)
    hidden, normed2 = call(
        functools.partial(merge_kernel, n_tp),
        "merge",
        None,
        [input_rows, wide_rows, *mixed_rows, *merge_all],
        [shape((height, wide), F32), shape((height, wide), BF16)],
        flops=2 * height * wide * wide,
    )

    normed_all = tp_gather(normed2)
    picks = [[o for o in range(n_tp) if o % 4 in (0, 2)], [o for o in range(n_tp) if o % 4 in (1, 3)]]
    acts, pres, parts, mlps = ([None] * n_tp for _ in range(4))
    sums = []
    for pick in picks:
        count = len(pick)
        if sums:
            normed_all[3] = after(normed_all[3], sums[0])
        out = call(
            functools.partial(dense_kernel, count),
            "dense",
            None,
            [expand_add]
            + [normed_all[o] for o in pick]
            + [grad_rows[o] for o in pick]
            + dense_all,
            [shape((height, hidden_width), BF16)] * (2 * count)
            + [shape((height, wide), BF16)] * (2 * count)
            + [shape((1, hidden_width), F32)],
            flops=8 * count * height * wide * hidden_width,
        )
        for i, o in enumerate(pick):
            acts[o], pres[o], parts[o], mlps[o] = (out[j * count + i] for j in range(4))
        sums.append(out[-1])
    grad_parts = tp_exchange(parts)
    if direct:
        (dense_outer,) = call(
            functools.partial(outer_kernel, order, [(n_tp, n_tp)] * 2),
            "dense_outer",
            place,
            [*normed_all, *pres, *grad_rows, *acts],
            [shape((group, 2 * block, hidden_width), BF16)],
            flops=4 * wide * hidden_width * q_len,
        )
        grad_parts[-1] = after(grad_parts[-1], dense_outer)
    out = call(
        functools.partial(hidden_back_kernel, n_tp),
        "hidden_back",
        None,
        [grad_rows[0], hidden, wide_rows, *grad_parts, *merge_all],
        [
            shape((height, wide), F32),
            shape((height, wide), BF16),
            shape((4, wide), F32),
        ]
        + [shape((height, width), BF16)] * n_tp,
        flops=2 * height * wide * wide,
    )
    hidden_grad, grad_attn, four, grad_mixed = out[0], out[1], out[2], tp_exchange(out[3:])
    mlps = tp_exchange([mlps[0]] + [after(v, grad_mixed[1]) for v in mlps[1:]])

    out = call(
        functools.partial(attend_back_kernel, heads, tile, tile, n_ctx, n_tp),
        "attention_back",
        limits,
        [lows, lse, query, *pairs, *mixed, *grad_mixed],
        [shape((q_len, width), BF16)] + [shape((q_len, 2 * width), BF16)] * n_ctx,
        [
            pltpu.VMEM((heads, q_len, width), BF16),
            pltpu.VMEM((heads, q_len, width), BF16),
            pltpu.VMEM((width, q_len), F32),
            pltpu.VMEM((tile, width), F32),
            pltpu.VMEM((tile, width), F32),
            pltpu.VMEM((q_len, width), BF16),
            pltpu.VMEM((q_len, width), BF16),
        ],
        flops=10 * q_len * q_len * n_ctx * width,
    )
    grad_query, grad_pairs = out[0], out[1:]
    joined = []
    for o in reversed(range(0, n_ctx, 2)):
        other = ctx_swap(grad_pairs[o + 1], 1)
        if joined:
            other = after(other, joined[-1])
        (total,) = call(
            join_kernel, "join", None, [other, grad_pairs[o]], [shape(other.shape, BF16)]
        )
        joined.append(total)
    joined = joined[::-1]
    (layer_part,) = call(
        functools.partial(layer_kernel, order),
        "layer",
        place,
        [after(hidden, joined[-1]), wide_rows, *mlps],
        [shape((height, wide), BF16)],
    )
    joined = [joined[0]] + [ctx_swap(v, 2 * i) for i, v in enumerate(joined) if i]
    joined[-1] = after(joined[-1], layer_part)
    out = call(
        functools.partial(project_back_kernel, span, len(joined), n_tp),
        "project_back",
        place,
        [grad_query, *joined, *first],
        [shape((height, wide), BF16)] * n_tp
        + [shape((q_len, 2 * width), BF16), shape((2, width), F32)],
        flops=6 * q_len * wide * width,
    )
    normed1_parts, grad_pair, attend_sums = tp_exchange(out[:n_tp]), out[n_tp], out[n_tp + 1]
    layer_parts = tp_gather(after(layer_part, normed1_parts[1]))
    if direct:
        dense_part = lax.psum_scatter(
            jnp.reshape(after(dense_outer, hidden_grad), (2 * wide, hidden_width)),
            plane,
            scatter_dimension=0,
            tiled=True,
        )
        (last_outer,) = call(
            functools.partial(last_outer_kernel, order, n_tp),
            "last_outer",
            place,
            [normed1, grad_query, grad_pair, grad_attn, *mixed_rows],
            [shape((group, block, 3 * width + wide), BF16)],
            flops=6 * wide * width * q_len + 2 * height * wide * wide,
        )
        last_part = lax.psum_scatter(
            jnp.reshape(last_outer, (wide, 3 * width + wide)),
            plane,
            scatter_dimension=0,
            tiled=True,
        )
        grad_expand, grad_shrink = call(
            dense_total_kernel,
            "dense_total",
            None,
            [after(dense_part, grad_pair)],
            [shape((block, hidden_width), F32), shape((hidden_width, block), F32)],
        )
        normed1_parts[-1] = after(normed1_parts[-1], last_outer, grad_expand)
    input_part, two = call(
        functools.partial(input_kernel, order),
        "input_back",
        place,
        [input_rows, hidden_grad, wide_rows, *normed1_parts],
        [shape((height, wide), BF16), shape((2, wide), F32)],
    )
    input_parts = tp_gather(input_part)

    def placed(parts):
        (result,) = call(
            functools.partial(place_kernel, n_tp),
            "place",
            place,
            parts,
            [shape((q_len, wide), BF16)],
        )
        return result

    layer_output = placed(layer_parts)

    if direct:
        out = call(
            last_total_kernel,
            "last_total",
            None,
            [last_part],
            [shape((3, block, width), F32)] + [shape((block, width), BF16)] * n_tp,
        )
        grad_attend = out[0]
        (grad_merge,) = call(
            merge_turned_kernel,
            "merge_turned",
            None,
            tp_exchange(out[1:]),
            [shape((width, block), F32)],
        )
        (small,) = call(
            functools.partial(small_kernel, order, head_block, n_tp),
            "small",
            place,
            [two, four, attend_sums, *sums],
            [shape((group * n_tp, 8, block), F32)],
        )
        table = call(
            functools.partial(small_total_kernel, n_tp),
            "small_total",
            place,
            [lax.all_to_all(small, ("dp", "ctx", "tp"), 0, 0)],
            [shape((1, block), F32)] * 7 + [shape((2, head_block), F32)],
        )
        rows = [jnp.reshape(v, (block,)) for v in table[:7]]
        expand_sum, attend_sum = rows[6], table[7]
        input_parts[-1] = after(input_parts[-1], layer_output, *table)
        grad_attend = jnp.swapaxes(grad_attend, 0, 1)
    else:

        def cut(value, axis):
            return lax.psum_scatter(value, plane, scatter_dimension=axis, tiled=True)

        def outer_of(left, right):
            return cut(
                dot(jnp.concatenate(left), jnp.concatenate(right), 0, 0).astype(BF16), 0
            ).astype(F32)

        grad_expand = outer_of(normed_all, pres)
        grad_shrink = outer_of(grad_rows, acts).T
        grad_merge = outer_of([grad_attn], [jnp.concatenate(mixed_rows, axis=1)]).astype(BF16)
        grad_merge = [grad_merge[:, o * width : (o + 1) * width] for o in range(n_tp)]
        grad_merge = sum(v.astype(F32) for v in tp_exchange(grad_merge)).T
        grad_attend = outer_of([normed1], [jnp.concatenate([grad_query, grad_pair], axis=1)])
        grad_attend = jnp.reshape(grad_attend, (block, 3, width))
        table = lax.psum(cut(jnp.concatenate([two, four], axis=0), 1), "tp")
        rows = [table[i] for i in range(6)]
        expand_sum = cut(sum(sums)[0], 0)
        attend_sum = cut(attend_sums, 1)
    input_grad = placed(input_parts)
    return (
        layer_output[None],
        input_grad[None],
        rows[0],
        rows[1],
        grad_attend,
        attend_sum,
        grad_merge,
        rows[2],
        rows[3],
        rows[4],
        grad_expand,
        expand_sum,
        grad_shrink,
        rows[5],
    )


def solution(mesh):
    sizes = (mesh.shape["dp"], mesh.shape["ctx"], mesh.shape["tp"])
    return jax.shard_map(
        functools.partial(body, sizes),
        mesh=mesh,
        in_specs=(
            P("dp", "ctx", None),
            P("dp", "ctx", None),
            P("dp", None),
            P(("dp", "ctx")),
            P(("dp", "ctx")),
            P(("dp", "ctx"), None, "tp"),
            P(None, ("tp", "dp", "ctx")),
            P("tp", ("dp", "ctx")),
            P(("dp", "ctx")),
            P(("dp", "ctx")),
            P(("dp", "ctx")),
            P(("dp", "ctx"), "tp"),
            P(("tp", "dp", "ctx")),
            P("tp", ("dp", "ctx")),
            P(("dp", "ctx")),
        ),
        out_specs=(
            P("dp", "ctx", None),
            P("dp", "ctx", None),
            P(("dp", "ctx")),
            P(("dp", "ctx")),
            P(("dp", "ctx"), None, "tp"),
            P(None, ("tp", "dp", "ctx")),
            P("tp", ("dp", "ctx")),
            P(("dp", "ctx")),
            P(("dp", "ctx")),
            P(("dp", "ctx")),
            P(("dp", "ctx"), "tp"),
            P(("tp", "dp", "ctx")),
            P("tp", ("dp", "ctx")),
            P(("dp", "ctx")),
        ),
        check_vma=False,
    )
```

```python
import functools

import jax
import jax.numpy as jnp
from jax import lax
from jax.experimental import pallas as pl
from jax.experimental.pallas import tpu as pltpu
from jax.sharding import PartitionSpec as P

HD = 64
NEG = -1e30
F32 = jnp.float32
BF16 = jnp.bfloat16


def dot(left, right, left_dim, right_dim):
    return lax.dot_general(
        left, right, (((left_dim,), (right_dim,)), ((), ())), preferred_element_type=F32
    )


def shape(dims, dtype):
    return jax.ShapeDtypeStruct(tuple(dims), dtype)


def call(kernel, name, scalars, ins, outs, scratch=(), flops=0, whole=None):
    first = [] if scalars is None else [scalars]
    specs, arrays, moved = [], [], 0
    for value in ins:
        if isinstance(value, tuple):
            value, dims, index = value
            specs.append(pl.BlockSpec(dims, lambda i, index=index: index))
            moved += value.dtype.itemsize * functools.reduce(lambda a, b: a * b, dims)
        else:
            specs.append(pl.BlockSpec(memory_space=pltpu.VMEM))
            moved += value.size * value.dtype.itemsize
        arrays.append(value)
    moved += sum(v.size * v.dtype.itemsize for v in outs)
    out_specs = [pl.BlockSpec(memory_space=pltpu.VMEM)] * len(outs)
    alias = {}
    if whole is not None:
        alias = {len(first) + len(arrays): len(outs)}
        specs.append(pl.BlockSpec(memory_space=pl.ANY))
        arrays.append(whole)
        outs = [*outs, shape(whole.shape, whole.dtype)]
        out_specs.append(pl.BlockSpec(memory_space=pl.ANY))
    return pl.pallas_call(
        kernel,
        grid=(1,),
        out_shape=tuple(outs),
        in_specs=[pl.BlockSpec(memory_space=pltpu.SMEM)] * len(first) + specs,
        out_specs=tuple(out_specs),
        input_output_aliases=alias,
        scratch_shapes=list(scratch),
        compiler_params=pltpu.CompilerParams(vmem_limit_bytes=56 << 20),
        cost_estimate=pl.CostEstimate(
            flops=flops, transcendentals=0, bytes_accessed=moved
        ),
        name=name,
    )(*first, *arrays)


def lanes(index, offset, size):
    return pl.ds(pl.multiple_of((index ^ offset) * size, size), size)


def rows_of(refs, low, high):
    return jnp.concatenate([ref[low:high, :] for ref in refs], axis=0)


def pack_kernel(attend_ref, *refs):
    smalls, (pair_ref, out_ref) = refs[:-2], refs[-2:]
    parts, block, width = attend_ref.shape
    for c in range(parts):
        out_ref[:block, c * width : (c + 1) * width] = attend_ref[c]
    size = smalls[0].shape[1]
    last = jnp.concatenate([pair_ref[0:1, :], pair_ref[1:2, :]], axis=1).astype(F32)
    last = jnp.concatenate([last, jnp.zeros((1, size - last.shape[1]), F32)], axis=1)
    rows = jnp.concatenate([ref[...].astype(F32) for ref in smalls] + [last], axis=0)
    out_ref[block:, :size] = rows.astype(BF16)
    out_ref[block:, size:] = jnp.zeros((8, parts * width - size), BF16)


def turn_kernel(expand_ref, shrink_ref, out_ref):
    block = expand_ref.shape[0]
    out_ref[:block, :] = expand_ref[...]
    out_ref[block:, :] = shrink_ref[...].T


def decode(order, head_block, index, first, start, size, wide_ref, expand_ref, attend_ref):
    total = jnp.zeros(attend_ref.shape, F32)
    for place, offset in enumerate(order):
        rows = first[place][start : start + 8, :size].astype(F32)
        wide_ref[:, place * size : (place + 1) * size] = rows
        expand_ref[:, lanes(index, offset, size)] = rows[6:7, :]
        flat = jnp.concatenate([rows[7:8, :head_block], rows[7:8, head_block : 2 * head_block]], 0)
        flat = jnp.concatenate(
            [flat, jnp.zeros((2, attend_ref.shape[1] - head_block), F32)], axis=1
        )
        flat = jnp.concatenate([flat, jnp.zeros((6, attend_ref.shape[1]), F32)], axis=0)
        total = total + pltpu.roll(flat, (index ^ offset) * head_block, 1)[:2]
    attend_ref[...] = total


def grad_order_kernel(order, count, scalars, cot_ref, keep_ref, *outs):
    index, tp = scalars[0], scalars[2]
    height, wide = outs[0].shape
    size = wide // len(order)
    for o in range(count):
        rows = pl.ds(pl.multiple_of((tp ^ o) * height, height), height)
        keep = keep_ref[rows, 0:1]
        for place, offset in enumerate(order):
            outs[o][:, place * size : (place + 1) * size] = (
                cot_ref[rows, lanes(index, offset, size)] * keep
            )


def project_kernel(order, block, head_block, scalars, x_ref, *refs):
    count = len(order)
    weights, refs = refs[:count], refs[count:]
    given, outs = refs[:-7], refs[-7:]
    normed_ref, query_ref, pair_ref, rows_ref = outs[:4]
    wide_ref, expand_ref, attend_ref = outs[4:]
    index, tp = scalars[0], scalars[2]
    q_len, wide = x_ref.shape
    size = wide // count
    for source, target in zip(given, outs[4:]):
        target[...] = source[...]
    if not given:
        decode(order, head_block, index, weights, block, size, wide_ref, expand_ref, attend_ref)
    width = query_ref.shape[1]
    weight = rows_of(weights, 0, block)
    step = min(q_len, 256)
    bias = jnp.concatenate(
        [attend_ref[0:1, :], jnp.zeros((1, width), F32), attend_ref[1:2, :]], axis=1
    )
    for start in range(0, q_len, step):
        rows = slice(start, start + step)
        value = x_ref[rows, :].astype(F32)
        mean = jnp.mean(value, axis=-1, keepdims=True)
        centered = value - mean
        inv = lax.rsqrt(jnp.mean(centered * centered, axis=-1, keepdims=True) + 1e-05)
        for place, offset in enumerate(order):
            plain = slice(place * size, (place + 1) * size)
            part = x_ref[rows, lanes(index, offset, size)].astype(F32)
            part = (part - mean) * inv * wide_ref[0:1, plain] + wide_ref[1:2, plain]
            normed_ref[rows, plain] = part.astype(BF16)
        made = dot(normed_ref[rows, :], weight, 1, 0) + bias
        query_ref[rows, :] = made[:, :width].astype(BF16)
        pair_ref[rows, :] = made[:, width:].astype(BF16)
    height = rows_ref.shape[0]
    mine = pl.ds(pl.multiple_of(tp * height, height), height)
    for place, offset in enumerate(order):
        plain = slice(place * size, (place + 1) * size)
        rows_ref[:, plain] = x_ref[mine, lanes(index, offset, size)]


def attend_kernel(heads, tq, tk, n_chunk, n_tp, scalars, lo_ref, q_ref, *refs):
    kv_refs = refs[:n_chunk]
    outs, refs = refs[n_chunk : n_chunk + n_tp], refs[n_chunk + n_tp :]
    lse_ref, qm_ref, acc_ref, m_ref, l_ref, mixed_ref = refs
    q_len, width = q_ref.shape
    ctx = scalars[1]
    lane = lax.broadcasted_iota(jnp.int32, (tq, width), 1)
    for qi in range(q_len // tq):
        rows = slice(qi * tq, (qi + 1) * tq)
        qv = q_ref[rows, :] * BF16(0.125)
        for h in range(heads):
            mine = (lane >= h * HD) & (lane < (h + 1) * HD)
            qm_ref[h] = jnp.where(mine, qv, jnp.zeros_like(qv))
        acc_ref[...] = jnp.zeros_like(acc_ref)
        m_ref[...] = jnp.full(m_ref.shape, NEG, F32)
        l_ref[...] = jnp.zeros_like(l_ref)
        qbase = ctx * q_len + qi * tq
        qpos = qbase + lax.broadcasted_iota(jnp.int32, (1, tq), 1)
        lo = lo_ref[0:1, rows]
        lo_first = scalars[3 + qi]
        for c in range(n_chunk):
            kv = kv_refs[c]
            cbase = (ctx ^ c) * q_len

            def step(ki, carry, kv=kv, cbase=cbase):
                kb = cbase + ki * tk

                @pl.when((kb <= qbase + tq - 1) & (kb + tk - 1 >= lo_first))
                def _():
                    krows = pl.ds(pl.multiple_of(ki * tk, tk), tk)
                    k = kv[krows, 0:width]
                    vt = kv[krows, width : 2 * width].T
                    kpos = kb + lax.broadcasted_iota(jnp.int32, (tk, 1), 0)
                    ok = (kpos >= lo) & (kpos <= qpos)
                    for h in range(heads):
                        s = jnp.where(ok, dot(k, qm_ref[h], 1, 1), NEG)
                        m0 = m_ref[h : h + 1, :]
                        m1 = jnp.maximum(m0, jnp.max(s, axis=0, keepdims=True))
                        p = jnp.exp(s - m1)
                        al = jnp.exp(m0 - m1)
                        l_ref[h : h + 1, :] = l_ref[h : h + 1, :] * al + jnp.sum(
                            p, axis=0, keepdims=True
                        )
                        m_ref[h : h + 1, :] = m1
                        hs = slice(h * HD, (h + 1) * HD)
                        acc_ref[hs, :] = acc_ref[hs, :] * al + dot(
                            vt[hs, :], p.astype(BF16), 1, 0
                        )

                return carry

            lax.fori_loop(0, q_len // tk, step, 0)
        lse_ref[:, rows] = m_ref[0:heads, :] + jnp.log(l_ref[0:heads, :])
        for h in range(heads):
            hs = slice(h * HD, (h + 1) * HD)
            acc_ref[hs, :] = acc_ref[hs, :] / l_ref[h : h + 1, :]
        mixed_ref[rows, :] = acc_ref[...].T.astype(BF16)
    for o in range(n_tp):
        outs[o][...] = mixed_ref[lanes(scalars[2], o, q_len // n_tp), :]


def attend_back_kernel(heads, tq, tk, n_chunk, n_tp, scalars, lo_ref, lse_ref, q_ref, *refs):
    kv_refs, refs = refs[:n_chunk], refs[n_chunk:]
    mixed_refs, refs = refs[:n_tp], refs[n_tp:]
    gm_refs, refs = refs[:n_tp], refs[n_tp:]
    dq_ref, refs = refs[0], refs[1:]
    dkv_refs, refs = refs[:n_chunk], refs[n_chunk:]
    qm_ref, gom_ref, dqt_ref, acck_ref, accv_ref, go_ref, mixed_ref = refs
    q_len, width = q_ref.shape
    ctx, tp = scalars[1], scalars[2]
    for o in range(n_tp):
        go_ref[lanes(tp, o, q_len // n_tp), :] = gm_refs[o][...]
        mixed_ref[lanes(tp, o, q_len // n_tp), :] = mixed_refs[o][...]
    deltas = []
    for start in range(0, q_len, tq):
        rows = slice(start, start + tq)
        prod = (go_ref[rows, :].astype(F32) * mixed_ref[rows, :].astype(F32)).T
        sums = [
            jnp.sum(prod[h * HD : (h + 1) * HD, :], axis=0, keepdims=True) for h in range(heads)
        ]
        deltas.append(sums)
    lane = lax.broadcasted_iota(jnp.int32, (tq, width), 1)
    nq = q_len // tq
    for qi in range(nq):
        rows = slice(qi * tq, (qi + 1) * tq)
        qv = q_ref[rows, :] * BF16(0.125)
        gv = go_ref[rows, :]
        for h in range(heads):
            mine = (lane >= h * HD) & (lane < (h + 1) * HD)
            qm_ref[h, rows, :] = jnp.where(mine, qv, jnp.zeros_like(qv))
            gom_ref[h, rows, :] = jnp.where(mine, gv, jnp.zeros_like(gv))
    dqt_ref[...] = jnp.zeros_like(dqt_ref)
    for c in range(n_chunk):
        kv = kv_refs[c]
        dkv = dkv_refs[c]
        cbase = (ctx ^ c) * q_len

        def step(ki, carry, kv=kv, dkv=dkv, cbase=cbase):
            kb = cbase + ki * tk
            krows = pl.ds(pl.multiple_of(ki * tk, tk), tk)
            live = [
                (kb <= ctx * q_len + (qi + 1) * tq - 1) & (kb + tk - 1 >= scalars[3 + qi])
                for qi in range(nq)
            ]
            some = functools.reduce(jnp.logical_or, live)

            @pl.when(jnp.logical_not(some))
            def _():
                dkv[krows, :] = jnp.zeros((tk, 2 * width), BF16)

            @pl.when(some)
            def _():
                acck_ref[...] = jnp.zeros_like(acck_ref)
                accv_ref[...] = jnp.zeros_like(accv_ref)
                k = kv[krows, 0:width]
                v = kv[krows, width : 2 * width]
                kt = k.T
                kpos = kb + lax.broadcasted_iota(jnp.int32, (tk, 1), 0)
                for qi in range(nq):

                    @pl.when(live[qi])
                    def _(qi=qi):
                        rows = slice(qi * tq, (qi + 1) * tq)
                        qpos = (
                            ctx * q_len + qi * tq + lax.broadcasted_iota(jnp.int32, (1, tq), 1)
                        )
                        ok = (kpos >= lo_ref[0:1, rows]) & (kpos <= qpos)
                        dk = acck_ref[...]
                        dv = accv_ref[...]
                        for h in range(heads):
                            qh = qm_ref[h, rows, :]
                            gh = gom_ref[h, rows, :]
                            s = dot(k, qh, 1, 1)
                            p = jnp.where(ok, jnp.exp(s - lse_ref[h : h + 1, rows]), 0.0)
                            dp = dot(v, gh, 1, 1)
                            ds = (p * (dp - deltas[qi][h])).astype(BF16)
                            dv = dv + dot(p.astype(BF16), gh, 1, 0)
                            dk = dk + dot(ds, qh, 1, 0)
                            hs = slice(h * HD, (h + 1) * HD)
                            dqt_ref[hs, rows] = dqt_ref[hs, rows] + dot(kt[hs, :], ds, 1, 0)
                        acck_ref[...] = dk
                        accv_ref[...] = dv

                dkv[krows, 0:width] = acck_ref[...].astype(BF16)
                dkv[krows, width : 2 * width] = accv_ref[...].astype(BF16)

            return carry

        lax.fori_loop(0, q_len // tk, step, 0)
    for qi in range(nq):
        rows = slice(qi * tq, (qi + 1) * tq)
        dq_ref[rows, :] = (dqt_ref[:, rows].T * 0.125).astype(BF16)


def normal(value):
    mean = jnp.mean(value, axis=-1, keepdims=True)
    centered = value - mean
    inv = lax.rsqrt(jnp.mean(centered * centered, axis=-1, keepdims=True) + 1e-05)
    return centered * inv, inv


def normal_back(grad_out, norm, inv, gain):
    grad = grad_out * gain
    centered = grad - jnp.mean(grad, axis=-1, keepdims=True)
    return inv * (centered - norm * jnp.mean(grad * norm, axis=-1, keepdims=True))


def merge_kernel(n_tp, order, scalars, rows_ref, wide_ref, weight_ref, *refs):
    mixed, (hidden_ref, normed_ref) = refs[:n_tp], refs[n_tp:]
    index, tp = scalars[0], scalars[2]
    hidden_ref[...] = rows_ref[...].astype(F32) + wide_ref[2:3, :]
    for o, ref in enumerate(mixed):
        weight = jnp.concatenate([weight_ref[index ^ p, tp ^ o] for p in order], axis=1)
        hidden_ref[...] += dot(ref[...], weight, 1, 0)
    norm, _ = normal(hidden_ref[...])
    normed_ref[...] = (norm * wide_ref[3:4, :] + wide_ref[4:5, :]).astype(BF16)


def dense_kernel(count, expand_ref, *refs):
    normed, refs = refs[:count], refs[count:]
    grads, refs = refs[:count], refs[count:]
    weights, outs = refs[: -4 * count - 1], refs[-4 * count - 1 :]
    acts, pres, normed_outs, mlp_outs = (outs[i * count : (i + 1) * count] for i in range(4))
    sum_ref = outs[-1]
    block = weights[0].shape[0] // 2
    height = normed[0].shape[0]
    hidden = expand_ref.shape[1]
    step = min(hidden, 512)
    value = jnp.concatenate([ref[...] for ref in normed], axis=0)
    grad = jnp.concatenate([ref[...] for ref in grads], axis=0)
    back = forth = None
    for start in range(0, hidden, step):
        cols = slice(start, start + step)
        expand = jnp.concatenate([ref[:block, cols] for ref in weights], axis=0)
        shrink = jnp.concatenate([ref[block:, cols] for ref in weights], axis=0)
        pre = dot(value, expand, 1, 0) + expand_ref[:, cols]
        square = pre * pre
        inner = jnp.tanh(0.7978845608028654 * (pre + 0.044715 * square * pre))
        act = (0.5 * pre * (1.0 + inner)).astype(BF16)
        slope = 0.5 * (1.0 + inner) + (0.5 * 0.7978845608028654) * pre * (
            1.0 - inner * inner
        ) * (1.0 + (3.0 * 0.044715) * square)
        low = (dot(grad, shrink, 1, 0) * slope).astype(BF16)
        sum_ref[:, cols] = jnp.sum(low.astype(F32), axis=0, keepdims=True)
        for i in range(count):
            rows = slice(i * height, (i + 1) * height)
            acts[i][:, cols] = act[rows]
            pres[i][:, cols] = low[rows]
        more = dot(low, expand, 1, 1)
        also = dot(act, shrink, 1, 1)
        back = more if back is None else back + more
        forth = also if forth is None else forth + also
    for i in range(count):
        rows = slice(i * height, (i + 1) * height)
        normed_outs[i][...] = back[rows].astype(BF16)
        mlp_outs[i][...] = forth[rows].astype(BF16)


def hidden_back_kernel(
    count, n_tp, order, scalars, grad_ref, hidden_ref, wide_ref, weight_ref, *refs
):
    parts, refs = refs[:count], refs[count:]
    mixed, refs = refs[:n_tp], refs[n_tp:]
    direct = len(order) > 1
    refs = refs[1:] if direct else refs
    back_ref, low_ref, sums_ref = refs[:3]
    outs, refs = refs[3 : 3 + n_tp], refs[3 + n_tp :]
    index, tp = scalars[0], scalars[2]
    total = total_of(parts)
    norm, inv = normal(hidden_ref[...])
    grad = grad_ref[...].astype(F32)
    back = grad + normal_back(total, norm, inv, wide_ref[3:4, :])
    back_ref[...] = back
    low = back.astype(BF16)
    low_ref[...] = low
    copies = []
    if direct:
        buffer_ref, made_ref, sems = refs
        values = jnp.concatenate([ref[...] for ref in mixed], axis=1)
        tall = made_ref.shape[1]
        for place, offset in enumerate(order):
            left = low[:, place * tall : (place + 1) * tall]
            made_ref[place] = dot(left, values, 0, 0).astype(BF16)
            copies.append(
                pltpu.make_async_copy(
                    made_ref.at[place],
                    buffer_ref.at[index ^ offset, pl.ds(2 * tall, tall), :],
                    sems.at[place],
                )
            )
            copies[-1].start()
    for o in range(n_tp):
        weight = jnp.concatenate([weight_ref[index ^ p, tp ^ o] for p in order], axis=1)
        outs[o][...] = dot(low, weight, 1, 1).astype(BF16)
    sums_ref[...] = jnp.concatenate(
        [jnp.sum(v, axis=0, keepdims=True) for v in (back, total * norm, total, grad)], axis=0
    )
    for copy in copies:
        copy.wait()


def outer_kernel(order, spans, scalars, *refs):
    out_ref = refs[-1]
    tall = out_ref.shape[1] // (len(spans) + 1)
    base = 0
    for many, more in spans:
        left, refs = refs[:many], refs[many:]
        right, refs = refs[:more], refs[more:]
        a = jnp.concatenate([ref[...] for ref in left], axis=0)
        b = jnp.concatenate([ref[...] for ref in right], axis=0)
        for place, offset in enumerate(order):
            made = dot(a[:, place * tall : (place + 1) * tall], b, 0, 0).astype(BF16)
            out_ref[scalars[0] ^ offset, base : base + tall, :] = made
        base += tall


def join_kernel(left_ref, right_ref, out_ref):
    total = left_ref[...].astype(F32) + right_ref[...].astype(F32)
    out_ref[...] = total.astype(out_ref.dtype)


def sum_of(ref):
    total = ref[0].astype(F32)
    for i in range(1, ref.shape[0]):
        total = total + ref[i].astype(F32)
    return total


def dense_total_kernel(in_ref, expand_ref, shrink_ref, *outs):
    block = expand_ref.shape[0]
    expand_ref[...] = in_ref[:block, :].astype(F32)
    shrink_ref[...] = in_ref[block : 2 * block, :].astype(F32).T
    width = outs[0].shape[1]
    for o, ref in enumerate(outs):
        ref[...] = in_ref[2 * block :, o * width : (o + 1) * width]


def attend_total_kernel(in_ref, out_ref):
    parts, _, width = out_ref.shape
    for c in range(parts):
        out_ref[c] = in_ref[:, c * width : (c + 1) * width].astype(F32)


def merge_turned_kernel(*refs):
    refs[-1][...] = total_of(refs[:-1]).T


def total_of(refs):
    total = refs[0][...].astype(F32)
    for ref in refs[1:]:
        total = total + ref[...].astype(F32)
    return total


def join_layer_kernel(order, scalars, left_ref, right_ref, hidden_ref, wide_ref, *refs):
    total = left_ref[...].astype(F32) + right_ref[...].astype(F32)
    refs[-2][...] = total.astype(BF16)
    value = (hidden_ref[...] + total_of(refs[:-2]) + wide_ref[5:6, :]).astype(BF16)
    size = value.shape[1] // len(order)
    for place, offset in enumerate(order):
        cols = slice(place * size, (place + 1) * size)
        refs[-1][:, lanes(scalars[0], offset, size)] = value[:, cols]


def input_kernel(order, scalars, rows_ref, back_ref, wide_ref, *refs):
    out_ref = refs[-1]
    total = total_of(refs[:-1])
    norm, inv = normal(rows_ref[...].astype(F32))
    value = (back_ref[...] + normal_back(total, norm, inv, wide_ref[0:1, :])).astype(BF16)
    size = value.shape[1] // len(order)
    for place, offset in enumerate(order):
        out_ref[:, lanes(scalars[0], offset, size)] = value[:, place * size : (place + 1) * size]


def first_sums_kernel(order, scalars, x_ref, *refs):
    parts, out_ref = refs[:-1], refs[-1]
    height, wide = parts[0].shape
    size = wide // len(order)
    out_ref[...] = jnp.zeros_like(out_ref)
    for o, ref in enumerate(parts):
        rows = lanes(scalars[2], o, height)
        value = x_ref[rows, :].astype(F32)
        mean = jnp.mean(value, axis=-1, keepdims=True)
        centered = value - mean
        inv = lax.rsqrt(jnp.mean(centered * centered, axis=-1, keepdims=True) + 1e-05)
        for place, offset in enumerate(order):
            cols = slice(place * size, (place + 1) * size)
            part = ref[:, cols].astype(F32)
            norm = (x_ref[rows, lanes(scalars[0], offset, size)].astype(F32) - mean) * inv
            out_ref[0:1, cols] += jnp.sum(part * norm, axis=0, keepdims=True)
            out_ref[1:2, cols] += jnp.sum(part, axis=0, keepdims=True)


def place_kernel(count, scalars, *refs):
    height = refs[0].shape[0]
    for o in range(count):
        start = pl.multiple_of((scalars[2] ^ o) * height, height)
        refs[count][pl.ds(start, height), :] = refs[o][...]


def project_back_kernel(block, order, n_pair, n_tp, scalars, normed_ref, dq_ref, *refs):
    joined, refs = refs[:n_pair], refs[n_pair:]
    weights, refs = refs[: len(order)], refs[len(order) :]
    outs, (pair_ref, sums_ref, outer_ref) = refs[:n_tp], refs[n_tp:]
    pair = total_of(joined).astype(BF16)
    pair_ref[...] = pair
    width = dq_ref.shape[1]
    weight = rows_of(weights, 0, block)
    height = outs[0].shape[0]
    for o in range(n_tp):
        rows = lanes(scalars[2], o, height)
        both = jnp.concatenate([dq_ref[rows, :], pair_ref[rows, :]], axis=1)
        outs[o][...] = dot(both, weight, 1, 1).astype(BF16)
    sums_ref[...] = jnp.concatenate(
        [
            jnp.sum(v, axis=0, keepdims=True)
            for v in (dq_ref[...].astype(F32), pair[:, width:].astype(F32))
        ],
        axis=0,
    )
    tall = outer_ref.shape[1]
    both = jnp.concatenate([dq_ref[...], pair], axis=1)
    for place, offset in enumerate(order):
        rows = slice(place * tall, (place + 1) * tall)
        outer_ref[scalars[0] ^ offset] = dot(normed_ref[:, rows], both, 0, 0).astype(BF16)


def add_kernel(left_ref, right_ref, out_ref):
    out_ref[...] = left_ref[...].astype(F32) + right_ref[...].astype(F32)


def small_kernel(order, head_block, n_tp, scalars, two_ref, four_ref, attend_ref, *refs):
    index = scalars[0]
    out_ref = refs[-1]
    hidden = total_of(refs[:-1])
    size = out_ref.shape[2]
    attend = jnp.concatenate([attend_ref[...], jnp.zeros((6, attend_ref.shape[1]), F32)], axis=0)
    for place, offset in enumerate(order):
        cols = slice(place * size, (place + 1) * size)
        block = index ^ offset
        turned = pltpu.roll(attend, attend.shape[1] - block * head_block, 1)
        last = jnp.concatenate(
            [
                turned[0:1, :head_block],
                turned[1:2, :head_block],
                jnp.zeros((1, size - 2 * head_block), F32),
            ],
            axis=1,
        )
        mine = jnp.zeros((1, size), F32)
        for j in range(len(order)):
            mine = mine + jnp.where(block == j, hidden[:, j * size : (j + 1) * size], 0.0)
        made = jnp.concatenate([two_ref[:, cols], four_ref[:, cols], mine, last], axis=0)
        for o in range(n_tp):
            out_ref[block * n_tp + o] = made


def small_total_kernel(n_tp, scalars, in_ref, *outs):
    total = sum_of(in_ref)
    local = in_ref[scalars[2]]
    for i in range(1, in_ref.shape[0] // n_tp):
        local = local + in_ref[i * n_tp + scalars[2]]
    for i in range(6):
        outs[i][...] = total[i : i + 1, :]
    outs[6][...] = local[6:7, :]
    size = outs[7].shape[1]
    outs[7][...] = jnp.concatenate([local[7:8, :size], local[7:8, size : 2 * size]], axis=0)


def after(value, *others):
    return lax.optimization_barrier((value, *others))[0]


def body(
    sizes,
    layer_input,
    cotangent,
    segment_ids,
    norm1_gain,
    norm1_bias,
    attend_weight,
    attend_bias,
    merge_weight,
    merge_bias,
    norm2_gain,
    norm2_bias,
    expand_weight,
    expand_bias,
    shrink_weight,
    shrink_bias,
):
    n_dp, n_ctx, n_tp = sizes
    group = n_dp * n_ctx
    seqs, q_len, wide = layer_input.shape
    assert seqs == 1
    block = wide // group
    width = attend_weight.shape[2]
    heads = width // HD
    hidden_width = expand_weight.shape[1]
    height = q_len // n_tp
    bias_block = expand_bias.shape[0]
    head_block = attend_bias.shape[1]
    tile = min(256, q_len)
    direct = (n_dp, n_ctx) == (2, 4) and block % 128 == 0
    direct = direct and bias_block == block and 2 * head_block <= block
    order = [0, 2, 4, 6, 1, 3, 5, 7] if direct else [0]
    ctx = lax.axis_index("ctx")
    tp = lax.axis_index("tp")
    me = lax.axis_index("dp") * n_ctx + ctx if direct else 0 * ctx
    plane = ("dp", "ctx")

    def plane_swap(value, offset):
        return lax.ppermute(value, plane, [(i, i ^ offset) for i in range(group)])

    def ctx_swap(value, offset):
        return lax.ppermute(value, "ctx", [(i, i ^ offset) for i in range(n_ctx)])

    def tp_swap(value, offset):
        return lax.ppermute(value, "tp", [(i, i ^ offset) for i in range(n_tp)])

    def with_cores(even):
        return even + [ctx_swap(v, 1) for v in even]

    def tp_gather(value):
        return [value] + [tp_swap(value, o) for o in range(1, n_tp)]

    def tp_exchange(parts):
        return [parts[0]] + [tp_swap(parts[o], o) for o in range(1, n_tp)]

    seg_all = segment_ids[0]
    seg_query = lax.dynamic_slice_in_dim(seg_all, ctx * q_len, q_len, 0)
    lows = jnp.sum(
        (seg_all[:, None] < seg_query[None, :]).astype(jnp.int32), axis=0, keepdims=True
    )
    place = jnp.stack([me, ctx, tp]).astype(jnp.int32)
    limits = jnp.concatenate([place, lows[0, ::tile]], axis=0)
    keep = jnp.broadcast_to((seg_query > 0).astype(BF16)[:, None], (q_len, 128))

    smalls = (
        norm1_gain,
        norm1_bias,
        merge_bias,
        norm2_gain,
        norm2_bias,
        shrink_bias,
        expand_bias,
    )
    if direct:
        (pack,) = call(
            pack_kernel,
            "pack",
            None,
            [jnp.swapaxes(attend_weight, 0, 1)]
            + [jnp.reshape(v, (1, block)) for v in smalls]
            + [attend_bias],
            [shape((block + 8, 3 * width), BF16)],
        )
        far = [plane_swap(pack, o) for o in order[1:4]]
        first = with_cores([after(v, limits, keep) for v in [pack] + far])
        (dense_rows,) = call(
            turn_kernel,
            "turn",
            None,
            [after(expand_weight, pack), shrink_weight],
            [shape((2 * block, hidden_width), BF16)],
        )
        merge_all = lax.all_gather(merge_weight, ("dp", "ctx", "tp"), axis=0)
        merge_all = jnp.reshape(merge_all, (group, n_tp, width, block))
        given = []
    else:

        def whole(value, axis):
            return lax.all_gather(value, plane, axis=axis, tiled=True)

        first = [jnp.reshape(whole(attend_weight, 0), (wide, 3 * width))]
        merge_all = whole(lax.all_gather(merge_weight, "tp", axis=0), 2)[None]
        dense_all = [jnp.concatenate([whole(expand_weight, 0), whole(shrink_weight.T, 0)], 0)]
        wide_rows = whole(jnp.stack(smalls[:6]), 1).astype(F32)
        given = [
            jnp.pad(wide_rows, ((0, 2), (0, 0))),
            whole(expand_bias, 0).astype(F32)[None],
            whole(attend_bias, 1).astype(F32),
        ]
    span = block if direct else wide

    normed1, query, pair, input_rows, wide_rows, expand_add, attend_add = call(
        functools.partial(project_kernel, order, span, head_block),
        "project",
        place,
        [layer_input[0], *first, *given],
        [
            shape((q_len, wide), BF16),
            shape((q_len, width), BF16),
            shape((q_len, 2 * width), BF16),
            shape((height, wide), BF16),
            shape((8, wide), F32),
            shape((1, hidden_width), F32),
            shape((2, width), F32),
        ],
        flops=6 * q_len * wide * width,
    )
    grad_rows = call(
        functools.partial(grad_order_kernel, order, n_tp),
        "order_grad",
        place,
        [after(cotangent[0], pair), keep],
        [shape((height, wide), BF16)] * n_tp,
    )
    near = [pair] + [ctx_swap(pair, o) for o in range(2, n_ctx, 2)]
    pairs = []
    for value in near:
        if pairs:
            value = after(value, grad_rows[0], limits)
        pairs += [value, ctx_swap(value, 1)]
    if direct:
        dense_y = plane_swap(after(dense_rows, grad_rows[0]), 4)
        dense_x = plane_swap(after(dense_rows, near[1]), 2)
        dense_all = [dense_rows, dense_x, dense_y]
        dense_cores = [ctx_swap(dense_rows, 1), None, ctx_swap(dense_y, 1)]
        pairs[-1] = after(pairs[-1], dense_cores[0], dense_cores[2])
    out = call(
        functools.partial(attend_kernel, heads, tile, tile, n_ctx, n_tp),
        "attention",
        limits,
        [lows, query, *pairs],
        [shape((height, width), BF16)] * n_tp + [shape((heads, q_len), F32)],
        [
            pltpu.VMEM((heads, tile, width), BF16),
            pltpu.VMEM((width, tile), F32),
            pltpu.VMEM((8, tile), F32),
            pltpu.VMEM((8, tile), F32),
            pltpu.VMEM((q_len, width), BF16),
        ],
        flops=4 * q_len * q_len * n_ctx * width,
    )
    mixed, lse = out[:n_tp], out[n_tp]
    if direct:
        dense_x = after(dense_x, mixed[0])
        dense_xy = plane_swap(dense_x, 4)
    mixed_rows = tp_exchange(mixed)
    hidden, normed2 = call(
        functools.partial(merge_kernel, n_tp, order),
        "merge",
        place,
        [input_rows, wide_rows, merge_all, *mixed_rows],
        [shape((height, wide), F32), shape((height, wide), BF16)],
        flops=2 * height * wide * wide,
    )

    if direct:
        dense_x, dense_xy = (after(v, normed2) for v in (dense_x, dense_xy))
        dense_all = [dense_rows, dense_x, dense_y, dense_xy, dense_cores[0]]
        dense_all += [ctx_swap(dense_x, 1), dense_cores[2], ctx_swap(dense_xy, 1)]
    normed_all = tp_gather(normed2)
    picks = [[o for o in range(n_tp) if o % 4 in (0, 2)], [o for o in range(n_tp) if o % 4 in (1, 3)]]
    acts, pres, parts, mlps = ([None] * n_tp for _ in range(4))
    sums = []
    for pick in picks:
        count = len(pick)
        if sums:
            normed_all[3] = after(normed_all[3], sums[0])
        out = call(
            functools.partial(dense_kernel, count),
            "dense",
            None,
            [expand_add]
            + [normed_all[o] for o in pick]
            + [grad_rows[o] for o in pick]
            + dense_all,
            [shape((height, hidden_width), BF16)] * (2 * count)
            + [shape((height, wide), BF16)] * (2 * count)
            + [shape((1, hidden_width), F32)],
            flops=8 * count * height * wide * hidden_width,
        )
        for i, o in enumerate(pick):
            acts[o], pres[o], parts[o], mlps[o] = (out[j * count + i] for j in range(4))
        sums.append(out[-1])
    grad_parts = tp_exchange(parts)
    dense_outer = None
    if direct:
        (dense_outer,) = call(
            functools.partial(outer_kernel, order, [(n_tp, n_tp)] * 2),
            "dense_outer",
            place,
            [*normed_all, *pres, *grad_rows, *acts],
            [shape((group, 3 * block, hidden_width), BF16)],
            flops=4 * wide * hidden_width * q_len,
        )
        grad_parts[2] = after(grad_parts[2], dense_outer)
    (grad_near,) = call(
        add_kernel, "add", None, [grad_parts[0], grad_parts[2]], [shape((height, wide), F32)]
    )
    grad_parts = [grad_near] + [grad_parts[o] for o in range(1, n_tp) if o != 2]
    out = call(
        functools.partial(hidden_back_kernel, len(grad_parts), n_tp, order),
        "hidden_back",
        place,
        [grad_rows[0], hidden, wide_rows, merge_all, *grad_parts, *mixed_rows],
        [
            shape((height, wide), F32),
            shape((height, wide), BF16),
            shape((4, wide), F32),
        ]
        + [shape((height, width), BF16)] * n_tp,
        [pltpu.VMEM((group, block, wide), BF16), pltpu.SemaphoreType.DMA((group,))]
        if direct
        else [],
        flops=2 * height * wide * wide,
        whole=dense_outer,
    )
    if direct:
        dense_outer = out[-1]
        out = out[:-1]
    hidden_grad, grad_attn, four, grad_mixed = out[0], out[1], out[2], tp_exchange(out[3:])
    mlps = tp_exchange([mlps[0]] + [after(v, hidden_grad) for v in mlps[1:]])

    out = call(
        functools.partial(attend_back_kernel, heads, tile, tile, n_ctx, n_tp),
        "attention_back",
        limits,
        [lows, lse, query, *pairs, *mixed, *grad_mixed],
        [shape((q_len, width), BF16)] + [shape((q_len, 2 * width), BF16)] * n_ctx,
        [
            pltpu.VMEM((heads, q_len, width), BF16),
            pltpu.VMEM((heads, q_len, width), BF16),
            pltpu.VMEM((width, q_len), F32),
            pltpu.VMEM((tile, width), F32),
            pltpu.VMEM((tile, width), F32),
            pltpu.VMEM((q_len, width), BF16),
            pltpu.VMEM((q_len, width), BF16),
        ],
        flops=10 * q_len * q_len * n_ctx * width,
    )
    grad_query, grad_pairs = out[0], out[1:]
    joined = []
    for o in reversed(range(0, n_ctx, 2)):
        if joined:
            other = after(ctx_swap(grad_pairs[o + 1], 1), joined[-1])
            (total,) = call(
                join_kernel, "join", None, [other, grad_pairs[o]], [shape(other.shape, BF16)]
            )
        else:
            other = ctx_swap(after(grad_pairs[o + 1], *mlps), 1)
            total, layer_part = call(
                functools.partial(join_layer_kernel, order),
                "join_layer",
                place,
                [other, grad_pairs[o], hidden, wide_rows, *mlps],
                [shape(other.shape, BF16), shape((height, wide), BF16)],
            )
        joined.append(total)
    joined = joined[::-1]
    layer_parts = tp_gather(layer_part)
    joined = [joined[0]] + [ctx_swap(v, 2 * i) for i, v in enumerate(joined) if i]
    joined[-1] = after(joined[-1], layer_parts[1], layer_parts[2])
    out = call(
        functools.partial(project_back_kernel, span, order, len(joined), n_tp),
        "project_back",
        place,
        [normed1, grad_query, *joined, *first],
        [shape((height, wide), BF16)] * n_tp
        + [
            shape((q_len, 2 * width), BF16),
            shape((2, width), F32),
            shape((len(order), span, 3 * width), BF16),
        ],
        flops=12 * q_len * wide * width,
    )
    normed1_parts, (grad_pair, attend_sums, attend_outer) = out[:n_tp], out[n_tp:]
    (two,) = call(
        functools.partial(first_sums_kernel, order),
        "first_sums",
        place,
        [layer_input[0], *normed1_parts],
        [shape((2, wide), F32)],
    )
    normed1_parts = tp_exchange(normed1_parts)

    def scattered(value):
        flat = jnp.reshape(value, (-1, value.shape[-1]))
        return lax.psum_scatter(flat, plane, scatter_dimension=0, tiled=True)

    if direct:
        attend_part = scattered(attend_outer)
        out = call(
            dense_total_kernel,
            "dense_total",
            None,
            [after(scattered(dense_outer), grad_pair)],
            [shape((block, hidden_width), F32), shape((hidden_width, block), F32)]
            + [shape((block, width), BF16)] * n_tp,
        )
        grad_expand, grad_shrink, merge_parts = out[0], out[1], out[2:]
        (grad_merge,) = call(
            merge_turned_kernel,
            "merge_turned",
            None,
            tp_exchange(merge_parts),
            [shape((width, block), F32)],
        )
        normed1_parts[-1] = after(normed1_parts[-1], grad_merge, two)
    (input_part,) = call(
        functools.partial(input_kernel, order),
        "input_back",
        place,
        [input_rows, hidden_grad, wide_rows, *normed1_parts],
        [shape((height, wide), BF16)],
    )
    input_parts = tp_gather(input_part)

    def placed(parts):
        (result,) = call(
            functools.partial(place_kernel, n_tp),
            "place",
            place,
            parts,
            [shape((q_len, wide), BF16)],
        )
        return result

    layer_output = placed(layer_parts)

    if direct:
        (grad_attend,) = call(
            attend_total_kernel,
            "attend_total",
            None,
            [attend_part],
            [shape((3, block, width), F32)],
        )
        (small,) = call(
            functools.partial(small_kernel, order, head_block, n_tp),
            "small",
            place,
            [two, four, attend_sums, *sums],
            [shape((group * n_tp, 8, block), F32)],
        )
        table = call(
            functools.partial(small_total_kernel, n_tp),
            "small_total",
            place,
            [lax.all_to_all(after(small, input_part), ("dp", "ctx", "tp"), 0, 0)],
            [shape((1, block), F32)] * 7 + [shape((2, head_block), F32)],
        )
        rows = [jnp.reshape(v, (block,)) for v in table[:7]]
        expand_sum, attend_sum = rows[6], table[7]
        input_parts[-1] = after(input_parts[-1], grad_attend, layer_output, *table)
        grad_attend = jnp.swapaxes(grad_attend, 0, 1)
    else:

        def cut(value, axis):
            return lax.psum_scatter(value, plane, scatter_dimension=axis, tiled=True)

        def outer_of(left, right):
            return cut(
                dot(jnp.concatenate(left), jnp.concatenate(right), 0, 0).astype(BF16), 0
            ).astype(F32)

        grad_expand = outer_of(normed_all, pres)
        grad_shrink = outer_of(grad_rows, acts).T
        grad_merge = outer_of([grad_attn], [jnp.concatenate(mixed_rows, axis=1)]).astype(BF16)
        grad_merge = [grad_merge[:, o * width : (o + 1) * width] for o in range(n_tp)]
        grad_merge = sum(v.astype(F32) for v in tp_exchange(grad_merge)).T
        grad_attend = jnp.reshape(cut(attend_outer[0], 0).astype(F32), (block, 3, width))
        table = lax.psum(cut(jnp.concatenate([two, four], axis=0), 1), "tp")
        rows = [table[i] for i in range(6)]
        expand_sum = cut(sum(sums)[0], 0)
        attend_sum = cut(attend_sums, 1)
    input_grad = placed(input_parts)
    return (
        layer_output[None],
        input_grad[None],
        rows[0],
        rows[1],
        grad_attend,
        attend_sum,
        grad_merge,
        rows[2],
        rows[3],
        rows[4],
        grad_expand,
        expand_sum,
        grad_shrink,
        rows[5],
    )


def solution(mesh):
    sizes = (mesh.shape["dp"], mesh.shape["ctx"], mesh.shape["tp"])
    return jax.shard_map(
        functools.partial(body, sizes),
        mesh=mesh,
        in_specs=(
            P("dp", "ctx", None),
            P("dp", "ctx", None),
            P("dp", None),
            P(("dp", "ctx")),
            P(("dp", "ctx")),
            P(("dp", "ctx"), None, "tp"),
            P(None, ("tp", "dp", "ctx")),
            P("tp", ("dp", "ctx")),
            P(("dp", "ctx")),
            P(("dp", "ctx")),
            P(("dp", "ctx")),
            P(("dp", "ctx"), "tp"),
            P(("tp", "dp", "ctx")),
            P("tp", ("dp", "ctx")),
            P(("dp", "ctx")),
        ),
        out_specs=(
            P("dp", "ctx", None),
            P("dp", "ctx", None),
            P(("dp", "ctx")),
            P(("dp", "ctx")),
            P(("dp", "ctx"), None, "tp"),
            P(None, ("tp", "dp", "ctx")),
            P("tp", ("dp", "ctx")),
            P(("dp", "ctx")),
            P(("dp", "ctx")),
            P(("dp", "ctx")),
            P(("dp", "ctx"), "tp"),
            P(("tp", "dp", "ctx")),
            P("tp", ("dp", "ctx")),
            P(("dp", "ctx")),
        ),
        check_vma=False,
    )
```

```python
import functools

import jax
import jax.numpy as jnp
from jax import lax
from jax.experimental import pallas as pl
from jax.experimental.pallas import tpu as pltpu
from jax.sharding import PartitionSpec as P

HD = 64
NEG = -1e30
F32 = jnp.float32
BF16 = jnp.bfloat16


def dot(left, right, left_dim, right_dim):
    return lax.dot_general(
        left, right, (((left_dim,), (right_dim,)), ((), ())), preferred_element_type=F32
    )


def shape(dims, dtype):
    return jax.ShapeDtypeStruct(tuple(dims), dtype)


def call(kernel, name, scalars, ins, outs, scratch=(), flops=0, whole=None):
    first = [] if scalars is None else [scalars]
    specs, arrays, moved = [], [], 0
    for value in ins:
        if isinstance(value, tuple):
            value, dims, index = value
            specs.append(pl.BlockSpec(dims, lambda i, index=index: index))
            moved += value.dtype.itemsize * functools.reduce(lambda a, b: a * b, dims)
        else:
            specs.append(pl.BlockSpec(memory_space=pltpu.VMEM))
            moved += value.size * value.dtype.itemsize
        arrays.append(value)
    moved += sum(v.size * v.dtype.itemsize for v in outs)
    out_specs = [pl.BlockSpec(memory_space=pltpu.VMEM)] * len(outs)
    alias = {}
    if whole is not None:
        alias = {len(first) + len(arrays): len(outs)}
        specs.append(pl.BlockSpec(memory_space=pl.ANY))
        arrays.append(whole)
        outs = [*outs, shape(whole.shape, whole.dtype)]
        out_specs.append(pl.BlockSpec(memory_space=pl.ANY))
    return pl.pallas_call(
        kernel,
        grid=(1,),
        out_shape=tuple(outs),
        in_specs=[pl.BlockSpec(memory_space=pltpu.SMEM)] * len(first) + specs,
        out_specs=tuple(out_specs),
        input_output_aliases=alias,
        scratch_shapes=list(scratch),
        compiler_params=pltpu.CompilerParams(vmem_limit_bytes=56 << 20),
        cost_estimate=pl.CostEstimate(
            flops=flops, transcendentals=0, bytes_accessed=moved
        ),
        name=name,
    )(*first, *arrays)


def lanes(index, offset, size):
    return pl.ds(pl.multiple_of((index ^ offset) * size, size), size)


def rows_of(refs, low, high):
    return jnp.concatenate([ref[low:high, :] for ref in refs], axis=0)


def pack_kernel(attend_ref, *refs):
    smalls, (pair_ref, out_ref) = refs[:-2], refs[-2:]
    parts, block, width = attend_ref.shape
    for c in range(parts):
        out_ref[:block, c * width : (c + 1) * width] = attend_ref[c]
    size = smalls[0].shape[1]
    last = jnp.concatenate([pair_ref[0:1, :], pair_ref[1:2, :]], axis=1).astype(F32)
    last = jnp.concatenate([last, jnp.zeros((1, size - last.shape[1]), F32)], axis=1)
    rows = jnp.concatenate([ref[...].astype(F32) for ref in smalls] + [last], axis=0)
    out_ref[block:, :size] = rows.astype(BF16)
    out_ref[block:, size:] = jnp.zeros((8, parts * width - size), BF16)


def turn_kernel(expand_ref, shrink_ref, out_ref):
    block = expand_ref.shape[0]
    out_ref[:block, :] = expand_ref[...]
    out_ref[block:, :] = shrink_ref[...].T


def decode(order, head_block, index, first, start, size, wide_ref, expand_ref, attend_ref):
    total = jnp.zeros(attend_ref.shape, F32)
    for place, offset in enumerate(order):
        rows = first[place][start : start + 8, :size].astype(F32)
        wide_ref[:, place * size : (place + 1) * size] = rows
        expand_ref[:, lanes(index, offset, size)] = rows[6:7, :]
        flat = jnp.concatenate([rows[7:8, :head_block], rows[7:8, head_block : 2 * head_block]], 0)
        flat = jnp.concatenate(
            [flat, jnp.zeros((2, attend_ref.shape[1] - head_block), F32)], axis=1
        )
        flat = jnp.concatenate([flat, jnp.zeros((6, attend_ref.shape[1]), F32)], axis=0)
        total = total + pltpu.roll(flat, (index ^ offset) * head_block, 1)[:2]
    attend_ref[...] = total


def grad_order_kernel(order, count, scalars, cot_ref, keep_ref, *outs):
    index, tp = scalars[0], scalars[2]
    height, wide = outs[0].shape
    size = wide // len(order)
    for o in range(count):
        rows = pl.ds(pl.multiple_of((tp ^ o) * height, height), height)
        keep = keep_ref[rows, 0:1]
        for place, offset in enumerate(order):
            outs[o][:, place * size : (place + 1) * size] = (
                cot_ref[rows, lanes(index, offset, size)] * keep
            )


def project_kernel(order, block, head_block, scalars, x_ref, *refs):
    count = len(order)
    weights, refs = refs[:count], refs[count:]
    given, outs = refs[:-7], refs[-7:]
    normed_ref, query_ref, pair_ref, rows_ref = outs[:4]
    wide_ref, expand_ref, attend_ref = outs[4:]
    index, tp = scalars[0], scalars[2]
    q_len, wide = x_ref.shape
    size = wide // count
    for source, target in zip(given, outs[4:]):
        target[...] = source[...]
    if not given:
        decode(order, head_block, index, weights, block, size, wide_ref, expand_ref, attend_ref)
    width = query_ref.shape[1]
    weight = rows_of(weights, 0, block)
    step = min(q_len, 256)
    bias = jnp.concatenate(
        [attend_ref[0:1, :], jnp.zeros((1, width), F32), attend_ref[1:2, :]], axis=1
    )
    for start in range(0, q_len, step):
        rows = slice(start, start + step)
        value = x_ref[rows, :].astype(F32)
        mean = jnp.mean(value, axis=-1, keepdims=True)
        centered = value - mean
        inv = lax.rsqrt(jnp.mean(centered * centered, axis=-1, keepdims=True) + 1e-05)
        for place, offset in enumerate(order):
            plain = slice(place * size, (place + 1) * size)
            part = x_ref[rows, lanes(index, offset, size)].astype(F32)
            part = (part - mean) * inv * wide_ref[0:1, plain] + wide_ref[1:2, plain]
            normed_ref[rows, plain] = part.astype(BF16)
        made = dot(normed_ref[rows, :], weight, 1, 0) + bias
        query_ref[rows, :] = made[:, :width].astype(BF16)
        pair_ref[rows, :] = made[:, width:].astype(BF16)
    height = rows_ref.shape[0]
    mine = pl.ds(pl.multiple_of(tp * height, height), height)
    for place, offset in enumerate(order):
        plain = slice(place * size, (place + 1) * size)
        rows_ref[:, plain] = x_ref[mine, lanes(index, offset, size)]


def attend_kernel(heads, tq, tk, n_chunk, n_tp, scalars, lo_ref, q_ref, *refs):
    kv_refs = refs[:n_chunk]
    outs, refs = refs[n_chunk : n_chunk + n_tp], refs[n_chunk + n_tp :]
    lse_ref, qm_ref, acc_ref, m_ref, l_ref, mixed_ref = refs
    q_len, width = q_ref.shape
    ctx = scalars[1]
    lane = lax.broadcasted_iota(jnp.int32, (tq, width), 1)
    for qi in range(q_len // tq):
        rows = slice(qi * tq, (qi + 1) * tq)
        qv = q_ref[rows, :] * BF16(0.125)
        for h in range(heads):
            mine = (lane >= h * HD) & (lane < (h + 1) * HD)
            qm_ref[h * tq : (h + 1) * tq, :] = jnp.where(mine, qv, jnp.zeros_like(qv))
        acc_ref[...] = jnp.zeros_like(acc_ref)
        m_ref[...] = jnp.full(m_ref.shape, NEG, F32)
        l_ref[...] = jnp.zeros_like(l_ref)
        qbase = ctx * q_len + qi * tq
        qpos = qbase + lax.broadcasted_iota(jnp.int32, (1, tq), 1)
        lo = lo_ref[0:1, rows]
        lo_first = scalars[3 + qi]
        for c in range(n_chunk):
            kv = kv_refs[c]
            cbase = (ctx ^ c) * q_len

            def step(ki, carry, kv=kv, cbase=cbase):
                kb = cbase + ki * tk

                @pl.when((kb <= qbase + tq - 1) & (kb + tk - 1 >= lo_first))
                def _():
                    krows = pl.ds(pl.multiple_of(ki * tk, tk), tk)
                    k = kv[krows, 0:width]
                    vt = kv[krows, width : 2 * width].T
                    kpos = kb + lax.broadcasted_iota(jnp.int32, (tk, 1), 0)
                    ok = (kpos >= lo) & (kpos <= qpos)
                    ok = jnp.concatenate([ok] * heads, axis=1)
                    s = jnp.where(ok, dot(k, qm_ref[...], 1, 1), NEG)
                    m0 = m_ref[...]
                    m1 = jnp.maximum(m0, jnp.max(s, axis=0, keepdims=True))
                    p = jnp.exp(s - m1)
                    al = jnp.exp(m0 - m1)
                    l_ref[...] = l_ref[...] * al + jnp.sum(p, axis=0, keepdims=True)
                    m_ref[...] = m1
                    low = p.astype(BF16)
                    made = [
                        dot(vt[h * HD : (h + 1) * HD, :], low[:, h * tq : (h + 1) * tq], 1, 0)
                        for h in range(heads)
                    ]
                    acc_ref[...] = acc_ref[...] * al + jnp.concatenate(made, axis=1)

                return carry

            lax.fori_loop(0, q_len // tk, step, 0)
        lse = m_ref[...] + jnp.log(l_ref[...])
        out = acc_ref[...] / l_ref[...]
        for h in range(heads):
            cols = slice(h * tq, (h + 1) * tq)
            lse_ref[h : h + 1, rows] = lse[:, cols]
        out = jnp.concatenate([out[:, h * tq : (h + 1) * tq] for h in range(heads)], axis=0)
        mixed_ref[rows, :] = out.T.astype(BF16)
    for o in range(n_tp):
        outs[o][...] = mixed_ref[lanes(scalars[2], o, q_len // n_tp), :]


def attend_back_kernel(heads, tq, tk, n_chunk, n_tp, scalars, lo_ref, lse_ref, q_ref, *refs):
    kv_refs, refs = refs[:n_chunk], refs[n_chunk:]
    mixed_refs, refs = refs[:n_tp], refs[n_tp:]
    gm_refs, refs = refs[:n_tp], refs[n_tp:]
    dq_ref, refs = refs[0], refs[1:]
    dkv_refs, refs = refs[:n_chunk], refs[n_chunk:]
    qm_ref, gom_ref, dqt_ref, acck_ref, accv_ref, go_ref, mixed_ref, row_ref = refs
    q_len, width = q_ref.shape
    ctx, tp = scalars[1], scalars[2]
    for o in range(n_tp):
        go_ref[lanes(tp, o, q_len // n_tp), :] = gm_refs[o][...]
        mixed_ref[lanes(tp, o, q_len // n_tp), :] = mixed_refs[o][...]
    lane = lax.broadcasted_iota(jnp.int32, (tq, width), 1)
    nq = q_len // tq
    for qi in range(nq):
        rows = slice(qi * tq, (qi + 1) * tq)
        qv = q_ref[rows, :] * BF16(0.125)
        gv = go_ref[rows, :]
        prod = (gv.astype(F32) * mixed_ref[rows, :].astype(F32)).T
        for h in range(heads):
            cols = slice(h * tq, (h + 1) * tq)
            mine = (lane >= h * HD) & (lane < (h + 1) * HD)
            qm_ref[qi, cols, :] = jnp.where(mine, qv, jnp.zeros_like(qv))
            gom_ref[qi, cols, :] = jnp.where(mine, gv, jnp.zeros_like(gv))
            row_ref[qi, 0:1, cols] = lse_ref[h : h + 1, rows]
            row_ref[qi, 1:2, cols] = jnp.sum(
                prod[h * HD : (h + 1) * HD, :], axis=0, keepdims=True
            )
    dqt_ref[...] = jnp.zeros_like(dqt_ref)
    for c in range(n_chunk):
        kv = kv_refs[c]
        dkv = dkv_refs[c]
        cbase = (ctx ^ c) * q_len

        def step(ki, carry, kv=kv, dkv=dkv, cbase=cbase):
            kb = cbase + ki * tk
            krows = pl.ds(pl.multiple_of(ki * tk, tk), tk)
            live = [
                (kb <= ctx * q_len + (qi + 1) * tq - 1) & (kb + tk - 1 >= scalars[3 + qi])
                for qi in range(nq)
            ]
            some = functools.reduce(jnp.logical_or, live)

            @pl.when(jnp.logical_not(some))
            def _():
                dkv[krows, :] = jnp.zeros((tk, 2 * width), BF16)

            @pl.when(some)
            def _():
                acck_ref[...] = jnp.zeros_like(acck_ref)
                accv_ref[...] = jnp.zeros_like(accv_ref)
                k = kv[krows, 0:width]
                v = kv[krows, width : 2 * width]
                kt = k.T
                kpos = kb + lax.broadcasted_iota(jnp.int32, (tk, 1), 0)
                for qi in range(nq):

                    @pl.when(live[qi])
                    def _(qi=qi):
                        rows = slice(qi * tq, (qi + 1) * tq)
                        qpos = (
                            ctx * q_len + qi * tq + lax.broadcasted_iota(jnp.int32, (1, tq), 1)
                        )
                        ok = (kpos >= lo_ref[0:1, rows]) & (kpos <= qpos)
                        ok = jnp.concatenate([ok] * heads, axis=1)
                        s = dot(k, qm_ref[qi], 1, 1)
                        dp = dot(v, gom_ref[qi], 1, 1)
                        p = jnp.where(ok, jnp.exp(s - row_ref[qi, 0:1, :]), 0.0)
                        ds = (p * (dp - row_ref[qi, 1:2, :])).astype(BF16)
                        accv_ref[...] += dot(p.astype(BF16), gom_ref[qi], 1, 0)
                        acck_ref[...] += dot(ds, qm_ref[qi], 1, 0)
                        for h in range(heads):
                            hs = slice(h * HD, (h + 1) * HD)
                            dqt_ref[hs, rows] += dot(
                                kt[hs, :], ds[:, h * tq : (h + 1) * tq], 1, 0
                            )

                dkv[krows, 0:width] = acck_ref[...].astype(BF16)
                dkv[krows, width : 2 * width] = accv_ref[...].astype(BF16)

            return carry

        lax.fori_loop(0, q_len // tk, step, 0)
    for qi in range(nq):
        rows = slice(qi * tq, (qi + 1) * tq)
        dq_ref[rows, :] = (dqt_ref[:, rows].T * 0.125).astype(BF16)


def attend_scratch(heads, tile, q_len, width):
    return [
        pltpu.VMEM((heads * tile, width), BF16),
        pltpu.VMEM((HD, heads * tile), F32),
        pltpu.VMEM((1, heads * tile), F32),
        pltpu.VMEM((1, heads * tile), F32),
        pltpu.VMEM((q_len, width), BF16),
    ]


def attend_back_scratch(heads, tile, span, q_len, width):
    return [
        pltpu.VMEM((q_len // tile, heads * tile, width), BF16),
        pltpu.VMEM((q_len // tile, heads * tile, width), BF16),
        pltpu.VMEM((width, q_len), F32),
        pltpu.VMEM((span, width), F32),
        pltpu.VMEM((span, width), F32),
        pltpu.VMEM((q_len, width), BF16),
        pltpu.VMEM((q_len, width), BF16),
        pltpu.VMEM((q_len // tile, 2, heads * tile), F32),
    ]


def normal(value):
    mean = jnp.mean(value, axis=-1, keepdims=True)
    centered = value - mean
    inv = lax.rsqrt(jnp.mean(centered * centered, axis=-1, keepdims=True) + 1e-05)
    return centered * inv, inv


def normal_back(grad_out, norm, inv, gain):
    grad = grad_out * gain
    centered = grad - jnp.mean(grad, axis=-1, keepdims=True)
    return inv * (centered - norm * jnp.mean(grad * norm, axis=-1, keepdims=True))


def merge_kernel(n_tp, order, scalars, rows_ref, wide_ref, weight_ref, *refs):
    mixed, (hidden_ref, normed_ref) = refs[:n_tp], refs[n_tp:]
    index, tp = scalars[0], scalars[2]
    hidden_ref[...] = rows_ref[...].astype(F32) + wide_ref[2:3, :]
    for o, ref in enumerate(mixed):
        weight = jnp.concatenate([weight_ref[index ^ p, tp ^ o] for p in order], axis=1)
        hidden_ref[...] += dot(ref[...], weight, 1, 0)
    norm, _ = normal(hidden_ref[...])
    normed_ref[...] = (norm * wide_ref[3:4, :] + wide_ref[4:5, :]).astype(BF16)


def dense_kernel(count, expand_ref, *refs):
    normed, refs = refs[:count], refs[count:]
    grads, refs = refs[:count], refs[count:]
    weights, outs = refs[: -4 * count - 1], refs[-4 * count - 1 :]
    acts, pres, normed_outs, mlp_outs = (outs[i * count : (i + 1) * count] for i in range(4))
    sum_ref = outs[-1]
    block = weights[0].shape[0] // 2
    height = normed[0].shape[0]
    hidden = expand_ref.shape[1]
    step = min(hidden, 512)
    value = jnp.concatenate([ref[...] for ref in normed], axis=0)
    grad = jnp.concatenate([ref[...] for ref in grads], axis=0)
    back = forth = None
    for start in range(0, hidden, step):
        cols = slice(start, start + step)
        expand = jnp.concatenate([ref[:block, cols] for ref in weights], axis=0)
        shrink = jnp.concatenate([ref[block:, cols] for ref in weights], axis=0)
        pre = dot(value, expand, 1, 0) + expand_ref[:, cols]
        square = pre * pre
        inner = jnp.tanh(0.7978845608028654 * (pre + 0.044715 * square * pre))
        act = (0.5 * pre * (1.0 + inner)).astype(BF16)
        slope = 0.5 * (1.0 + inner) + (0.5 * 0.7978845608028654) * pre * (
            1.0 - inner * inner
        ) * (1.0 + (3.0 * 0.044715) * square)
        low = (dot(grad, shrink, 1, 0) * slope).astype(BF16)
        sum_ref[:, cols] = jnp.sum(low.astype(F32), axis=0, keepdims=True)
        for i in range(count):
            rows = slice(i * height, (i + 1) * height)
            acts[i][:, cols] = act[rows]
            pres[i][:, cols] = low[rows]
        more = dot(low, expand, 1, 1)
        also = dot(act, shrink, 1, 1)
        back = more if back is None else back + more
        forth = also if forth is None else forth + also
    for i in range(count):
        rows = slice(i * height, (i + 1) * height)
        normed_outs[i][...] = back[rows].astype(BF16)
        mlp_outs[i][...] = forth[rows].astype(BF16)


def hidden_back_kernel(
    count, n_tp, order, scalars, grad_ref, hidden_ref, wide_ref, weight_ref, *refs
):
    parts, refs = refs[:count], refs[count:]
    mixed, refs = refs[:n_tp], refs[n_tp:]
    direct = len(order) > 1
    refs = refs[1:] if direct else refs
    back_ref, low_ref, sums_ref = refs[:3]
    outs, refs = refs[3 : 3 + n_tp], refs[3 + n_tp :]
    index, tp = scalars[0], scalars[2]
    total = total_of(parts)
    norm, inv = normal(hidden_ref[...])
    grad = grad_ref[...].astype(F32)
    back = grad + normal_back(total, norm, inv, wide_ref[3:4, :])
    back_ref[...] = back
    low = back.astype(BF16)
    low_ref[...] = low
    copies = []
    if direct:
        buffer_ref, made_ref, sems = refs
        values = jnp.concatenate([ref[...] for ref in mixed], axis=1)
        tall = made_ref.shape[1]
        for place, offset in enumerate(order):
            left = low[:, place * tall : (place + 1) * tall]
            made_ref[place] = dot(left, values, 0, 0).astype(BF16)
            copies.append(
                pltpu.make_async_copy(
                    made_ref.at[place],
                    buffer_ref.at[index ^ offset, pl.ds(2 * tall, tall), :],
                    sems.at[place],
                )
            )
            copies[-1].start()
    for o in range(n_tp):
        weight = jnp.concatenate([weight_ref[index ^ p, tp ^ o] for p in order], axis=1)
        outs[o][...] = dot(low, weight, 1, 1).astype(BF16)
    sums_ref[...] = jnp.concatenate(
        [jnp.sum(v, axis=0, keepdims=True) for v in (back, total * norm, total, grad)], axis=0
    )
    for copy in copies:
        copy.wait()


def outer_kernel(order, spans, scalars, *refs):
    out_ref = refs[-1]
    tall = out_ref.shape[1] // (len(spans) + 1)
    base = 0
    for many, more in spans:
        left, refs = refs[:many], refs[many:]
        right, refs = refs[:more], refs[more:]
        a = jnp.concatenate([ref[...] for ref in left], axis=0)
        b = jnp.concatenate([ref[...] for ref in right], axis=0)
        for place, offset in enumerate(order):
            made = dot(a[:, place * tall : (place + 1) * tall], b, 0, 0).astype(BF16)
            out_ref[scalars[0] ^ offset, base : base + tall, :] = made
        base += tall


def join_kernel(left_ref, right_ref, out_ref):
    total = left_ref[...].astype(F32) + right_ref[...].astype(F32)
    out_ref[...] = total.astype(out_ref.dtype)


def sum_of(ref):
    total = ref[0].astype(F32)
    for i in range(1, ref.shape[0]):
        total = total + ref[i].astype(F32)
    return total


def dense_total_kernel(in_ref, expand_ref, shrink_ref, *outs):
    block = expand_ref.shape[0]
    expand_ref[...] = in_ref[:block, :].astype(F32)
    shrink_ref[...] = in_ref[block : 2 * block, :].astype(F32).T
    width = outs[0].shape[1]
    for o, ref in enumerate(outs):
        ref[...] = in_ref[2 * block :, o * width : (o + 1) * width]


def attend_total_kernel(in_ref, out_ref):
    parts, _, width = out_ref.shape
    for c in range(parts):
        out_ref[c] = in_ref[:, c * width : (c + 1) * width].astype(F32)


def total_of(refs):
    total = refs[0][...].astype(F32)
    for ref in refs[1:]:
        total = total + ref[...].astype(F32)
    return total


def join_layer_kernel(order, scalars, left_ref, right_ref, hidden_ref, wide_ref, *refs):
    total = left_ref[...].astype(F32) + right_ref[...].astype(F32)
    refs[-2][...] = total.astype(BF16)
    value = (hidden_ref[...] + total_of(refs[:-2]) + wide_ref[5:6, :]).astype(BF16)
    size = value.shape[1] // len(order)
    for place, offset in enumerate(order):
        cols = slice(place * size, (place + 1) * size)
        refs[-1][:, lanes(scalars[0], offset, size)] = value[:, cols]


def input_kernel(order, count, scalars, rows_ref, back_ref, wide_ref, *refs):
    parts, refs = refs[:count], refs[count:]
    extra, outs = refs[: len(refs) - count], refs[len(refs) - count :]
    total = total_of(parts)
    norm, inv = normal(rows_ref[...].astype(F32))
    value = (back_ref[...] + normal_back(total, norm, inv, wide_ref[0:1, :])).astype(BF16)
    height, wide = value.shape
    size = wide // len(order)
    for o, out_ref in enumerate(outs):
        for place, offset in enumerate(order):
            cols = lanes(scalars[0], offset, size)
            out_ref[:height, cols] = value[:, place * size : (place + 1) * size]
        if extra:
            tall, width = extra[o].shape
            tall = tall * width // wide
            for j in range(wide // width):
                out_ref[height:, j * width : (j + 1) * width] = extra[o][
                    j * tall : (j + 1) * tall, :
                ]


def first_sums_kernel(order, scalars, x_ref, *refs):
    parts, out_ref = refs[:-1], refs[-1]
    height, wide = parts[0].shape
    size = wide // len(order)
    out_ref[...] = jnp.zeros_like(out_ref)
    for o, ref in enumerate(parts):
        rows = lanes(scalars[2], o, height)
        value = x_ref[rows, :].astype(F32)
        mean = jnp.mean(value, axis=-1, keepdims=True)
        centered = value - mean
        inv = lax.rsqrt(jnp.mean(centered * centered, axis=-1, keepdims=True) + 1e-05)
        for place, offset in enumerate(order):
            cols = slice(place * size, (place + 1) * size)
            part = ref[:, cols].astype(F32)
            norm = (x_ref[rows, lanes(scalars[0], offset, size)].astype(F32) - mean) * inv
            out_ref[0:1, cols] += jnp.sum(part * norm, axis=0, keepdims=True)
            out_ref[1:2, cols] += jnp.sum(part, axis=0, keepdims=True)


def place_kernel(count, height, scalars, *refs):
    parts, outs = refs[:count], refs[count:]
    wide = parts[0].shape[1]
    for o, ref in enumerate(parts):
        outs[0][lanes(scalars[2], o, height), :] = ref[:height, :]
    if len(outs) > 1:
        width = outs[1].shape[0]
        tall = parts[0].shape[0] - height
        total = total_of([ref.at[height:, :] for ref in parts])
        for j in range(wide // width):
            outs[1][:, j * tall : (j + 1) * tall] = total[:, j * width : (j + 1) * width].T


def project_back_kernel(block, order, n_pair, n_tp, scalars, normed_ref, dq_ref, *refs):
    joined, refs = refs[:n_pair], refs[n_pair:]
    weights, refs = refs[: len(order)], refs[len(order) :]
    outs, (pair_ref, sums_ref, outer_ref) = refs[:n_tp], refs[n_tp:]
    pair = total_of(joined).astype(BF16)
    pair_ref[...] = pair
    width = dq_ref.shape[1]
    weight = rows_of(weights, 0, block)
    height = outs[0].shape[0]
    for o in range(n_tp):
        rows = lanes(scalars[2], o, height)
        both = jnp.concatenate([dq_ref[rows, :], pair_ref[rows, :]], axis=1)
        outs[o][...] = dot(both, weight, 1, 1).astype(BF16)
    sums_ref[...] = jnp.concatenate(
        [
            jnp.sum(v, axis=0, keepdims=True)
            for v in (dq_ref[...].astype(F32), pair[:, width:].astype(F32))
        ],
        axis=0,
    )
    tall = outer_ref.shape[1]
    both = jnp.concatenate([dq_ref[...], pair], axis=1)
    for place, offset in enumerate(order):
        rows = slice(place * tall, (place + 1) * tall)
        outer_ref[scalars[0] ^ offset] = dot(normed_ref[:, rows], both, 0, 0).astype(BF16)


def add_kernel(left_ref, right_ref, out_ref):
    out_ref[...] = left_ref[...].astype(F32) + right_ref[...].astype(F32)


def small_kernel(order, head_block, n_tp, scalars, two_ref, four_ref, attend_ref, *refs):
    index = scalars[0]
    out_ref = refs[-1]
    hidden = total_of(refs[:-1])
    size = out_ref.shape[2]
    attend = jnp.concatenate([attend_ref[...], jnp.zeros((6, attend_ref.shape[1]), F32)], axis=0)
    for place, offset in enumerate(order):
        cols = slice(place * size, (place + 1) * size)
        block = index ^ offset
        turned = pltpu.roll(attend, attend.shape[1] - block * head_block, 1)
        last = jnp.concatenate(
            [
                turned[0:1, :head_block],
                turned[1:2, :head_block],
                jnp.zeros((1, size - 2 * head_block), F32),
            ],
            axis=1,
        )
        mine = jnp.zeros((1, size), F32)
        for j in range(len(order)):
            mine = mine + jnp.where(block == j, hidden[:, j * size : (j + 1) * size], 0.0)
        made = jnp.concatenate([two_ref[:, cols], four_ref[:, cols], mine, last], axis=0)
        for o in range(n_tp):
            out_ref[block * n_tp + o] = made


def small_total_kernel(n_tp, scalars, in_ref, *outs):
    total = sum_of(in_ref)
    local = in_ref[scalars[2]]
    for i in range(1, in_ref.shape[0] // n_tp):
        local = local + in_ref[i * n_tp + scalars[2]]
    for i in range(6):
        outs[i][...] = total[i : i + 1, :]
    outs[6][...] = local[6:7, :]
    size = outs[7].shape[1]
    outs[7][...] = jnp.concatenate([local[7:8, :size], local[7:8, size : 2 * size]], axis=0)


def after(value, *others):
    return lax.optimization_barrier((value, *others))[0]


def body(
    sizes,
    layer_input,
    cotangent,
    segment_ids,
    norm1_gain,
    norm1_bias,
    attend_weight,
    attend_bias,
    merge_weight,
    merge_bias,
    norm2_gain,
    norm2_bias,
    expand_weight,
    expand_bias,
    shrink_weight,
    shrink_bias,
):
    n_dp, n_ctx, n_tp = sizes
    group = n_dp * n_ctx
    seqs, q_len, wide = layer_input.shape
    assert seqs == 1
    block = wide // group
    width = attend_weight.shape[2]
    heads = width // HD
    hidden_width = expand_weight.shape[1]
    height = q_len // n_tp
    bias_block = expand_bias.shape[0]
    head_block = attend_bias.shape[1]
    tile = min(256, q_len)
    direct = (n_dp, n_ctx) == (2, 4) and block % 128 == 0
    direct = direct and bias_block == block and 2 * head_block <= block
    order = [0, 2, 4, 6, 1, 3, 5, 7] if direct else [0]
    ctx = lax.axis_index("ctx")
    tp = lax.axis_index("tp")
    me = lax.axis_index("dp") * n_ctx + ctx if direct else 0 * ctx
    plane = ("dp", "ctx")

    def plane_swap(value, offset):
        return lax.ppermute(value, plane, [(i, i ^ offset) for i in range(group)])

    def ctx_swap(value, offset):
        return lax.ppermute(value, "ctx", [(i, i ^ offset) for i in range(n_ctx)])

    def tp_swap(value, offset):
        return lax.ppermute(value, "tp", [(i, i ^ offset) for i in range(n_tp)])

    def with_cores(even):
        return even + [ctx_swap(v, 1) for v in even]

    def tp_gather(value):
        return [value] + [tp_swap(value, o) for o in range(1, n_tp)]

    def tp_relay(value):
        parts = [value, tp_swap(value, 1)]
        for step in (2 ** i for i in range(1, n_tp.bit_length() - 1)):
            far = tp_swap(value, step)
            parts += [far, tp_swap(far, 1)] + [tp_swap(value, o) for o in range(step + 2, 2 * step)]
        return parts

    def tp_exchange(parts):
        return [parts[0]] + [tp_swap(parts[o], o) for o in range(1, n_tp)]

    seg_all = segment_ids[0]
    seg_query = lax.dynamic_slice_in_dim(seg_all, ctx * q_len, q_len, 0)
    lows = jnp.sum(
        (seg_all[:, None] < seg_query[None, :]).astype(jnp.int32), axis=0, keepdims=True
    )
    place = jnp.stack([me, ctx, tp]).astype(jnp.int32)
    limits = jnp.concatenate([place, lows[0, ::tile]], axis=0)
    keep = jnp.broadcast_to((seg_query > 0).astype(BF16)[:, None], (q_len, 128))

    smalls = (
        norm1_gain,
        norm1_bias,
        merge_bias,
        norm2_gain,
        norm2_bias,
        shrink_bias,
        expand_bias,
    )
    if direct:
        (pack,) = call(
            pack_kernel,
            "pack",
            None,
            [jnp.swapaxes(attend_weight, 0, 1)]
            + [jnp.reshape(v, (1, block)) for v in smalls]
            + [attend_bias],
            [shape((block + 8, 3 * width), BF16)],
        )
        far = [plane_swap(pack, o) for o in order[1:4]]
        first = with_cores([after(v, limits, keep) for v in [pack] + far])
        merge_all = lax.all_gather(merge_weight, ("dp", "ctx", "tp"), axis=0)
        merge_all = jnp.reshape(merge_all, (group, n_tp, width, block))
        given = []
    else:

        def whole(value, axis):
            return lax.all_gather(value, plane, axis=axis, tiled=True)

        first = [jnp.reshape(whole(attend_weight, 0), (wide, 3 * width))]
        merge_all = whole(lax.all_gather(merge_weight, "tp", axis=0), 2)[None]
        dense_all = [jnp.concatenate([whole(expand_weight, 0), whole(shrink_weight.T, 0)], 0)]
        wide_rows = whole(jnp.stack(smalls[:6]), 1).astype(F32)
        given = [
            jnp.pad(wide_rows, ((0, 2), (0, 0))),
            whole(expand_bias, 0).astype(F32)[None],
            whole(attend_bias, 1).astype(F32),
        ]
    span = block if direct else wide

    normed1, query, pair, input_rows, wide_rows, expand_add, attend_add = call(
        functools.partial(project_kernel, order, span, head_block),
        "project",
        place,
        [layer_input[0], *first, *given],
        [
            shape((q_len, wide), BF16),
            shape((q_len, width), BF16),
            shape((q_len, 2 * width), BF16),
            shape((height, wide), BF16),
            shape((8, wide), F32),
            shape((1, hidden_width), F32),
            shape((2, width), F32),
        ],
        flops=6 * q_len * wide * width,
    )
    grad_rows = call(
        functools.partial(grad_order_kernel, order, n_tp),
        "order_grad",
        place,
        [after(cotangent[0], pair), keep],
        [shape((height, wide), BF16)] * n_tp,
    )
    ready = [grad_rows[0], limits]
    if direct:
        (dense_rows,) = call(
            turn_kernel,
            "turn",
            None,
            [after(expand_weight, pair), shrink_weight],
            [shape((2 * block, hidden_width), BF16)],
        )
        ready.append(dense_rows)
    near = [pair] + [ctx_swap(pair, o) for o in range(2, n_ctx, 2)]
    pairs = []
    for value in near:
        if pairs:
            value = after(value, *ready)
        pairs += [value, ctx_swap(value, 1)]
    if direct:
        dense_y = plane_swap(dense_rows, 4)
        pairs[-1] = after(pairs[-1], dense_y)
        dense_x, dense_xy = (plane_swap(after(dense_rows, near[1]), o) for o in (2, 6))
    out = call(
        functools.partial(attend_kernel, heads, tile, min(512, q_len), n_ctx, n_tp),
        "attention",
        limits,
        [lows, query, *pairs],
        [shape((height, width), BF16)] * n_tp + [shape((heads, q_len), F32)],
        attend_scratch(heads, tile, q_len, width),
        flops=4 * q_len * q_len * n_ctx * width,
    )
    mixed, lse = out[:n_tp], out[n_tp]
    mixed_rows = tp_exchange(mixed)
    hidden, normed2 = call(
        functools.partial(merge_kernel, n_tp, order),
        "merge",
        place,
        [input_rows, wide_rows, merge_all, *mixed_rows],
        [shape((height, wide), F32), shape((height, wide), BF16)],
        flops=2 * height * wide * wide,
    )

    if direct:
        dense_rows, dense_y = (after(v, mixed[0]) for v in (dense_rows, dense_y))
        dense_x, dense_xy = (after(v, normed2) for v in (dense_x, dense_xy))
        dense_all = with_cores([dense_rows, dense_x, dense_y, dense_xy])
    normed_all = tp_relay(normed2)
    picks = [[o for o in range(n_tp) if o % 4 in (0, 2)], [o for o in range(n_tp) if o % 4 in (1, 3)]]
    acts, pres, parts, mlps = ([None] * n_tp for _ in range(4))
    sums = []
    for pick in picks:
        count = len(pick)
        if sums:
            normed_all[3] = after(normed_all[3], sums[0])
        out = call(
            functools.partial(dense_kernel, count),
            "dense",
            None,
            [expand_add]
            + [normed_all[o] for o in pick]
            + [grad_rows[o] for o in pick]
            + dense_all,
            [shape((height, hidden_width), BF16)] * (2 * count)
            + [shape((height, wide), BF16)] * (2 * count)
            + [shape((1, hidden_width), F32)],
            flops=8 * count * height * wide * hidden_width,
        )
        for i, o in enumerate(pick):
            acts[o], pres[o], parts[o], mlps[o] = (out[j * count + i] for j in range(4))
        sums.append(out[-1])
    grad_parts = tp_exchange(parts)
    dense_outer = None
    if direct:
        (dense_outer,) = call(
            functools.partial(outer_kernel, order, [(n_tp, n_tp)] * 2),
            "dense_outer",
            place,
            [*normed_all, *pres, *grad_rows, *acts],
            [shape((group, 3 * block, hidden_width), BF16)],
            flops=4 * wide * hidden_width * q_len,
        )
        grad_parts[2] = after(grad_parts[2], dense_outer)
    (grad_near,) = call(
        add_kernel, "add", None, [grad_parts[0], grad_parts[2]], [shape((height, wide), F32)]
    )
    grad_parts = [grad_near] + [grad_parts[o] for o in range(1, n_tp) if o != 2]
    out = call(
        functools.partial(hidden_back_kernel, len(grad_parts), n_tp, order),
        "hidden_back",
        place,
        [grad_rows[0], hidden, wide_rows, merge_all, *grad_parts, *mixed_rows],
        [
            shape((height, wide), F32),
            shape((height, wide), BF16),
            shape((4, wide), F32),
        ]
        + [shape((height, width), BF16)] * n_tp,
        [pltpu.VMEM((group, block, wide), BF16), pltpu.SemaphoreType.DMA((group,))]
        if direct
        else [],
        flops=2 * height * wide * wide,
        whole=dense_outer,
    )
    if direct:
        dense_outer = out[-1]
        out = out[:-1]
    hidden_grad, grad_attn, four, grad_mixed = out[0], out[1], out[2], tp_exchange(out[3:])
    mlps = tp_exchange([mlps[0]] + [after(v, hidden_grad) for v in mlps[1:]])

    out = call(
        functools.partial(attend_back_kernel, heads, tile, tile, n_ctx, n_tp),
        "attention_back",
        limits,
        [lows, lse, query, *pairs, *mixed, *grad_mixed],
        [shape((q_len, width), BF16)] + [shape((q_len, 2 * width), BF16)] * n_ctx,
        attend_back_scratch(heads, tile, tile, q_len, width),
        flops=10 * q_len * q_len * n_ctx * width,
    )
    grad_query, grad_pairs = out[0], out[1:]
    joined = []
    for o in reversed(range(0, n_ctx, 2)):
        if joined:
            other = after(ctx_swap(grad_pairs[o + 1], 1), joined[-1])
            (total,) = call(
                join_kernel, "join", None, [other, grad_pairs[o]], [shape(other.shape, BF16)]
            )
        else:
            other = ctx_swap(after(grad_pairs[o + 1], *mlps), 1)
            total, layer_part = call(
                functools.partial(join_layer_kernel, order),
                "join_layer",
                place,
                [other, grad_pairs[o], hidden, wide_rows, *mlps],
                [shape(other.shape, BF16), shape((height, wide), BF16)],
            )
        joined.append(total)
    joined = joined[::-1]
    layer_parts = tp_relay(layer_part)
    joined = [joined[0]] + [ctx_swap(v, 2 * i) for i, v in enumerate(joined) if i]
    joined[-1] = after(joined[-1], layer_parts[1], layer_parts[2])
    out = call(
        functools.partial(project_back_kernel, span, order, len(joined), n_tp),
        "project_back",
        place,
        [normed1, grad_query, *joined, *first],
        [shape((height, wide), BF16)] * n_tp
        + [
            shape((q_len, 2 * width), BF16),
            shape((2, width), F32),
            shape((len(order), span, 3 * width), BF16),
        ],
        flops=12 * q_len * wide * width,
    )
    normed1_parts, (grad_pair, attend_sums, attend_outer) = out[:n_tp], out[n_tp:]
    (two,) = call(
        functools.partial(first_sums_kernel, order),
        "first_sums",
        place,
        [layer_input[0], *normed1_parts],
        [shape((2, wide), F32)],
    )
    normed1_parts = tp_exchange(normed1_parts)

    def scattered(value):
        flat = jnp.reshape(value, (-1, value.shape[-1]))
        return lax.psum_scatter(flat, plane, scatter_dimension=0, tiled=True)

    if direct:
        attend_part = scattered(attend_outer)
        out = call(
            dense_total_kernel,
            "dense_total",
            None,
            [after(scattered(dense_outer), grad_pair)],
            [shape((block, hidden_width), F32), shape((hidden_width, block), F32)]
            + [shape((block, width), BF16)] * n_tp,
        )
        grad_expand, grad_shrink, merge_parts = out[0], out[1], out[2:]
        normed1_parts[-1] = after(normed1_parts[-1], grad_expand, two)
    else:
        merge_parts = []
    low = block * width // wide if direct else 0
    input_parts = call(
        functools.partial(input_kernel, order, n_tp),
        "input_back",
        place,
        [input_rows, hidden_grad, wide_rows, *normed1_parts, *merge_parts],
        [shape((height + low, wide), BF16)] * n_tp,
    )
    input_part = input_parts[0]
    input_parts = tp_exchange(input_parts)

    def placed(parts, outs=()):
        return call(
            functools.partial(place_kernel, n_tp, height),
            "place",
            place,
            parts,
            [shape((q_len, wide), BF16), *outs],
        )

    (layer_output,) = placed(layer_parts)

    if direct:
        (grad_attend,) = call(
            attend_total_kernel,
            "attend_total",
            None,
            [attend_part],
            [shape((3, block, width), F32)],
        )
        (small,) = call(
            functools.partial(small_kernel, order, head_block, n_tp),
            "small",
            place,
            [two, four, attend_sums, *sums],
            [shape((group * n_tp, 8, block), F32)],
        )
        table = call(
            functools.partial(small_total_kernel, n_tp),
            "small_total",
            place,
            [lax.all_to_all(after(small, input_part), ("dp", "ctx", "tp"), 0, 0)],
            [shape((1, block), F32)] * 7 + [shape((2, head_block), F32)],
        )
        rows = [jnp.reshape(v, (block,)) for v in table[:7]]
        expand_sum, attend_sum = rows[6], table[7]
        input_parts[-1] = after(input_parts[-1], grad_attend, layer_output, *table)
        grad_attend = jnp.swapaxes(grad_attend, 0, 1)
    else:

        def cut(value, axis):
            return lax.psum_scatter(value, plane, scatter_dimension=axis, tiled=True)

        def outer_of(left, right):
            return cut(
                dot(jnp.concatenate(left), jnp.concatenate(right), 0, 0).astype(BF16), 0
            ).astype(F32)

        grad_expand = outer_of(normed_all, pres)
        grad_shrink = outer_of(grad_rows, acts).T
        grad_merge = outer_of([grad_attn], [jnp.concatenate(mixed_rows, axis=1)]).astype(BF16)
        grad_merge = [grad_merge[:, o * width : (o + 1) * width] for o in range(n_tp)]
        grad_merge = sum(v.astype(F32) for v in tp_exchange(grad_merge)).T
        grad_attend = jnp.reshape(cut(attend_outer[0], 0).astype(F32), (block, 3, width))
        table = lax.psum(cut(jnp.concatenate([two, four], axis=0), 1), "tp")
        rows = [table[i] for i in range(6)]
        expand_sum = cut(sum(sums)[0], 0)
        attend_sum = cut(attend_sums, 1)
    if direct:
        input_grad, grad_merge = placed(input_parts, [shape((width, block), F32)])
    else:
        (input_grad,) = placed(input_parts)
    return (
        layer_output[None],
        input_grad[None],
        rows[0],
        rows[1],
        grad_attend,
        attend_sum,
        grad_merge,
        rows[2],
        rows[3],
        rows[4],
        grad_expand,
        expand_sum,
        grad_shrink,
        rows[5],
    )


def solution(mesh):
    sizes = (mesh.shape["dp"], mesh.shape["ctx"], mesh.shape["tp"])
    return jax.shard_map(
        functools.partial(body, sizes),
        mesh=mesh,
        in_specs=(
            P("dp", "ctx", None),
            P("dp", "ctx", None),
            P("dp", None),
            P(("dp", "ctx")),
            P(("dp", "ctx")),
            P(("dp", "ctx"), None, "tp"),
            P(None, ("tp", "dp", "ctx")),
            P("tp", ("dp", "ctx")),
            P(("dp", "ctx")),
            P(("dp", "ctx")),
            P(("dp", "ctx")),
            P(("dp", "ctx"), "tp"),
            P(("tp", "dp", "ctx")),
            P("tp", ("dp", "ctx")),
            P(("dp", "ctx")),
        ),
        out_specs=(
            P("dp", "ctx", None),
            P("dp", "ctx", None),
            P(("dp", "ctx")),
            P(("dp", "ctx")),
            P(("dp", "ctx"), None, "tp"),
            P(None, ("tp", "dp", "ctx")),
            P("tp", ("dp", "ctx")),
            P(("dp", "ctx")),
            P(("dp", "ctx")),
            P(("dp", "ctx")),
            P(("dp", "ctx"), "tp"),
            P(("tp", "dp", "ctx")),
            P("tp", ("dp", "ctx")),
            P(("dp", "ctx")),
        ),
        check_vma=False,
    )
```

```python
import functools

import jax
import jax.numpy as jnp
from jax import lax
from jax.experimental import pallas as pl
from jax.experimental.pallas import tpu as pltpu
from jax.sharding import PartitionSpec as P

HD = 64
NEG = -1e30
F32 = jnp.float32
BF16 = jnp.bfloat16


def dot(left, right, left_dim, right_dim):
    return lax.dot_general(
        left, right, (((left_dim,), (right_dim,)), ((), ())), preferred_element_type=F32
    )


def shape(dims, dtype):
    return jax.ShapeDtypeStruct(tuple(dims), dtype)


def call(kernel, name, scalars, ins, outs, scratch=(), flops=0, whole=None):
    first = [] if scalars is None else [scalars]
    specs, arrays, moved = [], [], 0
    for value in ins:
        if isinstance(value, tuple):
            value, dims, index = value
            specs.append(pl.BlockSpec(dims, lambda i, index=index: index))
            moved += value.dtype.itemsize * functools.reduce(lambda a, b: a * b, dims)
        else:
            specs.append(pl.BlockSpec(memory_space=pltpu.VMEM))
            moved += value.size * value.dtype.itemsize
        arrays.append(value)
    moved += sum(v.size * v.dtype.itemsize for v in outs)
    out_specs = [pl.BlockSpec(memory_space=pltpu.VMEM)] * len(outs)
    alias = {}
    if whole is not None:
        alias = {len(first) + len(arrays): len(outs)}
        specs.append(pl.BlockSpec(memory_space=pl.ANY))
        arrays.append(whole)
        outs = [*outs, shape(whole.shape, whole.dtype)]
        out_specs.append(pl.BlockSpec(memory_space=pl.ANY))
    return pl.pallas_call(
        kernel,
        grid=(1,),
        out_shape=tuple(outs),
        in_specs=[pl.BlockSpec(memory_space=pltpu.SMEM)] * len(first) + specs,
        out_specs=tuple(out_specs),
        input_output_aliases=alias,
        scratch_shapes=list(scratch),
        compiler_params=pltpu.CompilerParams(vmem_limit_bytes=56 << 20),
        cost_estimate=pl.CostEstimate(
            flops=flops, transcendentals=0, bytes_accessed=moved
        ),
        name=name,
    )(*first, *arrays)


def lanes(index, offset, size):
    return pl.ds(pl.multiple_of((index ^ offset) * size, size), size)


def rows_of(refs, low, high):
    return jnp.concatenate([ref[low:high, :] for ref in refs], axis=0)


def pack_kernel(attend_ref, *refs):
    smalls, (pair_ref, out_ref) = refs[:-2], refs[-2:]
    parts, block, width = attend_ref.shape
    for c in range(parts):
        out_ref[:block, c * width : (c + 1) * width] = attend_ref[c]
    size = smalls[0].shape[1]
    last = jnp.concatenate([pair_ref[0:1, :], pair_ref[1:2, :]], axis=1).astype(F32)
    last = jnp.concatenate([last, jnp.zeros((1, size - last.shape[1]), F32)], axis=1)
    rows = jnp.concatenate([ref[...].astype(F32) for ref in smalls] + [last], axis=0)
    out_ref[block:, :size] = rows.astype(BF16)
    out_ref[block:, size:] = jnp.zeros((8, parts * width - size), BF16)


def turn_kernel(expand_ref, shrink_ref, out_ref):
    block = expand_ref.shape[0]
    out_ref[:block, :] = expand_ref[...]
    out_ref[block:, :] = shrink_ref[...].T


def decode(order, head_block, index, first, start, size, wide_ref, expand_ref, attend_ref):
    total = jnp.zeros(attend_ref.shape, F32)
    for place, offset in enumerate(order):
        rows = first[place][start : start + 8, :size].astype(F32)
        wide_ref[:, place * size : (place + 1) * size] = rows
        expand_ref[:, lanes(index, offset, size)] = rows[6:7, :]
        flat = jnp.concatenate([rows[7:8, :head_block], rows[7:8, head_block : 2 * head_block]], 0)
        flat = jnp.concatenate(
            [flat, jnp.zeros((2, attend_ref.shape[1] - head_block), F32)], axis=1
        )
        flat = jnp.concatenate([flat, jnp.zeros((6, attend_ref.shape[1]), F32)], axis=0)
        total = total + pltpu.roll(flat, (index ^ offset) * head_block, 1)[:2]
    attend_ref[...] = total


def grad_order_kernel(order, count, scalars, cot_ref, keep_ref, *outs):
    index, tp = scalars[0], scalars[2]
    height, wide = outs[0].shape
    size = wide // len(order)
    for o in range(count):
        rows = pl.ds(pl.multiple_of((tp ^ o) * height, height), height)
        keep = keep_ref[rows, 0:1]
        for place, offset in enumerate(order):
            outs[o][:, place * size : (place + 1) * size] = (
                cot_ref[rows, lanes(index, offset, size)] * keep
            )


def project_kernel(order, block, head_block, scalars, x_ref, *refs):
    count = len(order)
    weights, refs = refs[:count], refs[count:]
    given, outs = refs[:-7], refs[-7:]
    normed_ref, query_ref, pair_ref, rows_ref = outs[:4]
    wide_ref, expand_ref, attend_ref = outs[4:]
    index, tp = scalars[0], scalars[2]
    q_len, wide = x_ref.shape
    size = wide // count
    for source, target in zip(given, outs[4:]):
        target[...] = source[...]
    if not given:
        decode(order, head_block, index, weights, block, size, wide_ref, expand_ref, attend_ref)
    width = query_ref.shape[1]
    weight = rows_of(weights, 0, block)
    step = min(q_len, 256)
    bias = jnp.concatenate(
        [attend_ref[0:1, :], jnp.zeros((1, width), F32), attend_ref[1:2, :]], axis=1
    )
    for start in range(0, q_len, step):
        rows = slice(start, start + step)
        value = x_ref[rows, :].astype(F32)
        mean = jnp.mean(value, axis=-1, keepdims=True)
        centered = value - mean
        inv = lax.rsqrt(jnp.mean(centered * centered, axis=-1, keepdims=True) + 1e-05)
        for place, offset in enumerate(order):
            plain = slice(place * size, (place + 1) * size)
            part = x_ref[rows, lanes(index, offset, size)].astype(F32)
            part = (part - mean) * inv * wide_ref[0:1, plain] + wide_ref[1:2, plain]
            normed_ref[rows, plain] = part.astype(BF16)
        made = dot(normed_ref[rows, :], weight, 1, 0) + bias
        query_ref[rows, :] = made[:, :width].astype(BF16)
        pair_ref[rows, :] = made[:, width:].astype(BF16)
    height = rows_ref.shape[0]
    mine = pl.ds(pl.multiple_of(tp * height, height), height)
    for place, offset in enumerate(order):
        plain = slice(place * size, (place + 1) * size)
        rows_ref[:, plain] = x_ref[mine, lanes(index, offset, size)]


def attend_kernel(heads, tq, tk, n_chunk, n_tp, scalars, lo_ref, q_ref, *refs):
    kv_refs = refs[:n_chunk]
    outs, refs = refs[n_chunk : n_chunk + n_tp], refs[n_chunk + n_tp :]
    lse_ref, qm_ref, acc_ref, m_ref, l_ref, mixed_ref = refs
    q_len, width = q_ref.shape
    ctx = scalars[1]
    lane = lax.broadcasted_iota(jnp.int32, (tq, width), 1)

    def tile(qi, carry):
        rows = pl.ds(pl.multiple_of(qi * tq, tq), tq)
        qv = q_ref[rows, :] * BF16(0.125)
        for h in range(heads):
            mine = (lane >= h * HD) & (lane < (h + 1) * HD)
            qm_ref[h * tq : (h + 1) * tq, :] = jnp.where(mine, qv, jnp.zeros_like(qv))
        acc_ref[...] = jnp.zeros_like(acc_ref)
        m_ref[...] = jnp.full(m_ref.shape, NEG, F32)
        l_ref[...] = jnp.zeros_like(l_ref)
        qbase = ctx * q_len + qi * tq
        qpos = qbase + lax.broadcasted_iota(jnp.int32, (1, tq), 1)
        lo = lo_ref[0:1, rows]
        lo_first = scalars[3 + qi]
        for c in range(n_chunk):
            kv = kv_refs[c]
            cbase = (ctx ^ c) * q_len

            def step(ki, carry, kv=kv, cbase=cbase):
                kb = cbase + ki * tk

                @pl.when((kb <= qbase + tq - 1) & (kb + tk - 1 >= lo_first))
                def _():
                    krows = pl.ds(pl.multiple_of(ki * tk, tk), tk)
                    k = kv[krows, 0:width]
                    vt = kv[krows, width : 2 * width].T
                    kpos = kb + lax.broadcasted_iota(jnp.int32, (tk, 1), 0)
                    ok = (kpos >= lo) & (kpos <= qpos)
                    ok = jnp.concatenate([ok] * heads, axis=1)
                    s = jnp.where(ok, dot(k, qm_ref[...], 1, 1), NEG)
                    m0 = m_ref[...]
                    m1 = jnp.maximum(m0, jnp.max(s, axis=0, keepdims=True))
                    p = jnp.exp(s - m1)
                    al = jnp.exp(m0 - m1)
                    l_ref[...] = l_ref[...] * al + jnp.sum(p, axis=0, keepdims=True)
                    m_ref[...] = m1
                    low = p.astype(BF16)
                    made = [
                        dot(vt[h * HD : (h + 1) * HD, :], low[:, h * tq : (h + 1) * tq], 1, 0)
                        for h in range(heads)
                    ]
                    acc_ref[...] = acc_ref[...] * al + jnp.concatenate(made, axis=1)

                return carry

            lax.fori_loop(0, q_len // tk, step, 0)
        lse = m_ref[...] + jnp.log(l_ref[...])
        out = acc_ref[...] / l_ref[...]
        for h in range(heads):
            cols = slice(h * tq, (h + 1) * tq)
            lse_ref[h : h + 1, rows] = lse[:, cols]
        out = jnp.concatenate([out[:, h * tq : (h + 1) * tq] for h in range(heads)], axis=0)
        mixed_ref[rows, :] = out.T.astype(BF16)
        return carry

    lax.fori_loop(0, q_len // tq, tile, 0)
    for o in range(n_tp):
        outs[o][...] = mixed_ref[lanes(scalars[2], o, q_len // n_tp), :]


def attend_back_kernel(heads, tq, tk, n_chunk, n_tp, scalars, lo_ref, lse_ref, q_ref, *refs):
    kv_refs, refs = refs[:n_chunk], refs[n_chunk:]
    mixed_refs, refs = refs[:n_tp], refs[n_tp:]
    gm_refs, refs = refs[:n_tp], refs[n_tp:]
    dq_ref, refs = refs[0], refs[1:]
    dkv_refs, refs = refs[:n_chunk], refs[n_chunk:]
    qm_ref, gom_ref, dqt_ref, acck_ref, accv_ref, go_ref, mixed_ref, row_ref = refs
    q_len, width = q_ref.shape
    ctx, tp = scalars[1], scalars[2]
    for o in range(n_tp):
        go_ref[lanes(tp, o, q_len // n_tp), :] = gm_refs[o][...]
        mixed_ref[lanes(tp, o, q_len // n_tp), :] = mixed_refs[o][...]
    lane = lax.broadcasted_iota(jnp.int32, (tq, width), 1)
    nq = q_len // tq

    def ready(qi, carry):
        rows = pl.ds(pl.multiple_of(qi * tq, tq), tq)
        qv = q_ref[rows, :] * BF16(0.125)
        gv = go_ref[rows, :]
        prod = (gv.astype(F32) * mixed_ref[rows, :].astype(F32)).T
        for h in range(heads):
            cols = slice(h * tq, (h + 1) * tq)
            mine = (lane >= h * HD) & (lane < (h + 1) * HD)
            qm_ref[qi, cols, :] = jnp.where(mine, qv, jnp.zeros_like(qv))
            gom_ref[qi, cols, :] = jnp.where(mine, gv, jnp.zeros_like(gv))
            row_ref[qi, 0:1, cols] = lse_ref[h : h + 1, rows]
            row_ref[qi, 1:2, cols] = jnp.sum(
                prod[h * HD : (h + 1) * HD, :], axis=0, keepdims=True
            )
        return carry

    lax.fori_loop(0, nq, ready, 0)
    dqt_ref[...] = jnp.zeros_like(dqt_ref)
    for c in range(n_chunk):
        kv = kv_refs[c]
        dkv = dkv_refs[c]
        cbase = (ctx ^ c) * q_len

        def step(ki, carry, kv=kv, dkv=dkv, cbase=cbase):
            kb = cbase + ki * tk
            krows = pl.ds(pl.multiple_of(ki * tk, tk), tk)
            live = [
                (kb <= ctx * q_len + (qi + 1) * tq - 1) & (kb + tk - 1 >= scalars[3 + qi])
                for qi in range(nq)
            ]
            some = functools.reduce(jnp.logical_or, live)

            @pl.when(jnp.logical_not(some))
            def _():
                dkv[krows, :] = jnp.zeros((tk, 2 * width), BF16)

            @pl.when(some)
            def _():
                acck_ref[...] = jnp.zeros_like(acck_ref)
                accv_ref[...] = jnp.zeros_like(accv_ref)
                k = kv[krows, 0:width]
                v = kv[krows, width : 2 * width]
                kt = k.T
                kpos = kb + lax.broadcasted_iota(jnp.int32, (tk, 1), 0)

                def tile(qi, carry):
                    qbase = ctx * q_len + qi * tq

                    @pl.when((kb <= qbase + tq - 1) & (kb + tk - 1 >= scalars[3 + qi]))
                    def _():
                        rows = pl.ds(pl.multiple_of(qi * tq, tq), tq)
                        qpos = qbase + lax.broadcasted_iota(jnp.int32, (1, tq), 1)
                        ok = (kpos >= lo_ref[0:1, rows]) & (kpos <= qpos)
                        ok = jnp.concatenate([ok] * heads, axis=1)
                        s = dot(k, qm_ref[qi], 1, 1)
                        dp = dot(v, gom_ref[qi], 1, 1)
                        p = jnp.where(ok, jnp.exp(s - row_ref[qi, 0:1, :]), 0.0)
                        ds = (p * (dp - row_ref[qi, 1:2, :])).astype(BF16)
                        accv_ref[...] += dot(p.astype(BF16), gom_ref[qi], 1, 0)
                        acck_ref[...] += dot(ds, qm_ref[qi], 1, 0)
                        for h in range(heads):
                            hs = slice(h * HD, (h + 1) * HD)
                            dqt_ref[hs, rows] += dot(
                                kt[hs, :], ds[:, h * tq : (h + 1) * tq], 1, 0
                            )

                    return carry

                lax.fori_loop(0, nq, tile, 0)
                dkv[krows, 0:width] = acck_ref[...].astype(BF16)
                dkv[krows, width : 2 * width] = accv_ref[...].astype(BF16)

            return carry

        lax.fori_loop(0, q_len // tk, step, 0)
    for qi in range(nq):
        rows = slice(qi * tq, (qi + 1) * tq)
        dq_ref[rows, :] = (dqt_ref[:, rows].T * 0.125).astype(BF16)


def attend_scratch(heads, tile, q_len, width):
    return [
        pltpu.VMEM((heads * tile, width), BF16),
        pltpu.VMEM((HD, heads * tile), F32),
        pltpu.VMEM((1, heads * tile), F32),
        pltpu.VMEM((1, heads * tile), F32),
        pltpu.VMEM((q_len, width), BF16),
    ]


def attend_back_scratch(heads, tile, span, q_len, width):
    return [
        pltpu.VMEM((q_len // tile, heads * tile, width), BF16),
        pltpu.VMEM((q_len // tile, heads * tile, width), BF16),
        pltpu.VMEM((width, q_len), F32),
        pltpu.VMEM((span, width), F32),
        pltpu.VMEM((span, width), F32),
        pltpu.VMEM((q_len, width), BF16),
        pltpu.VMEM((q_len, width), BF16),
        pltpu.VMEM((q_len // tile, 2, heads * tile), F32),
    ]


def normal(value):
    mean = jnp.mean(value, axis=-1, keepdims=True)
    centered = value - mean
    inv = lax.rsqrt(jnp.mean(centered * centered, axis=-1, keepdims=True) + 1e-05)
    return centered * inv, inv


def normal_back(grad_out, norm, inv, gain):
    grad = grad_out * gain
    centered = grad - jnp.mean(grad, axis=-1, keepdims=True)
    return inv * (centered - norm * jnp.mean(grad * norm, axis=-1, keepdims=True))


def merge_kernel(n_tp, order, scalars, rows_ref, wide_ref, weight_ref, *refs):
    mixed, (hidden_ref, normed_ref) = refs[:n_tp], refs[n_tp:]
    index, tp = scalars[0], scalars[2]
    hidden_ref[...] = rows_ref[...].astype(F32) + wide_ref[2:3, :]
    for o, ref in enumerate(mixed):
        weight = jnp.concatenate([weight_ref[index ^ p, tp ^ o] for p in order], axis=1)
        hidden_ref[...] += dot(ref[...], weight, 1, 0)
    norm, _ = normal(hidden_ref[...])
    normed_ref[...] = (norm * wide_ref[3:4, :] + wide_ref[4:5, :]).astype(BF16)


def dense_kernel(count, expand_ref, *refs):
    normed, refs = refs[:count], refs[count:]
    grads, refs = refs[:count], refs[count:]
    weights, outs = refs[: -4 * count - 1], refs[-4 * count - 1 :]
    acts, pres, normed_outs, mlp_outs = (outs[i * count : (i + 1) * count] for i in range(4))
    sum_ref = outs[-1]
    block = weights[0].shape[0] // 2
    height = normed[0].shape[0]
    hidden = expand_ref.shape[1]
    step = min(hidden, 512)
    value = jnp.concatenate([ref[...] for ref in normed], axis=0)
    grad = jnp.concatenate([ref[...] for ref in grads], axis=0)
    back = forth = None
    for start in range(0, hidden, step):
        cols = slice(start, start + step)
        expand = jnp.concatenate([ref[:block, cols] for ref in weights], axis=0)
        shrink = jnp.concatenate([ref[block:, cols] for ref in weights], axis=0)
        pre = dot(value, expand, 1, 0) + expand_ref[:, cols]
        square = pre * pre
        inner = jnp.tanh(0.7978845608028654 * (pre + 0.044715 * square * pre))
        act = (0.5 * pre * (1.0 + inner)).astype(BF16)
        slope = 0.5 * (1.0 + inner) + (0.5 * 0.7978845608028654) * pre * (
            1.0 - inner * inner
        ) * (1.0 + (3.0 * 0.044715) * square)
        low = (dot(grad, shrink, 1, 0) * slope).astype(BF16)
        sum_ref[:, cols] = jnp.sum(low.astype(F32), axis=0, keepdims=True)
        for i in range(count):
            rows = slice(i * height, (i + 1) * height)
            acts[i][:, cols] = act[rows]
            pres[i][:, cols] = low[rows]
        more = dot(low, expand, 1, 1)
        also = dot(act, shrink, 1, 1)
        back = more if back is None else back + more
        forth = also if forth is None else forth + also
    for i in range(count):
        rows = slice(i * height, (i + 1) * height)
        normed_outs[i][...] = back[rows].astype(BF16)
        mlp_outs[i][...] = forth[rows].astype(BF16)


def hidden_back_kernel(
    count, n_tp, order, scalars, grad_ref, hidden_ref, wide_ref, weight_ref, *refs
):
    parts, refs = refs[:count], refs[count:]
    mixed, refs = refs[:n_tp], refs[n_tp:]
    direct = len(order) > 1
    refs = refs[1:] if direct else refs
    back_ref, low_ref, sums_ref = refs[:3]
    outs, refs = refs[3 : 3 + n_tp], refs[3 + n_tp :]
    index, tp = scalars[0], scalars[2]
    total = total_of(parts)
    norm, inv = normal(hidden_ref[...])
    grad = grad_ref[...].astype(F32)
    back = grad + normal_back(total, norm, inv, wide_ref[3:4, :])
    back_ref[...] = back
    low = back.astype(BF16)
    low_ref[...] = low
    copies = []
    if direct:
        buffer_ref, made_ref, sems = refs
        values = jnp.concatenate([ref[...] for ref in mixed], axis=1)
        tall = made_ref.shape[1]
        for place, offset in enumerate(order):
            left = low[:, place * tall : (place + 1) * tall]
            made_ref[place] = dot(left, values, 0, 0).astype(BF16)
            copies.append(
                pltpu.make_async_copy(
                    made_ref.at[place],
                    buffer_ref.at[index ^ offset, pl.ds(2 * tall, tall), :],
                    sems.at[place],
                )
            )
            copies[-1].start()
    for o in range(n_tp):
        weight = jnp.concatenate([weight_ref[index ^ p, tp ^ o] for p in order], axis=1)
        outs[o][...] = dot(low, weight, 1, 1).astype(BF16)
    sums_ref[...] = jnp.concatenate(
        [jnp.sum(v, axis=0, keepdims=True) for v in (back, total * norm, total, grad)], axis=0
    )
    for copy in copies:
        copy.wait()


def outer_kernel(order, spans, scalars, *refs):
    out_ref = refs[-1]
    tall = out_ref.shape[1] // (len(spans) + 1)
    base = 0
    for many, more in spans:
        left, refs = refs[:many], refs[many:]
        right, refs = refs[:more], refs[more:]
        a = jnp.concatenate([ref[...] for ref in left], axis=0)
        b = jnp.concatenate([ref[...] for ref in right], axis=0)
        for place, offset in enumerate(order):
            made = dot(a[:, place * tall : (place + 1) * tall], b, 0, 0).astype(BF16)
            out_ref[scalars[0] ^ offset, base : base + tall, :] = made
        base += tall


def join_kernel(left_ref, right_ref, out_ref):
    total = left_ref[...].astype(F32) + right_ref[...].astype(F32)
    out_ref[...] = total.astype(out_ref.dtype)


def sum_of(ref):
    total = ref[0].astype(F32)
    for i in range(1, ref.shape[0]):
        total = total + ref[i].astype(F32)
    return total


def dense_total_kernel(in_ref, expand_ref, shrink_ref, *outs):
    block = expand_ref.shape[0]
    expand_ref[...] = in_ref[:block, :].astype(F32)
    shrink_ref[...] = in_ref[block : 2 * block, :].astype(F32).T
    width = outs[0].shape[1]
    for o, ref in enumerate(outs):
        ref[...] = in_ref[2 * block :, o * width : (o + 1) * width]


def attend_total_kernel(in_ref, out_ref):
    parts, _, width = out_ref.shape
    for c in range(parts):
        out_ref[c] = in_ref[:, c * width : (c + 1) * width].astype(F32)


def total_of(refs):
    total = refs[0][...].astype(F32)
    for ref in refs[1:]:
        total = total + ref[...].astype(F32)
    return total


def join_layer_kernel(order, scalars, left_ref, right_ref, hidden_ref, wide_ref, *refs):
    total = left_ref[...].astype(F32) + right_ref[...].astype(F32)
    refs[-2][...] = total.astype(BF16)
    value = (hidden_ref[...] + total_of(refs[:-2]) + wide_ref[5:6, :]).astype(BF16)
    size = value.shape[1] // len(order)
    for place, offset in enumerate(order):
        cols = slice(place * size, (place + 1) * size)
        refs[-1][:, lanes(scalars[0], offset, size)] = value[:, cols]


def input_kernel(order, count, scalars, rows_ref, back_ref, wide_ref, *refs):
    parts, refs = refs[:count], refs[count:]
    extra, outs = refs[: len(refs) - count], refs[len(refs) - count :]
    total = total_of(parts)
    norm, inv = normal(rows_ref[...].astype(F32))
    value = (back_ref[...] + normal_back(total, norm, inv, wide_ref[0:1, :])).astype(BF16)
    height, wide = value.shape
    size = wide // len(order)
    for o, out_ref in enumerate(outs):
        for place, offset in enumerate(order):
            cols = lanes(scalars[0], offset, size)
            out_ref[:height, cols] = value[:, place * size : (place + 1) * size]
        if extra:
            tall, width = extra[o].shape
            tall = tall * width // wide
            for j in range(wide // width):
                out_ref[height:, j * width : (j + 1) * width] = extra[o][
                    j * tall : (j + 1) * tall, :
                ]


def first_sums_kernel(order, scalars, x_ref, *refs):
    parts, out_ref = refs[:-1], refs[-1]
    height, wide = parts[0].shape
    size = wide // len(order)
    out_ref[...] = jnp.zeros_like(out_ref)
    for o, ref in enumerate(parts):
        rows = lanes(scalars[2], o, height)
        value = x_ref[rows, :].astype(F32)
        mean = jnp.mean(value, axis=-1, keepdims=True)
        centered = value - mean
        inv = lax.rsqrt(jnp.mean(centered * centered, axis=-1, keepdims=True) + 1e-05)
        for place, offset in enumerate(order):
            cols = slice(place * size, (place + 1) * size)
            part = ref[:, cols].astype(F32)
            norm = (x_ref[rows, lanes(scalars[0], offset, size)].astype(F32) - mean) * inv
            out_ref[0:1, cols] += jnp.sum(part * norm, axis=0, keepdims=True)
            out_ref[1:2, cols] += jnp.sum(part, axis=0, keepdims=True)


def place_kernel(count, height, scalars, *refs):
    parts, outs = refs[:count], refs[count:]
    wide = parts[0].shape[1]
    for o, ref in enumerate(parts):
        outs[0][lanes(scalars[2], o, height), :] = ref[:height, :]
    if len(outs) > 1:
        width = outs[1].shape[0]
        tall = parts[0].shape[0] - height
        total = total_of([ref.at[height:, :] for ref in parts])
        for j in range(wide // width):
            outs[1][:, j * tall : (j + 1) * tall] = total[:, j * width : (j + 1) * width].T


def project_back_kernel(block, order, n_pair, n_tp, scalars, normed_ref, dq_ref, *refs):
    joined, refs = refs[:n_pair], refs[n_pair:]
    weights, refs = refs[: len(order)], refs[len(order) :]
    outs, (pair_ref, sums_ref, outer_ref) = refs[:n_tp], refs[n_tp:]
    pair = total_of(joined).astype(BF16)
    pair_ref[...] = pair
    width = dq_ref.shape[1]
    weight = rows_of(weights, 0, block)
    height = outs[0].shape[0]
    for o in range(n_tp):
        rows = lanes(scalars[2], o, height)
        both = jnp.concatenate([dq_ref[rows, :], pair_ref[rows, :]], axis=1)
        outs[o][...] = dot(both, weight, 1, 1).astype(BF16)
    sums_ref[...] = jnp.concatenate(
        [
            jnp.sum(v, axis=0, keepdims=True)
            for v in (dq_ref[...].astype(F32), pair[:, width:].astype(F32))
        ],
        axis=0,
    )
    tall = outer_ref.shape[1]
    both = jnp.concatenate([dq_ref[...], pair], axis=1)
    for place, offset in enumerate(order):
        rows = slice(place * tall, (place + 1) * tall)
        outer_ref[scalars[0] ^ offset] = dot(normed_ref[:, rows], both, 0, 0).astype(BF16)


def add_kernel(left_ref, right_ref, out_ref):
    out_ref[...] = left_ref[...].astype(F32) + right_ref[...].astype(F32)


def small_kernel(order, head_block, n_tp, scalars, two_ref, four_ref, attend_ref, *refs):
    index = scalars[0]
    out_ref = refs[-1]
    hidden = total_of(refs[:-1])
    size = out_ref.shape[2]
    attend = jnp.concatenate([attend_ref[...], jnp.zeros((6, attend_ref.shape[1]), F32)], axis=0)
    for place, offset in enumerate(order):
        cols = slice(place * size, (place + 1) * size)
        block = index ^ offset
        turned = pltpu.roll(attend, attend.shape[1] - block * head_block, 1)
        last = jnp.concatenate(
            [
                turned[0:1, :head_block],
                turned[1:2, :head_block],
                jnp.zeros((1, size - 2 * head_block), F32),
            ],
            axis=1,
        )
        mine = jnp.zeros((1, size), F32)
        for j in range(len(order)):
            mine = mine + jnp.where(block == j, hidden[:, j * size : (j + 1) * size], 0.0)
        made = jnp.concatenate([two_ref[:, cols], four_ref[:, cols], mine, last], axis=0)
        for o in range(n_tp):
            out_ref[block * n_tp + o] = made


def small_total_kernel(n_tp, scalars, in_ref, *outs):
    total = sum_of(in_ref)
    local = in_ref[scalars[2]]
    for i in range(1, in_ref.shape[0] // n_tp):
        local = local + in_ref[i * n_tp + scalars[2]]
    for i in range(6):
        outs[i][...] = total[i : i + 1, :]
    outs[6][...] = local[6:7, :]
    size = outs[7].shape[1]
    outs[7][...] = jnp.concatenate([local[7:8, :size], local[7:8, size : 2 * size]], axis=0)


def after(value, *others):
    return lax.optimization_barrier((value, *others))[0]


def body(
    sizes,
    layer_input,
    cotangent,
    segment_ids,
    norm1_gain,
    norm1_bias,
    attend_weight,
    attend_bias,
    merge_weight,
    merge_bias,
    norm2_gain,
    norm2_bias,
    expand_weight,
    expand_bias,
    shrink_weight,
    shrink_bias,
):
    n_dp, n_ctx, n_tp = sizes
    group = n_dp * n_ctx
    seqs, q_len, wide = layer_input.shape
    assert seqs == 1
    block = wide // group
    width = attend_weight.shape[2]
    heads = width // HD
    hidden_width = expand_weight.shape[1]
    height = q_len // n_tp
    bias_block = expand_bias.shape[0]
    head_block = attend_bias.shape[1]
    tile = min(256, q_len)
    direct = (n_dp, n_ctx) == (2, 4) and block % 128 == 0
    direct = direct and bias_block == block and 2 * head_block <= block
    order = [0, 2, 4, 6, 1, 3, 5, 7] if direct else [0]
    ctx = lax.axis_index("ctx")
    tp = lax.axis_index("tp")
    me = lax.axis_index("dp") * n_ctx + ctx if direct else 0 * ctx
    plane = ("dp", "ctx")

    def plane_swap(value, offset):
        return lax.ppermute(value, plane, [(i, i ^ offset) for i in range(group)])

    def ctx_swap(value, offset):
        return lax.ppermute(value, "ctx", [(i, i ^ offset) for i in range(n_ctx)])

    def tp_swap(value, offset):
        return lax.ppermute(value, "tp", [(i, i ^ offset) for i in range(n_tp)])

    def with_cores(even):
        return even + [ctx_swap(v, 1) for v in even]

    def tp_gather(value):
        return [value] + [tp_swap(value, o) for o in range(1, n_tp)]

    def tp_relay(value):
        parts = [value, tp_swap(value, 1)]
        for step in (2 ** i for i in range(1, n_tp.bit_length() - 1)):
            far = tp_swap(value, step)
            parts += [far, tp_swap(far, 1)] + [tp_swap(value, o) for o in range(step + 2, 2 * step)]
        return parts

    def tp_exchange(parts):
        return [parts[0]] + [tp_swap(parts[o], o) for o in range(1, n_tp)]

    seg_all = segment_ids[0]
    seg_query = lax.dynamic_slice_in_dim(seg_all, ctx * q_len, q_len, 0)
    lows = jnp.sum(
        (seg_all[:, None] < seg_query[None, :]).astype(jnp.int32), axis=0, keepdims=True
    )
    place = jnp.stack([me, ctx, tp]).astype(jnp.int32)
    limits = jnp.concatenate([place, lows[0, ::tile]], axis=0)
    keep = jnp.broadcast_to((seg_query > 0).astype(BF16)[:, None], (q_len, 128))

    smalls = (
        norm1_gain,
        norm1_bias,
        merge_bias,
        norm2_gain,
        norm2_bias,
        shrink_bias,
        expand_bias,
    )
    if direct:
        (pack,) = call(
            pack_kernel,
            "pack",
            None,
            [jnp.swapaxes(attend_weight, 0, 1)]
            + [jnp.reshape(v, (1, block)) for v in smalls]
            + [attend_bias],
            [shape((block + 8, 3 * width), BF16)],
        )
        far = [plane_swap(pack, o) for o in order[1:4]]
        first = with_cores([after(v, limits, keep) for v in [pack] + far])
        merge_all = lax.all_gather(merge_weight, ("dp", "ctx", "tp"), axis=0)
        merge_all = jnp.reshape(merge_all, (group, n_tp, width, block))
        given = []
    else:

        def whole(value, axis):
            return lax.all_gather(value, plane, axis=axis, tiled=True)

        first = [jnp.reshape(whole(attend_weight, 0), (wide, 3 * width))]
        merge_all = whole(lax.all_gather(merge_weight, "tp", axis=0), 2)[None]
        dense_all = [jnp.concatenate([whole(expand_weight, 0), whole(shrink_weight.T, 0)], 0)]
        wide_rows = whole(jnp.stack(smalls[:6]), 1).astype(F32)
        given = [
            jnp.pad(wide_rows, ((0, 2), (0, 0))),
            whole(expand_bias, 0).astype(F32)[None],
            whole(attend_bias, 1).astype(F32),
        ]
    span = block if direct else wide

    normed1, query, pair, input_rows, wide_rows, expand_add, attend_add = call(
        functools.partial(project_kernel, order, span, head_block),
        "project",
        place,
        [layer_input[0], *first, *given],
        [
            shape((q_len, wide), BF16),
            shape((q_len, width), BF16),
            shape((q_len, 2 * width), BF16),
            shape((height, wide), BF16),
            shape((8, wide), F32),
            shape((1, hidden_width), F32),
            shape((2, width), F32),
        ],
        flops=6 * q_len * wide * width,
    )
    grad_rows = call(
        functools.partial(grad_order_kernel, order, n_tp),
        "order_grad",
        place,
        [after(cotangent[0], pair), keep],
        [shape((height, wide), BF16)] * n_tp,
    )
    ready = [grad_rows[0], limits]
    if direct:
        (dense_rows,) = call(
            turn_kernel,
            "turn",
            None,
            [after(expand_weight, pair), shrink_weight],
            [shape((2 * block, hidden_width), BF16)],
        )
        ready.append(dense_rows)
    near = [pair] + [ctx_swap(pair, o) for o in range(2, n_ctx, 2)]
    pairs = []
    for value in near:
        if pairs:
            value = after(value, *ready)
        pairs += [value, ctx_swap(value, 1)]
    if direct:
        dense_y = plane_swap(dense_rows, 4)
        dense_core = ctx_swap(dense_rows, 1)
        pairs[-1] = after(pairs[-1], dense_y, dense_core)
        dense_x, dense_xy = (plane_swap(after(dense_rows, near[1]), o) for o in (2, 6))
    out = call(
        functools.partial(attend_kernel, heads, tile, min(512, q_len), n_ctx, n_tp),
        "attention",
        limits,
        [lows, query, *pairs],
        [shape((height, width), BF16)] * n_tp + [shape((heads, q_len), F32)],
        attend_scratch(heads, tile, q_len, width),
        flops=4 * q_len * q_len * n_ctx * width,
    )
    mixed, lse = out[:n_tp], out[n_tp]
    mixed_rows = tp_exchange(mixed)
    hidden, normed2 = call(
        functools.partial(merge_kernel, n_tp, order),
        "merge",
        place,
        [input_rows, wide_rows, merge_all, *mixed_rows],
        [shape((height, wide), F32), shape((height, wide), BF16)],
        flops=2 * height * wide * wide,
    )

    if direct:
        dense_far = [after(v, normed2) for v in (dense_x, dense_y, dense_xy)]
        dense_all = [dense_rows, *dense_far, dense_core] + [ctx_swap(v, 1) for v in dense_far]
    normed_all = tp_relay(normed2)
    normed_all[2] = after(normed_all[2], normed_all[1])
    picks = [[o for o in range(n_tp) if o % 4 in (0, 2)], [o for o in range(n_tp) if o % 4 in (1, 3)]]
    acts, pres, parts, mlps = ([None] * n_tp for _ in range(4))
    sums = []
    for pick in picks:
        count = len(pick)
        if sums:
            normed_all[3] = after(normed_all[3], sums[0])
        out = call(
            functools.partial(dense_kernel, count),
            "dense",
            None,
            [expand_add]
            + [normed_all[o] for o in pick]
            + [grad_rows[o] for o in pick]
            + dense_all,
            [shape((height, hidden_width), BF16)] * (2 * count)
            + [shape((height, wide), BF16)] * (2 * count)
            + [shape((1, hidden_width), F32)],
            flops=8 * count * height * wide * hidden_width,
        )
        for i, o in enumerate(pick):
            acts[o], pres[o], parts[o], mlps[o] = (out[j * count + i] for j in range(4))
        sums.append(out[-1])
    grad_parts = tp_exchange(parts)
    dense_outer = None
    if direct:
        (dense_outer,) = call(
            functools.partial(outer_kernel, order, [(n_tp, n_tp)] * 2),
            "dense_outer",
            place,
            [*normed_all, *pres, *grad_rows, *acts],
            [shape((group, 3 * block, hidden_width), BF16)],
            flops=4 * wide * hidden_width * q_len,
        )
        grad_parts[2] = after(grad_parts[2], dense_outer)
    (grad_near,) = call(
        add_kernel, "add", None, [grad_parts[0], grad_parts[2]], [shape((height, wide), F32)]
    )
    grad_parts = [grad_near] + [grad_parts[o] for o in range(1, n_tp) if o != 2]
    out = call(
        functools.partial(hidden_back_kernel, len(grad_parts), n_tp, order),
        "hidden_back",
        place,
        [grad_rows[0], hidden, wide_rows, merge_all, *grad_parts, *mixed_rows],
        [
            shape((height, wide), F32),
            shape((height, wide), BF16),
            shape((4, wide), F32),
        ]
        + [shape((height, width), BF16)] * n_tp,
        [pltpu.VMEM((group, block, wide), BF16), pltpu.SemaphoreType.DMA((group,))]
        if direct
        else [],
        flops=2 * height * wide * wide,
        whole=dense_outer,
    )
    if direct:
        dense_outer = out[-1]
        out = out[:-1]
    hidden_grad, grad_attn, four, grad_mixed = out[0], out[1], out[2], tp_exchange(out[3:])
    mlps = tp_exchange([mlps[0]] + [after(v, hidden_grad) for v in mlps[1:]])

    out = call(
        functools.partial(attend_back_kernel, heads, tile, tile, n_ctx, n_tp),
        "attention_back",
        limits,
        [lows, lse, query, *pairs, *mixed, *grad_mixed],
        [shape((q_len, width), BF16)] + [shape((q_len, 2 * width), BF16)] * n_ctx,
        attend_back_scratch(heads, tile, tile, q_len, width),
        flops=10 * q_len * q_len * n_ctx * width,
    )
    grad_query, grad_pairs = out[0], out[1:]
    joined = []
    for o in reversed(range(0, n_ctx, 2)):
        if joined:
            other = after(ctx_swap(grad_pairs[o + 1], 1), joined[-1])
            (total,) = call(
                join_kernel, "join", None, [other, grad_pairs[o]], [shape(other.shape, BF16)]
            )
        else:
            other = ctx_swap(after(grad_pairs[o + 1], *mlps), 1)
            total, layer_part = call(
                functools.partial(join_layer_kernel, order),
                "join_layer",
                place,
                [other, grad_pairs[o], hidden, wide_rows, *mlps],
                [shape(other.shape, BF16), shape((height, wide), BF16)],
            )
        joined.append(total)
    joined = joined[::-1]
    layer_parts = tp_relay(layer_part)
    joined = [joined[0]] + [ctx_swap(v, 2 * i) for i, v in enumerate(joined) if i]
    joined[-1] = after(joined[-1], layer_parts[1], layer_parts[2])
    out = call(
        functools.partial(project_back_kernel, span, order, len(joined), n_tp),
        "project_back",
        place,
        [normed1, grad_query, *joined, *first],
        [shape((height, wide), BF16)] * n_tp
        + [
            shape((q_len, 2 * width), BF16),
            shape((2, width), F32),
            shape((len(order), span, 3 * width), BF16),
        ],
        flops=12 * q_len * wide * width,
    )
    normed1_parts, (grad_pair, attend_sums, attend_outer) = out[:n_tp], out[n_tp:]
    (two,) = call(
        functools.partial(first_sums_kernel, order),
        "first_sums",
        place,
        [layer_input[0], *normed1_parts],
        [shape((2, wide), F32)],
    )
    normed1_parts = tp_exchange(normed1_parts)

    def placed(parts, outs=()):
        return call(
            functools.partial(place_kernel, n_tp, height),
            "place",
            place,
            parts,
            [shape((q_len, wide), BF16), *outs],
        )

    (layer_output,) = placed(layer_parts)

    def scattered(value):
        flat = jnp.reshape(value, (-1, value.shape[-1]))
        return lax.psum_scatter(flat, plane, scatter_dimension=0, tiled=True)

    if direct:
        attend_part = scattered(attend_outer)
        out = call(
            dense_total_kernel,
            "dense_total",
            None,
            [after(scattered(dense_outer), grad_pair)],
            [shape((block, hidden_width), F32), shape((hidden_width, block), F32)]
            + [shape((block, width), BF16)] * n_tp,
        )
        grad_expand, grad_shrink, merge_parts = out[0], out[1], out[2:]
        normed1_parts[-1] = after(normed1_parts[-1], grad_expand, two, layer_output)
    else:
        merge_parts = []
    low = block * width // wide if direct else 0
    input_parts = call(
        functools.partial(input_kernel, order, n_tp),
        "input_back",
        place,
        [input_rows, hidden_grad, wide_rows, *normed1_parts, *merge_parts],
        [shape((height + low, wide), BF16)] * n_tp,
    )
    input_part = input_parts[0]
    input_parts = tp_exchange(input_parts)

    if direct:
        (grad_attend,) = call(
            attend_total_kernel,
            "attend_total",
            None,
            [attend_part],
            [shape((3, block, width), F32)],
        )
        (small,) = call(
            functools.partial(small_kernel, order, head_block, n_tp),
            "small",
            place,
            [two, four, attend_sums, *sums],
            [shape((group * n_tp, 8, block), F32)],
        )
        table = call(
            functools.partial(small_total_kernel, n_tp),
            "small_total",
            place,
            [lax.all_to_all(after(small, input_part), ("dp", "ctx", "tp"), 0, 0)],
            [shape((1, block), F32)] * 7 + [shape((2, head_block), F32)],
        )
        rows = [jnp.reshape(v, (block,)) for v in table[:7]]
        expand_sum, attend_sum = rows[6], table[7]
        input_parts[-1] = after(input_parts[-1], grad_attend, *table)
        grad_attend = jnp.swapaxes(grad_attend, 0, 1)
    else:

        def cut(value, axis):
            return lax.psum_scatter(value, plane, scatter_dimension=axis, tiled=True)

        def outer_of(left, right):
            return cut(
                dot(jnp.concatenate(left), jnp.concatenate(right), 0, 0).astype(BF16), 0
            ).astype(F32)

        grad_expand = outer_of(normed_all, pres)
        grad_shrink = outer_of(grad_rows, acts).T
        grad_merge = outer_of([grad_attn], [jnp.concatenate(mixed_rows, axis=1)]).astype(BF16)
        grad_merge = [grad_merge[:, o * width : (o + 1) * width] for o in range(n_tp)]
        grad_merge = sum(v.astype(F32) for v in tp_exchange(grad_merge)).T
        grad_attend = jnp.reshape(cut(attend_outer[0], 0).astype(F32), (block, 3, width))
        table = lax.psum(cut(jnp.concatenate([two, four], axis=0), 1), "tp")
        rows = [table[i] for i in range(6)]
        expand_sum = cut(sum(sums)[0], 0)
        attend_sum = cut(attend_sums, 1)
    if direct:
        input_grad, grad_merge = placed(input_parts, [shape((width, block), F32)])
    else:
        (input_grad,) = placed(input_parts)
    return (
        layer_output[None],
        input_grad[None],
        rows[0],
        rows[1],
        grad_attend,
        attend_sum,
        grad_merge,
        rows[2],
        rows[3],
        rows[4],
        grad_expand,
        expand_sum,
        grad_shrink,
        rows[5],
    )


def solution(mesh):
    sizes = (mesh.shape["dp"], mesh.shape["ctx"], mesh.shape["tp"])
    return jax.shard_map(
        functools.partial(body, sizes),
        mesh=mesh,
        in_specs=(
            P("dp", "ctx", None),
            P("dp", "ctx", None),
            P("dp", None),
            P(("dp", "ctx")),
            P(("dp", "ctx")),
            P(("dp", "ctx"), None, "tp"),
            P(None, ("tp", "dp", "ctx")),
            P("tp", ("dp", "ctx")),
            P(("dp", "ctx")),
            P(("dp", "ctx")),
            P(("dp", "ctx")),
            P(("dp", "ctx"), "tp"),
            P(("tp", "dp", "ctx")),
            P("tp", ("dp", "ctx")),
            P(("dp", "ctx")),
        ),
        out_specs=(
            P("dp", "ctx", None),
            P("dp", "ctx", None),
            P(("dp", "ctx")),
            P(("dp", "ctx")),
            P(("dp", "ctx"), None, "tp"),
            P(None, ("tp", "dp", "ctx")),
            P("tp", ("dp", "ctx")),
            P(("dp", "ctx")),
            P(("dp", "ctx")),
            P(("dp", "ctx")),
            P(("dp", "ctx"), "tp"),
            P(("tp", "dp", "ctx")),
            P("tp", ("dp", "ctx")),
            P(("dp", "ctx")),
        ),
        check_vma=False,
    )
```

```python
import functools

import jax
import jax.numpy as jnp
from jax import lax
from jax.experimental import pallas as pl
from jax.experimental.pallas import tpu as pltpu
from jax.sharding import PartitionSpec as P

HD = 64
NEG = -1e30
ROOMY = (
    "dense",
    "dense_outer",
    "add",
    "join_layer",
    "join",
    "first_sums",
    "dense_total",
    "input_back",
    "place",
)
F32 = jnp.float32
BF16 = jnp.bfloat16


def dot(left, right, left_dim, right_dim):
    return lax.dot_general(
        left, right, (((left_dim,), (right_dim,)), ((), ())), preferred_element_type=F32
    )


def shape(dims, dtype):
    return jax.ShapeDtypeStruct(tuple(dims), dtype)


def call(kernel, name, scalars, ins, outs, scratch=(), flops=0, whole=None):
    first = [] if scalars is None else [scalars]
    specs, arrays, moved = [], [], 0
    for value in ins:
        if isinstance(value, tuple):
            value, dims, index = value
            specs.append(pl.BlockSpec(dims, lambda i, index=index: index))
            moved += value.dtype.itemsize * functools.reduce(lambda a, b: a * b, dims)
        else:
            specs.append(pl.BlockSpec(memory_space=pltpu.VMEM))
            moved += value.size * value.dtype.itemsize
        arrays.append(value)
    moved += sum(v.size * v.dtype.itemsize for v in outs)
    out_specs = [pl.BlockSpec(memory_space=pltpu.VMEM)] * len(outs)
    alias = {}
    if whole is not None:
        alias = {len(first) + len(arrays): len(outs)}
        specs.append(pl.BlockSpec(memory_space=pl.ANY))
        arrays.append(whole)
        outs = [*outs, shape(whole.shape, whole.dtype)]
        out_specs.append(pl.BlockSpec(memory_space=pl.ANY))
    return pl.pallas_call(
        kernel,
        grid=(1,),
        out_shape=tuple(outs),
        in_specs=[pl.BlockSpec(memory_space=pltpu.SMEM)] * len(first) + specs,
        out_specs=tuple(out_specs),
        input_output_aliases=alias,
        scratch_shapes=list(scratch),
        compiler_params=pltpu.CompilerParams(vmem_limit_bytes=(24 if name in ROOMY else 56) << 20),
        cost_estimate=pl.CostEstimate(
            flops=flops, transcendentals=0, bytes_accessed=moved
        ),
        name=name,
    )(*first, *arrays)


def lanes(index, offset, size):
    return pl.ds(pl.multiple_of((index ^ offset) * size, size), size)


def rows_of(refs, low, high):
    return jnp.concatenate([ref[low:high, :] for ref in refs], axis=0)


def pack_kernel(attend_ref, *refs):
    smalls, (pair_ref, out_ref) = refs[:-2], refs[-2:]
    parts, block, width = attend_ref.shape
    for c in range(parts):
        out_ref[:block, c * width : (c + 1) * width] = attend_ref[c]
    size = smalls[0].shape[1]
    last = jnp.concatenate([pair_ref[0:1, :], pair_ref[1:2, :]], axis=1).astype(F32)
    last = jnp.concatenate([last, jnp.zeros((1, size - last.shape[1]), F32)], axis=1)
    rows = jnp.concatenate([ref[...].astype(F32) for ref in smalls] + [last], axis=0)
    out_ref[block:, :size] = rows.astype(BF16)
    out_ref[block:, size:] = jnp.zeros((8, parts * width - size), BF16)


def turn_kernel(expand_ref, shrink_ref, out_ref):
    block = expand_ref.shape[0]
    out_ref[:block, :] = expand_ref[...]
    out_ref[block:, :] = shrink_ref[...].T


def decode(order, head_block, index, first, start, size, wide_ref, expand_ref, attend_ref):
    total = jnp.zeros(attend_ref.shape, F32)
    for place, offset in enumerate(order):
        rows = first[place][start : start + 8, :size].astype(F32)
        wide_ref[:, place * size : (place + 1) * size] = rows
        expand_ref[:, lanes(index, offset, size)] = rows[6:7, :]
        flat = jnp.concatenate([rows[7:8, :head_block], rows[7:8, head_block : 2 * head_block]], 0)
        flat = jnp.concatenate(
            [flat, jnp.zeros((2, attend_ref.shape[1] - head_block), F32)], axis=1
        )
        flat = jnp.concatenate([flat, jnp.zeros((6, attend_ref.shape[1]), F32)], axis=0)
        total = total + pltpu.roll(flat, (index ^ offset) * head_block, 1)[:2]
    attend_ref[...] = total


def grad_order_kernel(order, count, scalars, cot_ref, keep_ref, *outs):
    index, tp = scalars[0], scalars[2]
    height, wide = outs[0].shape
    size = wide // len(order)
    for o in range(count):
        rows = pl.ds(pl.multiple_of((tp ^ o) * height, height), height)
        keep = keep_ref[rows, 0:1]
        for place, offset in enumerate(order):
            outs[o][:, place * size : (place + 1) * size] = (
                cot_ref[rows, lanes(index, offset, size)] * keep
            )


def project_kernel(order, block, head_block, scalars, x_ref, *refs):
    count = len(order)
    weights, refs = refs[:count], refs[count:]
    given, outs = refs[:-7], refs[-7:]
    normed_ref, query_ref, pair_ref, rows_ref = outs[:4]
    wide_ref, expand_ref, attend_ref = outs[4:]
    index, tp = scalars[0], scalars[2]
    q_len, wide = x_ref.shape
    size = wide // count
    for source, target in zip(given, outs[4:]):
        target[...] = source[...]
    if not given:
        decode(order, head_block, index, weights, block, size, wide_ref, expand_ref, attend_ref)
    width = query_ref.shape[1]
    weight = rows_of(weights, 0, block)
    step = min(q_len, 256)
    bias = jnp.concatenate(
        [attend_ref[0:1, :], jnp.zeros((1, width), F32), attend_ref[1:2, :]], axis=1
    )
    for start in range(0, q_len, step):
        rows = slice(start, start + step)
        value = x_ref[rows, :].astype(F32)
        mean = jnp.mean(value, axis=-1, keepdims=True)
        centered = value - mean
        inv = lax.rsqrt(jnp.mean(centered * centered, axis=-1, keepdims=True) + 1e-05)
        for place, offset in enumerate(order):
            plain = slice(place * size, (place + 1) * size)
            part = x_ref[rows, lanes(index, offset, size)].astype(F32)
            part = (part - mean) * inv * wide_ref[0:1, plain] + wide_ref[1:2, plain]
            normed_ref[rows, plain] = part.astype(BF16)
        made = dot(normed_ref[rows, :], weight, 1, 0) + bias
        query_ref[rows, :] = made[:, :width].astype(BF16)
        pair_ref[rows, :] = made[:, width:].astype(BF16)
    height = rows_ref.shape[0]
    mine = pl.ds(pl.multiple_of(tp * height, height), height)
    for place, offset in enumerate(order):
        plain = slice(place * size, (place + 1) * size)
        rows_ref[:, plain] = x_ref[mine, lanes(index, offset, size)]


def attend_kernel(heads, tq, tk, n_chunk, n_tp, scalars, lo_ref, q_ref, *refs):
    kv_refs = refs[:n_chunk]
    outs, refs = refs[n_chunk : n_chunk + n_tp], refs[n_chunk + n_tp :]
    lse_ref, qm_ref, acc_ref, m_ref, l_ref, mixed_ref = refs
    q_len, width = q_ref.shape
    ctx = scalars[1]
    lane = lax.broadcasted_iota(jnp.int32, (tq, width), 1)

    def tile(qi, carry):
        rows = pl.ds(pl.multiple_of(qi * tq, tq), tq)
        qv = q_ref[rows, :] * BF16(0.125)
        for h in range(heads):
            mine = (lane >= h * HD) & (lane < (h + 1) * HD)
            qm_ref[h * tq : (h + 1) * tq, :] = jnp.where(mine, qv, jnp.zeros_like(qv))
        acc_ref[...] = jnp.zeros_like(acc_ref)
        m_ref[...] = jnp.full(m_ref.shape, NEG, F32)
        l_ref[...] = jnp.zeros_like(l_ref)
        qbase = ctx * q_len + qi * tq
        qpos = qbase + lax.broadcasted_iota(jnp.int32, (1, tq), 1)
        lo = lo_ref[0:1, rows]
        lo_first = scalars[3 + qi]
        for c in range(n_chunk):
            kv = kv_refs[c]
            cbase = (ctx ^ c) * q_len

            def step(ki, carry, kv=kv, cbase=cbase):
                kb = cbase + ki * tk

                @pl.when((kb <= qbase + tq - 1) & (kb + tk - 1 >= lo_first))
                def _():
                    krows = pl.ds(pl.multiple_of(ki * tk, tk), tk)
                    k = kv[krows, 0:width]
                    vt = kv[krows, width : 2 * width].T
                    kpos = kb + lax.broadcasted_iota(jnp.int32, (tk, 1), 0)
                    ok = (kpos >= lo) & (kpos <= qpos)
                    ok = jnp.concatenate([ok] * heads, axis=1)
                    s = jnp.where(ok, dot(k, qm_ref[...], 1, 1), NEG)
                    m0 = m_ref[...]
                    m1 = jnp.maximum(m0, jnp.max(s, axis=0, keepdims=True))
                    p = jnp.exp(s - m1)
                    al = jnp.exp(m0 - m1)
                    l_ref[...] = l_ref[...] * al + jnp.sum(p, axis=0, keepdims=True)
                    m_ref[...] = m1
                    low = p.astype(BF16)
                    made = [
                        dot(vt[h * HD : (h + 1) * HD, :], low[:, h * tq : (h + 1) * tq], 1, 0)
                        for h in range(heads)
                    ]
                    acc_ref[...] = acc_ref[...] * al + jnp.concatenate(made, axis=1)

                return carry

            lax.fori_loop(0, q_len // tk, step, 0)
        lse = m_ref[...] + jnp.log(l_ref[...])
        out = acc_ref[...] / l_ref[...]
        for h in range(heads):
            cols = slice(h * tq, (h + 1) * tq)
            lse_ref[h : h + 1, rows] = lse[:, cols]
        out = jnp.concatenate([out[:, h * tq : (h + 1) * tq] for h in range(heads)], axis=0)
        mixed_ref[rows, :] = out.T.astype(BF16)
        return carry

    lax.fori_loop(0, q_len // tq, tile, 0)
    for o in range(n_tp):
        outs[o][...] = mixed_ref[lanes(scalars[2], o, q_len // n_tp), :]


def attend_back_kernel(heads, tq, tk, n_chunk, n_tp, scalars, lo_ref, lse_ref, q_ref, *refs):
    kv_refs, refs = refs[:n_chunk], refs[n_chunk:]
    mixed_refs, refs = refs[:n_tp], refs[n_tp:]
    gm_refs, refs = refs[:n_tp], refs[n_tp:]
    dq_ref, refs = refs[0], refs[1:]
    dkv_refs, refs = refs[:n_chunk], refs[n_chunk:]
    qm_ref, gom_ref, dqt_ref, acck_ref, accv_ref, go_ref, mixed_ref, row_ref = refs
    q_len, width = q_ref.shape
    ctx, tp = scalars[1], scalars[2]
    for o in range(n_tp):
        go_ref[lanes(tp, o, q_len // n_tp), :] = gm_refs[o][...]
        mixed_ref[lanes(tp, o, q_len // n_tp), :] = mixed_refs[o][...]
    lane = lax.broadcasted_iota(jnp.int32, (tq, width), 1)
    nq = q_len // tq

    def ready(qi, carry):
        rows = pl.ds(pl.multiple_of(qi * tq, tq), tq)
        qv = q_ref[rows, :] * BF16(0.125)
        gv = go_ref[rows, :]
        prod = (gv.astype(F32) * mixed_ref[rows, :].astype(F32)).T
        for h in range(heads):
            cols = slice(h * tq, (h + 1) * tq)
            mine = (lane >= h * HD) & (lane < (h + 1) * HD)
            qm_ref[qi, cols, :] = jnp.where(mine, qv, jnp.zeros_like(qv))
            gom_ref[qi, cols, :] = jnp.where(mine, gv, jnp.zeros_like(gv))
            row_ref[qi, 0:1, cols] = lse_ref[h : h + 1, rows]
            row_ref[qi, 1:2, cols] = jnp.sum(
                prod[h * HD : (h + 1) * HD, :], axis=0, keepdims=True
            )
        return carry

    lax.fori_loop(0, nq, ready, 0)
    dqt_ref[...] = jnp.zeros_like(dqt_ref)
    for c in range(n_chunk):
        kv = kv_refs[c]
        dkv = dkv_refs[c]
        cbase = (ctx ^ c) * q_len

        def step(ki, carry, kv=kv, dkv=dkv, cbase=cbase):
            kb = cbase + ki * tk
            krows = pl.ds(pl.multiple_of(ki * tk, tk), tk)
            live = [
                (kb <= ctx * q_len + (qi + 1) * tq - 1) & (kb + tk - 1 >= scalars[3 + qi])
                for qi in range(nq)
            ]
            some = functools.reduce(jnp.logical_or, live)

            @pl.when(jnp.logical_not(some))
            def _():
                dkv[krows, :] = jnp.zeros((tk, 2 * width), BF16)

            @pl.when(some)
            def _():
                acck_ref[...] = jnp.zeros_like(acck_ref)
                accv_ref[...] = jnp.zeros_like(accv_ref)
                k = kv[krows, 0:width]
                v = kv[krows, width : 2 * width]
                kt = k.T
                kpos = kb + lax.broadcasted_iota(jnp.int32, (tk, 1), 0)

                def tile(qi, carry):
                    qbase = ctx * q_len + qi * tq

                    @pl.when((kb <= qbase + tq - 1) & (kb + tk - 1 >= scalars[3 + qi]))
                    def _():
                        rows = pl.ds(pl.multiple_of(qi * tq, tq), tq)
                        qpos = qbase + lax.broadcasted_iota(jnp.int32, (1, tq), 1)
                        ok = (kpos >= lo_ref[0:1, rows]) & (kpos <= qpos)
                        ok = jnp.concatenate([ok] * heads, axis=1)
                        s = dot(k, qm_ref[qi], 1, 1)
                        dp = dot(v, gom_ref[qi], 1, 1)
                        p = jnp.where(ok, jnp.exp(s - row_ref[qi, 0:1, :]), 0.0)
                        ds = (p * (dp - row_ref[qi, 1:2, :])).astype(BF16)
                        accv_ref[...] += dot(p.astype(BF16), gom_ref[qi], 1, 0)
                        acck_ref[...] += dot(ds, qm_ref[qi], 1, 0)
                        for h in range(heads):
                            hs = slice(h * HD, (h + 1) * HD)
                            dqt_ref[hs, rows] += dot(
                                kt[hs, :], ds[:, h * tq : (h + 1) * tq], 1, 0
                            )

                    return carry

                lax.fori_loop(0, nq, tile, 0)
                dkv[krows, 0:width] = acck_ref[...].astype(BF16)
                dkv[krows, width : 2 * width] = accv_ref[...].astype(BF16)

            return carry

        lax.fori_loop(0, q_len // tk, step, 0)
    for qi in range(nq):
        rows = slice(qi * tq, (qi + 1) * tq)
        dq_ref[rows, :] = (dqt_ref[:, rows].T * 0.125).astype(BF16)


def attend_scratch(heads, tile, q_len, width):
    return [
        pltpu.VMEM((heads * tile, width), BF16),
        pltpu.VMEM((HD, heads * tile), F32),
        pltpu.VMEM((1, heads * tile), F32),
        pltpu.VMEM((1, heads * tile), F32),
        pltpu.VMEM((q_len, width), BF16),
    ]


def attend_back_scratch(heads, tile, span, q_len, width):
    return [
        pltpu.VMEM((q_len // tile, heads * tile, width), BF16),
        pltpu.VMEM((q_len // tile, heads * tile, width), BF16),
        pltpu.VMEM((width, q_len), F32),
        pltpu.VMEM((span, width), F32),
        pltpu.VMEM((span, width), F32),
        pltpu.VMEM((q_len, width), BF16),
        pltpu.VMEM((q_len, width), BF16),
        pltpu.VMEM((q_len // tile, 2, heads * tile), F32),
    ]


def normal(value):
    mean = jnp.mean(value, axis=-1, keepdims=True)
    centered = value - mean
    inv = lax.rsqrt(jnp.mean(centered * centered, axis=-1, keepdims=True) + 1e-05)
    return centered * inv, inv


def normal_back(grad_out, norm, inv, gain):
    grad = grad_out * gain
    centered = grad - jnp.mean(grad, axis=-1, keepdims=True)
    return inv * (centered - norm * jnp.mean(grad * norm, axis=-1, keepdims=True))


def merge_kernel(n_tp, order, scalars, rows_ref, wide_ref, weight_ref, *refs):
    mixed, (hidden_ref, normed_ref) = refs[:n_tp], refs[n_tp:]
    index, tp = scalars[0], scalars[2]
    hidden_ref[...] = rows_ref[...].astype(F32) + wide_ref[2:3, :]
    for o, ref in enumerate(mixed):
        weight = jnp.concatenate([weight_ref[index ^ p, tp ^ o] for p in order], axis=1)
        hidden_ref[...] += dot(ref[...], weight, 1, 0)
    norm, _ = normal(hidden_ref[...])
    normed_ref[...] = (norm * wide_ref[3:4, :] + wide_ref[4:5, :]).astype(BF16)


def dense_kernel(count, expand_ref, *refs):
    normed, refs = refs[:count], refs[count:]
    grads, refs = refs[:count], refs[count:]
    weights, outs = refs[: -4 * count - 1], refs[-4 * count - 1 :]
    acts, pres, normed_outs, mlp_outs = (outs[i * count : (i + 1) * count] for i in range(4))
    sum_ref = outs[-1]
    block = weights[0].shape[0] // 2
    height = normed[0].shape[0]
    hidden = expand_ref.shape[1]
    step = min(hidden, 512)
    value = jnp.concatenate([ref[...] for ref in normed], axis=0)
    grad = jnp.concatenate([ref[...] for ref in grads], axis=0)
    back = forth = None
    for start in range(0, hidden, step):
        cols = slice(start, start + step)
        expand = jnp.concatenate([ref[:block, cols] for ref in weights], axis=0)
        shrink = jnp.concatenate([ref[block:, cols] for ref in weights], axis=0)
        pre = dot(value, expand, 1, 0) + expand_ref[:, cols]
        square = pre * pre
        inner = jnp.tanh(0.7978845608028654 * (pre + 0.044715 * square * pre))
        act = (0.5 * pre * (1.0 + inner)).astype(BF16)
        slope = 0.5 * (1.0 + inner) + (0.5 * 0.7978845608028654) * pre * (
            1.0 - inner * inner
        ) * (1.0 + (3.0 * 0.044715) * square)
        low = (dot(grad, shrink, 1, 0) * slope).astype(BF16)
        sum_ref[:, cols] = jnp.sum(low.astype(F32), axis=0, keepdims=True)
        for i in range(count):
            rows = slice(i * height, (i + 1) * height)
            acts[i][:, cols] = act[rows]
            pres[i][:, cols] = low[rows]
        more = dot(low, expand, 1, 1)
        also = dot(act, shrink, 1, 1)
        back = more if back is None else back + more
        forth = also if forth is None else forth + also
    for i in range(count):
        rows = slice(i * height, (i + 1) * height)
        normed_outs[i][...] = back[rows].astype(BF16)
        mlp_outs[i][...] = forth[rows].astype(BF16)


def hidden_back_kernel(
    count, n_tp, order, scalars, grad_ref, hidden_ref, wide_ref, weight_ref, *refs
):
    parts, refs = refs[:count], refs[count:]
    mixed, refs = refs[:n_tp], refs[n_tp:]
    direct = len(order) > 1
    refs = refs[1:] if direct else refs
    back_ref, low_ref, sums_ref = refs[:3]
    outs, refs = refs[3 : 3 + n_tp], refs[3 + n_tp :]
    index, tp = scalars[0], scalars[2]
    total = total_of(parts)
    norm, inv = normal(hidden_ref[...])
    grad = grad_ref[...].astype(F32)
    back = grad + normal_back(total, norm, inv, wide_ref[3:4, :])
    back_ref[...] = back
    low = back.astype(BF16)
    low_ref[...] = low
    copies = []
    if direct:
        buffer_ref, made_ref, sems = refs
        values = jnp.concatenate([ref[...] for ref in mixed], axis=1)
        tall = made_ref.shape[1]
        for place, offset in enumerate(order):
            left = low[:, place * tall : (place + 1) * tall]
            made_ref[place] = dot(left, values, 0, 0).astype(BF16)
            copies.append(
                pltpu.make_async_copy(
                    made_ref.at[place],
                    buffer_ref.at[index ^ offset, pl.ds(2 * tall, tall), :],
                    sems.at[place],
                )
            )
            copies[-1].start()
    for o in range(n_tp):
        weight = jnp.concatenate([weight_ref[index ^ p, tp ^ o] for p in order], axis=1)
        outs[o][...] = dot(low, weight, 1, 1).astype(BF16)
    sums_ref[...] = jnp.concatenate(
        [jnp.sum(v, axis=0, keepdims=True) for v in (back, total * norm, total, grad)], axis=0
    )
    for copy in copies:
        copy.wait()


def outer_kernel(order, spans, scalars, *refs):
    out_ref = refs[-1]
    tall = out_ref.shape[1] // (len(spans) + 1)
    base = 0
    for many, more in spans:
        left, refs = refs[:many], refs[many:]
        right, refs = refs[:more], refs[more:]
        a = jnp.concatenate([ref[...] for ref in left], axis=0)
        b = jnp.concatenate([ref[...] for ref in right], axis=0)
        for place, offset in enumerate(order):
            made = dot(a[:, place * tall : (place + 1) * tall], b, 0, 0).astype(BF16)
            out_ref[scalars[0] ^ offset, base : base + tall, :] = made
        base += tall


def join_kernel(left_ref, right_ref, out_ref):
    total = left_ref[...].astype(F32) + right_ref[...].astype(F32)
    out_ref[...] = total.astype(out_ref.dtype)


def sum_of(ref):
    total = ref[0].astype(F32)
    for i in range(1, ref.shape[0]):
        total = total + ref[i].astype(F32)
    return total


def dense_total_kernel(in_ref, expand_ref, shrink_ref, *outs):
    block = expand_ref.shape[0]
    expand_ref[...] = in_ref[:block, :].astype(F32)
    shrink_ref[...] = in_ref[block : 2 * block, :].astype(F32).T
    width = outs[0].shape[1]
    for o, ref in enumerate(outs):
        ref[...] = in_ref[2 * block :, o * width : (o + 1) * width]


def attend_total_kernel(in_ref, out_ref):
    parts, _, width = out_ref.shape
    for c in range(parts):
        out_ref[c] = in_ref[:, c * width : (c + 1) * width].astype(F32)


def total_of(refs):
    total = refs[0][...].astype(F32)
    for ref in refs[1:]:
        total = total + ref[...].astype(F32)
    return total


def join_layer_kernel(order, scalars, left_ref, right_ref, hidden_ref, wide_ref, *refs):
    total = left_ref[...].astype(F32) + right_ref[...].astype(F32)
    refs[-2][...] = total.astype(BF16)
    value = (hidden_ref[...] + total_of(refs[:-2]) + wide_ref[5:6, :]).astype(BF16)
    size = value.shape[1] // len(order)
    for place, offset in enumerate(order):
        cols = slice(place * size, (place + 1) * size)
        refs[-1][:, lanes(scalars[0], offset, size)] = value[:, cols]


def input_kernel(order, count, scalars, rows_ref, back_ref, wide_ref, *refs):
    parts, refs = refs[:count], refs[count:]
    extra, outs = refs[: len(refs) - count], refs[len(refs) - count :]
    total = total_of(parts)
    norm, inv = normal(rows_ref[...].astype(F32))
    value = (back_ref[...] + normal_back(total, norm, inv, wide_ref[0:1, :])).astype(BF16)
    height, wide = value.shape
    size = wide // len(order)
    for o, out_ref in enumerate(outs):
        for place, offset in enumerate(order):
            cols = lanes(scalars[0], offset, size)
            out_ref[:height, cols] = value[:, place * size : (place + 1) * size]
        if extra:
            tall, width = extra[o].shape
            tall = tall * width // wide
            for j in range(wide // width):
                out_ref[height:, j * width : (j + 1) * width] = extra[o][
                    j * tall : (j + 1) * tall, :
                ]


def first_sums_kernel(order, scalars, x_ref, *refs):
    parts, out_ref = refs[:-1], refs[-1]
    height, wide = parts[0].shape
    size = wide // len(order)
    out_ref[...] = jnp.zeros_like(out_ref)
    for o, ref in enumerate(parts):
        rows = lanes(scalars[2], o, height)
        value = x_ref[rows, :].astype(F32)
        mean = jnp.mean(value, axis=-1, keepdims=True)
        centered = value - mean
        inv = lax.rsqrt(jnp.mean(centered * centered, axis=-1, keepdims=True) + 1e-05)
        for place, offset in enumerate(order):
            cols = slice(place * size, (place + 1) * size)
            part = ref[:, cols].astype(F32)
            norm = (x_ref[rows, lanes(scalars[0], offset, size)].astype(F32) - mean) * inv
            out_ref[0:1, cols] += jnp.sum(part * norm, axis=0, keepdims=True)
            out_ref[1:2, cols] += jnp.sum(part, axis=0, keepdims=True)


def place_kernel(count, height, scalars, *refs):
    parts, outs = refs[:count], refs[count:]
    wide = parts[0].shape[1]
    for o, ref in enumerate(parts):
        outs[0][lanes(scalars[2], o, height), :] = ref[:height, :]
    if len(outs) > 1:
        width = outs[1].shape[0]
        tall = parts[0].shape[0] - height
        total = total_of([ref.at[height:, :] for ref in parts])
        for j in range(wide // width):
            outs[1][:, j * tall : (j + 1) * tall] = total[:, j * width : (j + 1) * width].T


def project_back_kernel(block, order, n_pair, n_tp, scalars, normed_ref, dq_ref, *refs):
    joined, refs = refs[:n_pair], refs[n_pair:]
    weights, refs = refs[: len(order)], refs[len(order) :]
    outs, (pair_ref, sums_ref, outer_ref) = refs[:n_tp], refs[n_tp:]
    pair = total_of(joined).astype(BF16)
    pair_ref[...] = pair
    width = dq_ref.shape[1]
    weight = rows_of(weights, 0, block)
    height = outs[0].shape[0]
    for o in range(n_tp):
        rows = lanes(scalars[2], o, height)
        both = jnp.concatenate([dq_ref[rows, :], pair_ref[rows, :]], axis=1)
        outs[o][...] = dot(both, weight, 1, 1).astype(BF16)
    sums_ref[...] = jnp.concatenate(
        [
            jnp.sum(v, axis=0, keepdims=True)
            for v in (dq_ref[...].astype(F32), pair[:, width:].astype(F32))
        ],
        axis=0,
    )
    tall = outer_ref.shape[1]
    both = jnp.concatenate([dq_ref[...], pair], axis=1)
    for place, offset in enumerate(order):
        rows = slice(place * tall, (place + 1) * tall)
        outer_ref[scalars[0] ^ offset] = dot(normed_ref[:, rows], both, 0, 0).astype(BF16)


def add_kernel(left_ref, right_ref, out_ref):
    out_ref[...] = left_ref[...].astype(F32) + right_ref[...].astype(F32)


def small_kernel(order, head_block, n_tp, scalars, two_ref, four_ref, attend_ref, *refs):
    index = scalars[0]
    out_ref = refs[-1]
    hidden = total_of(refs[:-1])
    size = out_ref.shape[2]
    attend = jnp.concatenate([attend_ref[...], jnp.zeros((6, attend_ref.shape[1]), F32)], axis=0)
    for place, offset in enumerate(order):
        cols = slice(place * size, (place + 1) * size)
        block = index ^ offset
        turned = pltpu.roll(attend, attend.shape[1] - block * head_block, 1)
        last = jnp.concatenate(
            [
                turned[0:1, :head_block],
                turned[1:2, :head_block],
                jnp.zeros((1, size - 2 * head_block), F32),
            ],
            axis=1,
        )
        mine = jnp.zeros((1, size), F32)
        for j in range(len(order)):
            mine = mine + jnp.where(block == j, hidden[:, j * size : (j + 1) * size], 0.0)
        made = jnp.concatenate([two_ref[:, cols], four_ref[:, cols], mine, last], axis=0)
        for o in range(n_tp):
            out_ref[block * n_tp + o] = made


def small_total_kernel(n_tp, scalars, in_ref, *outs):
    total = sum_of(in_ref)
    local = in_ref[scalars[2]]
    for i in range(1, in_ref.shape[0] // n_tp):
        local = local + in_ref[i * n_tp + scalars[2]]
    for i in range(6):
        outs[i][...] = total[i : i + 1, :]
    outs[6][...] = local[6:7, :]
    size = outs[7].shape[1]
    outs[7][...] = jnp.concatenate([local[7:8, :size], local[7:8, size : 2 * size]], axis=0)


def after(value, *others):
    return lax.optimization_barrier((value, *others))[0]


def body(
    sizes,
    layer_input,
    cotangent,
    segment_ids,
    norm1_gain,
    norm1_bias,
    attend_weight,
    attend_bias,
    merge_weight,
    merge_bias,
    norm2_gain,
    norm2_bias,
    expand_weight,
    expand_bias,
    shrink_weight,
    shrink_bias,
):
    n_dp, n_ctx, n_tp = sizes
    group = n_dp * n_ctx
    seqs, q_len, wide = layer_input.shape
    assert seqs == 1
    block = wide // group
    width = attend_weight.shape[2]
    heads = width // HD
    hidden_width = expand_weight.shape[1]
    height = q_len // n_tp
    bias_block = expand_bias.shape[0]
    head_block = attend_bias.shape[1]
    tile = min(256, q_len)
    direct = (n_dp, n_ctx) == (2, 4) and block % 128 == 0
    direct = direct and bias_block == block and 2 * head_block <= block
    order = [0, 2, 4, 6, 1, 3, 5, 7] if direct else [0]
    ctx = lax.axis_index("ctx")
    tp = lax.axis_index("tp")
    me = lax.axis_index("dp") * n_ctx + ctx if direct else 0 * ctx
    plane = ("dp", "ctx")

    def plane_swap(value, offset):
        return lax.ppermute(value, plane, [(i, i ^ offset) for i in range(group)])

    def ctx_swap(value, offset):
        return lax.ppermute(value, "ctx", [(i, i ^ offset) for i in range(n_ctx)])

    def tp_swap(value, offset):
        return lax.ppermute(value, "tp", [(i, i ^ offset) for i in range(n_tp)])

    def with_cores(even):
        return even + [ctx_swap(v, 1) for v in even]

    def tp_gather(value):
        return [value] + [tp_swap(value, o) for o in range(1, n_tp)]

    def tp_relay(value):
        parts = [value, tp_swap(value, 1)]
        for step in (2 ** i for i in range(1, n_tp.bit_length() - 1)):
            far = tp_swap(value, step)
            parts += [far, tp_swap(far, 1)] + [tp_swap(value, o) for o in range(step + 2, 2 * step)]
        return parts

    def tp_exchange(parts):
        return [parts[0]] + [tp_swap(parts[o], o) for o in range(1, n_tp)]

    seg_all = segment_ids[0]
    seg_query = lax.dynamic_slice_in_dim(seg_all, ctx * q_len, q_len, 0)
    lows = jnp.sum(
        (seg_all[:, None] < seg_query[None, :]).astype(jnp.int32), axis=0, keepdims=True
    )
    place = jnp.stack([me, ctx, tp]).astype(jnp.int32)
    limits = jnp.concatenate([place, lows[0, ::tile]], axis=0)
    keep = jnp.broadcast_to((seg_query > 0).astype(BF16)[:, None], (q_len, 128))

    smalls = (
        norm1_gain,
        norm1_bias,
        merge_bias,
        norm2_gain,
        norm2_bias,
        shrink_bias,
        expand_bias,
    )
    if direct:
        (pack,) = call(
            pack_kernel,
            "pack",
            None,
            [jnp.swapaxes(attend_weight, 0, 1)]
            + [jnp.reshape(v, (1, block)) for v in smalls]
            + [attend_bias],
            [shape((block + 8, 3 * width), BF16)],
        )
        far = [plane_swap(pack, o) for o in order[1:4]]
        first = with_cores([after(v, limits, keep) for v in [pack] + far])
        merge_all = lax.all_gather(merge_weight, ("dp", "ctx", "tp"), axis=0)
        merge_all = jnp.reshape(merge_all, (group, n_tp, width, block))
        given = []
    else:

        def whole(value, axis):
            return lax.all_gather(value, plane, axis=axis, tiled=True)

        first = [jnp.reshape(whole(attend_weight, 0), (wide, 3 * width))]
        merge_all = whole(lax.all_gather(merge_weight, "tp", axis=0), 2)[None]
        dense_all = [jnp.concatenate([whole(expand_weight, 0), whole(shrink_weight.T, 0)], 0)]
        wide_rows = whole(jnp.stack(smalls[:6]), 1).astype(F32)
        given = [
            jnp.pad(wide_rows, ((0, 2), (0, 0))),
            whole(expand_bias, 0).astype(F32)[None],
            whole(attend_bias, 1).astype(F32),
        ]
    span = block if direct else wide

    normed1, query, pair, input_rows, wide_rows, expand_add, attend_add = call(
        functools.partial(project_kernel, order, span, head_block),
        "project",
        place,
        [layer_input[0], *first, *given],
        [
            shape((q_len, wide), BF16),
            shape((q_len, width), BF16),
            shape((q_len, 2 * width), BF16),
            shape((height, wide), BF16),
            shape((8, wide), F32),
            shape((1, hidden_width), F32),
            shape((2, width), F32),
        ],
        flops=6 * q_len * wide * width,
    )
    grad_rows = call(
        functools.partial(grad_order_kernel, order, n_tp),
        "order_grad",
        place,
        [after(cotangent[0], pair), keep],
        [shape((height, wide), BF16)] * n_tp,
    )
    ready = [grad_rows[0], limits]
    if direct:
        (dense_rows,) = call(
            turn_kernel,
            "turn",
            None,
            [after(expand_weight, pair), shrink_weight],
            [shape((2 * block, hidden_width), BF16)],
        )
        ready.append(dense_rows)
    near = [pair] + [ctx_swap(pair, o) for o in range(2, n_ctx, 2)]
    pairs = []
    for value in near:
        if pairs:
            value = after(value, *ready)
        pairs += [value, ctx_swap(value, 1)]
    if direct:
        dense_y = plane_swap(dense_rows, 4)
        dense_core = ctx_swap(dense_rows, 1)
        pairs[-1] = after(pairs[-1], dense_y, dense_core)
        dense_x, dense_xy = (plane_swap(after(dense_rows, near[1]), o) for o in (2, 6))
    out = call(
        functools.partial(attend_kernel, heads, tile, min(512, q_len), n_ctx, n_tp),
        "attention",
        limits,
        [lows, query, *pairs],
        [shape((height, width), BF16)] * n_tp + [shape((heads, q_len), F32)],
        attend_scratch(heads, tile, q_len, width),
        flops=4 * q_len * q_len * n_ctx * width,
    )
    mixed, lse = out[:n_tp], out[n_tp]
    mixed_rows = tp_exchange(mixed)
    hidden, normed2 = call(
        functools.partial(merge_kernel, n_tp, order),
        "merge",
        place,
        [input_rows, wide_rows, merge_all, *mixed_rows],
        [shape((height, wide), F32), shape((height, wide), BF16)],
        flops=2 * height * wide * wide,
    )

    if direct:
        dense_far = [after(v, normed2) for v in (dense_x, dense_y, dense_xy)]
        dense_all = [dense_rows, *dense_far, dense_core] + [ctx_swap(v, 1) for v in dense_far]
    normed_all = tp_relay(normed2)
    normed_all[2] = after(normed_all[2], normed_all[1])
    picks = [[o for o in range(n_tp) if o % 4 in (0, 2)], [o for o in range(n_tp) if o % 4 in (1, 3)]]
    acts, pres, parts, mlps = ([None] * n_tp for _ in range(4))
    sums = []
    for pick in picks:
        count = len(pick)
        if sums:
            normed_all[3] = after(normed_all[3], sums[0])
        out = call(
            functools.partial(dense_kernel, count),
            "dense",
            None,
            [expand_add]
            + [normed_all[o] for o in pick]
            + [grad_rows[o] for o in pick]
            + dense_all,
            [shape((height, hidden_width), BF16)] * (2 * count)
            + [shape((height, wide), BF16)] * (2 * count)
            + [shape((1, hidden_width), F32)],
            flops=8 * count * height * wide * hidden_width,
        )
        for i, o in enumerate(pick):
            acts[o], pres[o], parts[o], mlps[o] = (out[j * count + i] for j in range(4))
        sums.append(out[-1])
    grad_parts = tp_exchange(parts)
    dense_outer = None
    if direct:
        (dense_outer,) = call(
            functools.partial(outer_kernel, order, [(n_tp, n_tp)] * 2),
            "dense_outer",
            place,
            [*normed_all, *pres, *grad_rows, *acts],
            [shape((group, 3 * block, hidden_width), BF16)],
            flops=4 * wide * hidden_width * q_len,
        )
        grad_parts[2] = after(grad_parts[2], dense_outer)
    (grad_near,) = call(
        add_kernel, "add", None, [grad_parts[0], grad_parts[2]], [shape((height, wide), F32)]
    )
    grad_parts = [grad_near] + [grad_parts[o] for o in range(1, n_tp) if o != 2]
    out = call(
        functools.partial(hidden_back_kernel, len(grad_parts), n_tp, order),
        "hidden_back",
        place,
        [grad_rows[0], hidden, wide_rows, merge_all, *grad_parts, *mixed_rows],
        [
            shape((height, wide), F32),
            shape((height, wide), BF16),
            shape((4, wide), F32),
        ]
        + [shape((height, width), BF16)] * n_tp,
        [pltpu.VMEM((group, block, wide), BF16), pltpu.SemaphoreType.DMA((group,))]
        if direct
        else [],
        flops=2 * height * wide * wide,
        whole=dense_outer,
    )
    if direct:
        dense_outer = out[-1]
        out = out[:-1]
    hidden_grad, grad_attn, four, grad_mixed = out[0], out[1], out[2], tp_exchange(out[3:])
    mlps = tp_exchange([mlps[0]] + [after(v, hidden_grad) for v in mlps[1:]])

    out = call(
        functools.partial(attend_back_kernel, heads, tile, tile, n_ctx, n_tp),
        "attention_back",
        limits,
        [lows, lse, query, *pairs, *mixed, *grad_mixed],
        [shape((q_len, width), BF16)] + [shape((q_len, 2 * width), BF16)] * n_ctx,
        attend_back_scratch(heads, tile, tile, q_len, width),
        flops=10 * q_len * q_len * n_ctx * width,
    )
    grad_query, grad_pairs = out[0], out[1:]
    joined = []
    for o in reversed(range(0, n_ctx, 2)):
        if joined:
            other = after(ctx_swap(grad_pairs[o + 1], 1), joined[-1])
            (total,) = call(
                join_kernel, "join", None, [other, grad_pairs[o]], [shape(other.shape, BF16)]
            )
        else:
            other = ctx_swap(after(grad_pairs[o + 1], *mlps), 1)
            total, layer_part = call(
                functools.partial(join_layer_kernel, order),
                "join_layer",
                place,
                [other, grad_pairs[o], hidden, wide_rows, *mlps],
                [shape(other.shape, BF16), shape((height, wide), BF16)],
            )
        joined.append(total)
    joined = joined[::-1]
    layer_parts = tp_relay(layer_part)
    joined = [joined[0]] + [ctx_swap(v, 2 * i) for i, v in enumerate(joined) if i]
    joined[-1] = after(joined[-1], layer_parts[1], layer_parts[2])
    out = call(
        functools.partial(project_back_kernel, span, order, len(joined), n_tp),
        "project_back",
        place,
        [normed1, grad_query, *joined, *first],
        [shape((height, wide), BF16)] * n_tp
        + [
            shape((q_len, 2 * width), BF16),
            shape((2, width), F32),
            shape((len(order), span, 3 * width), BF16),
        ],
        flops=12 * q_len * wide * width,
    )
    normed1_parts, (grad_pair, attend_sums, attend_outer) = out[:n_tp], out[n_tp:]
    (two,) = call(
        functools.partial(first_sums_kernel, order),
        "first_sums",
        place,
        [layer_input[0], *normed1_parts],
        [shape((2, wide), F32)],
    )
    normed1_parts = tp_exchange(normed1_parts)

    def placed(parts, outs=()):
        return call(
            functools.partial(place_kernel, n_tp, height),
            "place",
            place,
            parts,
            [shape((q_len, wide), BF16), *outs],
        )

    (layer_output,) = placed(layer_parts)

    def scattered(value):
        flat = jnp.reshape(value, (-1, value.shape[-1]))
        return lax.psum_scatter(flat, plane, scatter_dimension=0, tiled=True)

    if direct:
        attend_part = scattered(attend_outer)
        out = call(
            dense_total_kernel,
            "dense_total",
            None,
            [after(scattered(dense_outer), grad_pair)],
            [shape((block, hidden_width), F32), shape((hidden_width, block), F32)]
            + [shape((block, width), BF16)] * n_tp,
        )
        grad_expand, grad_shrink, merge_parts = out[0], out[1], out[2:]
        normed1_parts[-1] = after(normed1_parts[-1], grad_expand, two, layer_output)
    else:
        merge_parts = []
    low = block * width // wide if direct else 0
    input_parts = call(
        functools.partial(input_kernel, order, n_tp),
        "input_back",
        place,
        [input_rows, hidden_grad, wide_rows, *normed1_parts, *merge_parts],
        [shape((height + low, wide), BF16)] * n_tp,
    )
    input_part = input_parts[0]
    input_parts = tp_exchange(input_parts)

    if direct:
        (grad_attend,) = call(
            attend_total_kernel,
            "attend_total",
            None,
            [attend_part],
            [shape((3, block, width), F32)],
        )
        (small,) = call(
            functools.partial(small_kernel, order, head_block, n_tp),
            "small",
            place,
            [two, four, attend_sums, *sums],
            [shape((group * n_tp, 8, block), F32)],
        )
        input_parts[-1] = after(input_parts[-1], grad_attend)
        input_grad, grad_merge = placed(input_parts, [shape((width, block), F32)])
        table = call(
            functools.partial(small_total_kernel, n_tp),
            "small_total",
            place,
            [
                after(
                    lax.all_to_all(after(small, input_part), ("dp", "ctx", "tp"), 0, 0), input_grad
                )
            ],
            [shape((1, block), F32)] * 7 + [shape((2, head_block), F32)],
        )
        rows = [jnp.reshape(v, (block,)) for v in table[:7]]
        expand_sum, attend_sum = rows[6], table[7]
        grad_attend = jnp.swapaxes(grad_attend, 0, 1)
    else:

        def cut(value, axis):
            return lax.psum_scatter(value, plane, scatter_dimension=axis, tiled=True)

        def outer_of(left, right):
            return cut(
                dot(jnp.concatenate(left), jnp.concatenate(right), 0, 0).astype(BF16), 0
            ).astype(F32)

        grad_expand = outer_of(normed_all, pres)
        grad_shrink = outer_of(grad_rows, acts).T
        grad_merge = outer_of([grad_attn], [jnp.concatenate(mixed_rows, axis=1)]).astype(BF16)
        grad_merge = [grad_merge[:, o * width : (o + 1) * width] for o in range(n_tp)]
        grad_merge = sum(v.astype(F32) for v in tp_exchange(grad_merge)).T
        grad_attend = jnp.reshape(cut(attend_outer[0], 0).astype(F32), (block, 3, width))
        (input_grad,) = placed(input_parts)
        table = lax.psum(cut(jnp.concatenate([two, four], axis=0), 1), "tp")
        rows = [table[i] for i in range(6)]
        expand_sum = cut(sum(sums)[0], 0)
        attend_sum = cut(attend_sums, 1)
    return (
        layer_output[None],
        input_grad[None],
        rows[0],
        rows[1],
        grad_attend,
        attend_sum,
        grad_merge,
        rows[2],
        rows[3],
        rows[4],
        grad_expand,
        expand_sum,
        grad_shrink,
        rows[5],
    )


def solution(mesh):
    sizes = (mesh.shape["dp"], mesh.shape["ctx"], mesh.shape["tp"])
    return jax.shard_map(
        functools.partial(body, sizes),
        mesh=mesh,
        in_specs=(
            P("dp", "ctx", None),
            P("dp", "ctx", None),
            P("dp", None),
            P(("dp", "ctx")),
            P(("dp", "ctx")),
            P(("dp", "ctx"), None, "tp"),
            P(None, ("tp", "dp", "ctx")),
            P("tp", ("dp", "ctx")),
            P(("dp", "ctx")),
            P(("dp", "ctx")),
            P(("dp", "ctx")),
            P(("dp", "ctx"), "tp"),
            P(("tp", "dp", "ctx")),
            P("tp", ("dp", "ctx")),
            P(("dp", "ctx")),
        ),
        out_specs=(
            P("dp", "ctx", None),
            P("dp", "ctx", None),
            P(("dp", "ctx")),
            P(("dp", "ctx")),
            P(("dp", "ctx"), None, "tp"),
            P(None, ("tp", "dp", "ctx")),
            P("tp", ("dp", "ctx")),
            P(("dp", "ctx")),
            P(("dp", "ctx")),
            P(("dp", "ctx")),
            P(("dp", "ctx"), "tp"),
            P(("tp", "dp", "ctx")),
            P("tp", ("dp", "ctx")),
            P(("dp", "ctx")),
        ),
        check_vma=False,
    )
```

```python
import functools

import jax
import jax.numpy as jnp
from jax import lax
from jax.experimental import pallas as pl
from jax.experimental.pallas import tpu as pltpu
from jax.sharding import PartitionSpec as P

HD = 64
NEG = -1e30
ROOMY = (
    "dense",
    "dense_outer",
    "add",
    "join_layer",
    "join",
    "first_sums",
    "dense_total",
    "input_back",
    "place",
    "small_total",
    "attend_total",
)
F32 = jnp.float32
BF16 = jnp.bfloat16


def dot(left, right, left_dim, right_dim):
    return lax.dot_general(
        left, right, (((left_dim,), (right_dim,)), ((), ())), preferred_element_type=F32
    )


def shape(dims, dtype):
    return jax.ShapeDtypeStruct(tuple(dims), dtype)


def call(kernel, name, scalars, ins, outs, scratch=(), flops=0, whole=None):
    first = [] if scalars is None else [scalars]
    specs, arrays, moved = [], [], 0
    for value in ins:
        if isinstance(value, tuple):
            value, dims, index = value
            specs.append(pl.BlockSpec(dims, lambda i, index=index: index))
            moved += value.dtype.itemsize * functools.reduce(lambda a, b: a * b, dims)
        else:
            specs.append(pl.BlockSpec(memory_space=pltpu.VMEM))
            moved += value.size * value.dtype.itemsize
        arrays.append(value)
    moved += sum(v.size * v.dtype.itemsize for v in outs)
    out_specs = [pl.BlockSpec(memory_space=pltpu.VMEM)] * len(outs)
    alias = {}
    if whole is not None:
        alias = {len(first) + len(arrays): len(outs)}
        specs.append(pl.BlockSpec(memory_space=pl.ANY))
        arrays.append(whole)
        outs = [*outs, shape(whole.shape, whole.dtype)]
        out_specs.append(pl.BlockSpec(memory_space=pl.ANY))
    return pl.pallas_call(
        kernel,
        grid=(1,),
        out_shape=tuple(outs),
        in_specs=[pl.BlockSpec(memory_space=pltpu.SMEM)] * len(first) + specs,
        out_specs=tuple(out_specs),
        input_output_aliases=alias,
        scratch_shapes=list(scratch),
        compiler_params=pltpu.CompilerParams(vmem_limit_bytes=(24 if name in ROOMY else 56) << 20),
        cost_estimate=pl.CostEstimate(
            flops=flops, transcendentals=0, bytes_accessed=moved
        ),
        name=name,
    )(*first, *arrays)


def lanes(index, offset, size):
    return pl.ds(pl.multiple_of((index ^ offset) * size, size), size)


def rows_of(refs, low, high):
    return jnp.concatenate([ref[low:high, :] for ref in refs], axis=0)


def pack_kernel(attend_ref, *refs):
    smalls, (pair_ref, out_ref) = refs[:-2], refs[-2:]
    parts, block, width = attend_ref.shape
    for c in range(parts):
        out_ref[:block, c * width : (c + 1) * width] = attend_ref[c]
    size = smalls[0].shape[1]
    last = jnp.concatenate([pair_ref[0:1, :], pair_ref[1:2, :]], axis=1).astype(F32)
    last = jnp.concatenate([last, jnp.zeros((1, size - last.shape[1]), F32)], axis=1)
    rows = jnp.concatenate([ref[...].astype(F32) for ref in smalls] + [last], axis=0)
    out_ref[block:, :size] = rows.astype(BF16)
    out_ref[block:, size:] = jnp.zeros((8, parts * width - size), BF16)


def turn_kernel(expand_ref, shrink_ref, out_ref):
    block = expand_ref.shape[0]
    out_ref[:block, :] = expand_ref[...]
    out_ref[block:, :] = shrink_ref[...].T


def decode(order, head_block, index, first, start, size, wide_ref, expand_ref, attend_ref):
    total = jnp.zeros(attend_ref.shape, F32)
    for place, offset in enumerate(order):
        rows = first[place][start : start + 8, :size].astype(F32)
        wide_ref[:, place * size : (place + 1) * size] = rows
        expand_ref[:, lanes(index, offset, size)] = rows[6:7, :]
        flat = jnp.concatenate([rows[7:8, :head_block], rows[7:8, head_block : 2 * head_block]], 0)
        flat = jnp.concatenate(
            [flat, jnp.zeros((2, attend_ref.shape[1] - head_block), F32)], axis=1
        )
        flat = jnp.concatenate([flat, jnp.zeros((6, attend_ref.shape[1]), F32)], axis=0)
        total = total + pltpu.roll(flat, (index ^ offset) * head_block, 1)[:2]
    attend_ref[...] = total


def grad_order_kernel(order, count, scalars, cot_ref, keep_ref, *outs):
    index, tp = scalars[0], scalars[2]
    height, wide = outs[0].shape
    size = wide // len(order)
    for o in range(count):
        rows = pl.ds(pl.multiple_of((tp ^ o) * height, height), height)
        keep = keep_ref[rows, 0:1]
        for place, offset in enumerate(order):
            outs[o][:, place * size : (place + 1) * size] = (
                cot_ref[rows, lanes(index, offset, size)] * keep
            )


def project_kernel(order, block, head_block, scalars, x_ref, *refs):
    count = len(order)
    weights, refs = refs[:count], refs[count:]
    given, outs = refs[:-7], refs[-7:]
    normed_ref, query_ref, pair_ref, rows_ref = outs[:4]
    wide_ref, expand_ref, attend_ref = outs[4:]
    index, tp = scalars[0], scalars[2]
    q_len, wide = x_ref.shape
    size = wide // count
    for source, target in zip(given, outs[4:]):
        target[...] = source[...]
    if not given:
        decode(order, head_block, index, weights, block, size, wide_ref, expand_ref, attend_ref)
    width = query_ref.shape[1]
    weight = rows_of(weights, 0, block)
    step = min(q_len, 256)
    bias = jnp.concatenate(
        [attend_ref[0:1, :], jnp.zeros((1, width), F32), attend_ref[1:2, :]], axis=1
    )
    for start in range(0, q_len, step):
        rows = slice(start, start + step)
        value = x_ref[rows, :].astype(F32)
        mean = jnp.mean(value, axis=-1, keepdims=True)
        centered = value - mean
        inv = lax.rsqrt(jnp.mean(centered * centered, axis=-1, keepdims=True) + 1e-05)
        for place, offset in enumerate(order):
            plain = slice(place * size, (place + 1) * size)
            part = x_ref[rows, lanes(index, offset, size)].astype(F32)
            part = (part - mean) * inv * wide_ref[0:1, plain] + wide_ref[1:2, plain]
            normed_ref[rows, plain] = part.astype(BF16)
        made = dot(normed_ref[rows, :], weight, 1, 0) + bias
        query_ref[rows, :] = made[:, :width].astype(BF16)
        pair_ref[rows, :] = made[:, width:].astype(BF16)
    height = rows_ref.shape[0]
    mine = pl.ds(pl.multiple_of(tp * height, height), height)
    for place, offset in enumerate(order):
        plain = slice(place * size, (place + 1) * size)
        rows_ref[:, plain] = x_ref[mine, lanes(index, offset, size)]


def attend_kernel(heads, tq, tk, n_chunk, n_tp, scalars, lo_ref, q_ref, *refs):
    kv_refs = refs[:n_chunk]
    outs, refs = refs[n_chunk : n_chunk + n_tp], refs[n_chunk + n_tp :]
    lse_ref, qm_ref, acc_ref, m_ref, l_ref, mixed_ref = refs
    q_len, width = q_ref.shape
    ctx = scalars[1]
    lane = lax.broadcasted_iota(jnp.int32, (tq, width), 1)

    def tile(qi, carry):
        rows = pl.ds(pl.multiple_of(qi * tq, tq), tq)
        qv = q_ref[rows, :] * BF16(0.125)
        for h in range(heads):
            mine = (lane >= h * HD) & (lane < (h + 1) * HD)
            qm_ref[h * tq : (h + 1) * tq, :] = jnp.where(mine, qv, jnp.zeros_like(qv))
        acc_ref[...] = jnp.zeros_like(acc_ref)
        m_ref[...] = jnp.full(m_ref.shape, NEG, F32)
        l_ref[...] = jnp.zeros_like(l_ref)
        qbase = ctx * q_len + qi * tq
        qpos = qbase + lax.broadcasted_iota(jnp.int32, (1, tq), 1)
        lo = lo_ref[0:1, rows]
        lo_first = scalars[3 + qi]
        for c in range(n_chunk):
            kv = kv_refs[c]
            cbase = (ctx ^ c) * q_len

            def step(ki, carry, kv=kv, cbase=cbase):
                kb = cbase + ki * tk

                @pl.when((kb <= qbase + tq - 1) & (kb + tk - 1 >= lo_first))
                def _():
                    krows = pl.ds(pl.multiple_of(ki * tk, tk), tk)
                    k = kv[krows, 0:width]
                    vt = kv[krows, width : 2 * width].T
                    kpos = kb + lax.broadcasted_iota(jnp.int32, (tk, 1), 0)
                    ok = (kpos >= lo) & (kpos <= qpos)
                    ok = jnp.concatenate([ok] * heads, axis=1)
                    s = jnp.where(ok, dot(k, qm_ref[...], 1, 1), NEG)
                    m0 = m_ref[...]
                    m1 = jnp.maximum(m0, jnp.max(s, axis=0, keepdims=True))
                    p = jnp.exp(s - m1)
                    al = jnp.exp(m0 - m1)
                    l_ref[...] = l_ref[...] * al + jnp.sum(p, axis=0, keepdims=True)
                    m_ref[...] = m1
                    low = p.astype(BF16)
                    made = [
                        dot(vt[h * HD : (h + 1) * HD, :], low[:, h * tq : (h + 1) * tq], 1, 0)
                        for h in range(heads)
                    ]
                    acc_ref[...] = acc_ref[...] * al + jnp.concatenate(made, axis=1)

                return carry

            lax.fori_loop(0, q_len // tk, step, 0)
        lse = m_ref[...] + jnp.log(l_ref[...])
        out = acc_ref[...] / l_ref[...]
        for h in range(heads):
            cols = slice(h * tq, (h + 1) * tq)
            lse_ref[h : h + 1, rows] = lse[:, cols]
        out = jnp.concatenate([out[:, h * tq : (h + 1) * tq] for h in range(heads)], axis=0)
        mixed_ref[rows, :] = out.T.astype(BF16)
        return carry

    lax.fori_loop(0, q_len // tq, tile, 0)
    for o in range(n_tp):
        outs[o][...] = mixed_ref[lanes(scalars[2], o, q_len // n_tp), :]


def attend_back_kernel(heads, tq, tk, n_chunk, n_tp, scalars, lo_ref, lse_ref, q_ref, *refs):
    kv_refs, refs = refs[:n_chunk], refs[n_chunk:]
    mixed_refs, refs = refs[:n_tp], refs[n_tp:]
    gm_refs, refs = refs[:n_tp], refs[n_tp:]
    dq_ref, refs = refs[0], refs[1:]
    dkv_refs, refs = refs[:n_chunk], refs[n_chunk:]
    qm_ref, gom_ref, dqt_ref, acck_ref, accv_ref, go_ref, mixed_ref, row_ref = refs
    q_len, width = q_ref.shape
    ctx, tp = scalars[1], scalars[2]
    for o in range(n_tp):
        go_ref[lanes(tp, o, q_len // n_tp), :] = gm_refs[o][...]
        mixed_ref[lanes(tp, o, q_len // n_tp), :] = mixed_refs[o][...]
    lane = lax.broadcasted_iota(jnp.int32, (tq, width), 1)
    nq = q_len // tq

    def ready(qi, carry):
        rows = pl.ds(pl.multiple_of(qi * tq, tq), tq)
        qv = q_ref[rows, :] * BF16(0.125)
        gv = go_ref[rows, :]
        prod = (gv.astype(F32) * mixed_ref[rows, :].astype(F32)).T
        for h in range(heads):
            cols = slice(h * tq, (h + 1) * tq)
            mine = (lane >= h * HD) & (lane < (h + 1) * HD)
            qm_ref[qi, cols, :] = jnp.where(mine, qv, jnp.zeros_like(qv))
            gom_ref[qi, cols, :] = jnp.where(mine, gv, jnp.zeros_like(gv))
            row_ref[qi, 0:1, cols] = lse_ref[h : h + 1, rows]
            row_ref[qi, 1:2, cols] = jnp.sum(
                prod[h * HD : (h + 1) * HD, :], axis=0, keepdims=True
            )
        return carry

    lax.fori_loop(0, nq, ready, 0)
    dqt_ref[...] = jnp.zeros_like(dqt_ref)
    for c in range(n_chunk):
        kv = kv_refs[c]
        dkv = dkv_refs[c]
        cbase = (ctx ^ c) * q_len

        def step(ki, carry, kv=kv, dkv=dkv, cbase=cbase):
            kb = cbase + ki * tk
            krows = pl.ds(pl.multiple_of(ki * tk, tk), tk)
            live = [
                (kb <= ctx * q_len + (qi + 1) * tq - 1) & (kb + tk - 1 >= scalars[3 + qi])
                for qi in range(nq)
            ]
            some = functools.reduce(jnp.logical_or, live)

            @pl.when(jnp.logical_not(some))
            def _():
                dkv[krows, :] = jnp.zeros((tk, 2 * width), BF16)

            @pl.when(some)
            def _():
                acck_ref[...] = jnp.zeros_like(acck_ref)
                accv_ref[...] = jnp.zeros_like(accv_ref)
                k = kv[krows, 0:width]
                v = kv[krows, width : 2 * width]
                kt = k.T
                kpos = kb + lax.broadcasted_iota(jnp.int32, (tk, 1), 0)

                def tile(qi, carry):
                    qbase = ctx * q_len + qi * tq

                    @pl.when((kb <= qbase + tq - 1) & (kb + tk - 1 >= scalars[3 + qi]))
                    def _():
                        rows = pl.ds(pl.multiple_of(qi * tq, tq), tq)
                        qpos = qbase + lax.broadcasted_iota(jnp.int32, (1, tq), 1)
                        ok = (kpos >= lo_ref[0:1, rows]) & (kpos <= qpos)
                        ok = jnp.concatenate([ok] * heads, axis=1)
                        s = dot(k, qm_ref[qi], 1, 1)
                        dp = dot(v, gom_ref[qi], 1, 1)
                        p = jnp.where(ok, jnp.exp(s - row_ref[qi, 0:1, :]), 0.0)
                        ds = (p * (dp - row_ref[qi, 1:2, :])).astype(BF16)
                        accv_ref[...] += dot(p.astype(BF16), gom_ref[qi], 1, 0)
                        acck_ref[...] += dot(ds, qm_ref[qi], 1, 0)
                        for h in range(heads):
                            hs = slice(h * HD, (h + 1) * HD)
                            dqt_ref[hs, rows] += dot(
                                kt[hs, :], ds[:, h * tq : (h + 1) * tq], 1, 0
                            )

                    return carry

                lax.fori_loop(0, nq, tile, 0)
                dkv[krows, 0:width] = acck_ref[...].astype(BF16)
                dkv[krows, width : 2 * width] = accv_ref[...].astype(BF16)

            return carry

        lax.fori_loop(0, q_len // tk, step, 0)
    for qi in range(nq):
        rows = slice(qi * tq, (qi + 1) * tq)
        dq_ref[rows, :] = (dqt_ref[:, rows].T * 0.125).astype(BF16)


def attend_scratch(heads, tile, q_len, width):
    return [
        pltpu.VMEM((heads * tile, width), BF16),
        pltpu.VMEM((HD, heads * tile), F32),
        pltpu.VMEM((1, heads * tile), F32),
        pltpu.VMEM((1, heads * tile), F32),
        pltpu.VMEM((q_len, width), BF16),
    ]


def attend_back_scratch(heads, tile, span, q_len, width):
    return [
        pltpu.VMEM((q_len // tile, heads * tile, width), BF16),
        pltpu.VMEM((q_len // tile, heads * tile, width), BF16),
        pltpu.VMEM((width, q_len), F32),
        pltpu.VMEM((span, width), F32),
        pltpu.VMEM((span, width), F32),
        pltpu.VMEM((q_len, width), BF16),
        pltpu.VMEM((q_len, width), BF16),
        pltpu.VMEM((q_len // tile, 2, heads * tile), F32),
    ]


def normal(value):
    mean = jnp.mean(value, axis=-1, keepdims=True)
    centered = value - mean
    inv = lax.rsqrt(jnp.mean(centered * centered, axis=-1, keepdims=True) + 1e-05)
    return centered * inv, inv


def normal_back(grad_out, norm, inv, gain):
    grad = grad_out * gain
    centered = grad - jnp.mean(grad, axis=-1, keepdims=True)
    return inv * (centered - norm * jnp.mean(grad * norm, axis=-1, keepdims=True))


def merge_kernel(n_tp, order, scalars, rows_ref, wide_ref, weight_ref, *refs):
    mixed, (hidden_ref, normed_ref) = refs[:n_tp], refs[n_tp:]
    index, tp = scalars[0], scalars[2]
    hidden_ref[...] = rows_ref[...].astype(F32) + wide_ref[2:3, :]
    for o, ref in enumerate(mixed):
        weight = jnp.concatenate([weight_ref[index ^ p, tp ^ o] for p in order], axis=1)
        hidden_ref[...] += dot(ref[...], weight, 1, 0)
    norm, _ = normal(hidden_ref[...])
    normed_ref[...] = (norm * wide_ref[3:4, :] + wide_ref[4:5, :]).astype(BF16)


def dense_kernel(count, expand_ref, *refs):
    normed, refs = refs[:count], refs[count:]
    grads, refs = refs[:count], refs[count:]
    weights, outs = refs[: -4 * count - 1], refs[-4 * count - 1 :]
    acts, pres, normed_outs, mlp_outs = (outs[i * count : (i + 1) * count] for i in range(4))
    sum_ref = outs[-1]
    block = weights[0].shape[0] // 2
    height = normed[0].shape[0]
    hidden = expand_ref.shape[1]
    step = min(hidden, 512)
    value = jnp.concatenate([ref[...] for ref in normed], axis=0)
    grad = jnp.concatenate([ref[...] for ref in grads], axis=0)
    back = forth = None
    for start in range(0, hidden, step):
        cols = slice(start, start + step)
        expand = jnp.concatenate([ref[:block, cols] for ref in weights], axis=0)
        shrink = jnp.concatenate([ref[block:, cols] for ref in weights], axis=0)
        pre = dot(value, expand, 1, 0) + expand_ref[:, cols]
        square = pre * pre
        inner = jnp.tanh(0.7978845608028654 * (pre + 0.044715 * square * pre))
        act = (0.5 * pre * (1.0 + inner)).astype(BF16)
        slope = 0.5 * (1.0 + inner) + (0.5 * 0.7978845608028654) * pre * (
            1.0 - inner * inner
        ) * (1.0 + (3.0 * 0.044715) * square)
        low = (dot(grad, shrink, 1, 0) * slope).astype(BF16)
        sum_ref[:, cols] = jnp.sum(low.astype(F32), axis=0, keepdims=True)
        for i in range(count):
            rows = slice(i * height, (i + 1) * height)
            acts[i][:, cols] = act[rows]
            pres[i][:, cols] = low[rows]
        more = dot(low, expand, 1, 1)
        also = dot(act, shrink, 1, 1)
        back = more if back is None else back + more
        forth = also if forth is None else forth + also
    for i in range(count):
        rows = slice(i * height, (i + 1) * height)
        normed_outs[i][...] = back[rows].astype(BF16)
        mlp_outs[i][...] = forth[rows].astype(BF16)


def hidden_back_kernel(
    count, n_tp, order, scalars, grad_ref, hidden_ref, wide_ref, weight_ref, *refs
):
    parts, refs = refs[:count], refs[count:]
    mixed, refs = refs[:n_tp], refs[n_tp:]
    direct = len(order) > 1
    refs = refs[1:] if direct else refs
    back_ref, low_ref, sums_ref = refs[:3]
    outs, refs = refs[3 : 3 + n_tp], refs[3 + n_tp :]
    index, tp = scalars[0], scalars[2]
    total = total_of(parts)
    norm, inv = normal(hidden_ref[...])
    grad = grad_ref[...].astype(F32)
    back = grad + normal_back(total, norm, inv, wide_ref[3:4, :])
    back_ref[...] = back
    low = back.astype(BF16)
    low_ref[...] = low
    copies = []
    if direct:
        buffer_ref, made_ref, sems = refs
        values = jnp.concatenate([ref[...] for ref in mixed], axis=1)
        tall = made_ref.shape[1]
        for place, offset in enumerate(order):
            left = low[:, place * tall : (place + 1) * tall]
            made_ref[place] = dot(left, values, 0, 0).astype(BF16)
            copies.append(
                pltpu.make_async_copy(
                    made_ref.at[place],
                    buffer_ref.at[index ^ offset, pl.ds(2 * tall, tall), :],
                    sems.at[place],
                )
            )
            copies[-1].start()
    for o in range(n_tp):
        weight = jnp.concatenate([weight_ref[index ^ p, tp ^ o] for p in order], axis=1)
        outs[o][...] = dot(low, weight, 1, 1).astype(BF16)
    sums_ref[...] = jnp.concatenate(
        [jnp.sum(v, axis=0, keepdims=True) for v in (back, total * norm, total, grad)], axis=0
    )
    for copy in copies:
        copy.wait()


def outer_kernel(order, spans, scalars, *refs):
    out_ref = refs[-1]
    tall = out_ref.shape[1] // (len(spans) + 1)
    base = 0
    for many, more in spans:
        left, refs = refs[:many], refs[many:]
        right, refs = refs[:more], refs[more:]
        a = jnp.concatenate([ref[...] for ref in left], axis=0)
        b = jnp.concatenate([ref[...] for ref in right], axis=0)
        for place, offset in enumerate(order):
            made = dot(a[:, place * tall : (place + 1) * tall], b, 0, 0).astype(BF16)
            out_ref[scalars[0] ^ offset, base : base + tall, :] = made
        base += tall


def join_kernel(left_ref, right_ref, out_ref):
    total = left_ref[...].astype(F32) + right_ref[...].astype(F32)
    out_ref[...] = total.astype(out_ref.dtype)


def sum_of(ref):
    total = ref[0].astype(F32)
    for i in range(1, ref.shape[0]):
        total = total + ref[i].astype(F32)
    return total


def dense_total_kernel(in_ref, expand_ref, shrink_ref, *outs):
    block = expand_ref.shape[0]
    expand_ref[...] = in_ref[:block, :].astype(F32)
    shrink_ref[...] = in_ref[block : 2 * block, :].astype(F32).T
    width = outs[0].shape[1]
    for o, ref in enumerate(outs):
        ref[...] = in_ref[2 * block :, o * width : (o + 1) * width]


def attend_total_kernel(in_ref, out_ref):
    parts, _, width = out_ref.shape
    for c in range(parts):
        out_ref[c] = in_ref[:, c * width : (c + 1) * width].astype(F32)


def total_of(refs):
    total = refs[0][...].astype(F32)
    for ref in refs[1:]:
        total = total + ref[...].astype(F32)
    return total


def join_layer_kernel(order, scalars, left_ref, right_ref, hidden_ref, wide_ref, *refs):
    total = left_ref[...].astype(F32) + right_ref[...].astype(F32)
    refs[-2][...] = total.astype(BF16)
    value = (hidden_ref[...] + total_of(refs[:-2]) + wide_ref[5:6, :]).astype(BF16)
    size = value.shape[1] // len(order)
    for place, offset in enumerate(order):
        cols = slice(place * size, (place + 1) * size)
        refs[-1][:, lanes(scalars[0], offset, size)] = value[:, cols]


def input_kernel(order, count, scalars, rows_ref, back_ref, wide_ref, *refs):
    parts, refs = refs[:count], refs[count:]
    extra, outs = refs[: len(refs) - count], refs[len(refs) - count :]
    total = total_of(parts)
    norm, inv = normal(rows_ref[...].astype(F32))
    value = (back_ref[...] + normal_back(total, norm, inv, wide_ref[0:1, :])).astype(BF16)
    height, wide = value.shape
    size = wide // len(order)
    for o, out_ref in enumerate(outs):
        for place, offset in enumerate(order):
            cols = lanes(scalars[0], offset, size)
            out_ref[:height, cols] = value[:, place * size : (place + 1) * size]
        if extra:
            tall, width = extra[o].shape
            tall = tall * width // wide
            for j in range(wide // width):
                out_ref[height:, j * width : (j + 1) * width] = extra[o][
                    j * tall : (j + 1) * tall, :
                ]


def first_sums_kernel(order, scalars, x_ref, *refs):
    parts, out_ref = refs[:-1], refs[-1]
    height, wide = parts[0].shape
    size = wide // len(order)
    out_ref[...] = jnp.zeros_like(out_ref)
    for o, ref in enumerate(parts):
        rows = lanes(scalars[2], o, height)
        value = x_ref[rows, :].astype(F32)
        mean = jnp.mean(value, axis=-1, keepdims=True)
        centered = value - mean
        inv = lax.rsqrt(jnp.mean(centered * centered, axis=-1, keepdims=True) + 1e-05)
        for place, offset in enumerate(order):
            cols = slice(place * size, (place + 1) * size)
            part = ref[:, cols].astype(F32)
            norm = (x_ref[rows, lanes(scalars[0], offset, size)].astype(F32) - mean) * inv
            out_ref[0:1, cols] += jnp.sum(part * norm, axis=0, keepdims=True)
            out_ref[1:2, cols] += jnp.sum(part, axis=0, keepdims=True)


def place_kernel(count, height, scalars, *refs):
    parts, outs = refs[:count], refs[count:]
    wide = parts[0].shape[1]
    for o, ref in enumerate(parts):
        outs[0][lanes(scalars[2], o, height), :] = ref[:height, :]
    if len(outs) > 1:
        width = outs[1].shape[0]
        tall = parts[0].shape[0] - height
        total = total_of([ref.at[height:, :] for ref in parts])
        for j in range(wide // width):
            outs[1][:, j * tall : (j + 1) * tall] = total[:, j * width : (j + 1) * width].T


def project_back_kernel(block, order, n_pair, n_tp, scalars, normed_ref, dq_ref, *refs):
    joined, refs = refs[:n_pair], refs[n_pair:]
    weights, refs = refs[: len(order)], refs[len(order) :]
    outs, (pair_ref, sums_ref, outer_ref) = refs[:n_tp], refs[n_tp:]
    pair = total_of(joined).astype(BF16)
    pair_ref[...] = pair
    width = dq_ref.shape[1]
    weight = rows_of(weights, 0, block)
    height = outs[0].shape[0]
    for o in range(n_tp):
        rows = lanes(scalars[2], o, height)
        both = jnp.concatenate([dq_ref[rows, :], pair_ref[rows, :]], axis=1)
        outs[o][...] = dot(both, weight, 1, 1).astype(BF16)
    sums_ref[...] = jnp.concatenate(
        [
            jnp.sum(v, axis=0, keepdims=True)
            for v in (dq_ref[...].astype(F32), pair[:, width:].astype(F32))
        ],
        axis=0,
    )
    tall = outer_ref.shape[1]
    both = jnp.concatenate([dq_ref[...], pair], axis=1)
    for place, offset in enumerate(order):
        rows = slice(place * tall, (place + 1) * tall)
        outer_ref[scalars[0] ^ offset] = dot(normed_ref[:, rows], both, 0, 0).astype(BF16)


def add_kernel(left_ref, right_ref, out_ref):
    out_ref[...] = left_ref[...].astype(F32) + right_ref[...].astype(F32)


def small_kernel(order, head_block, n_tp, scalars, two_ref, four_ref, attend_ref, *refs):
    index = scalars[0]
    out_ref = refs[-1]
    hidden = total_of(refs[:-1])
    size = out_ref.shape[2]
    attend = jnp.concatenate([attend_ref[...], jnp.zeros((6, attend_ref.shape[1]), F32)], axis=0)
    for place, offset in enumerate(order):
        cols = slice(place * size, (place + 1) * size)
        block = index ^ offset
        turned = pltpu.roll(attend, attend.shape[1] - block * head_block, 1)
        last = jnp.concatenate(
            [
                turned[0:1, :head_block],
                turned[1:2, :head_block],
                jnp.zeros((1, size - 2 * head_block), F32),
            ],
            axis=1,
        )
        mine = jnp.zeros((1, size), F32)
        for j in range(len(order)):
            mine = mine + jnp.where(block == j, hidden[:, j * size : (j + 1) * size], 0.0)
        made = jnp.concatenate([two_ref[:, cols], four_ref[:, cols], mine, last], axis=0)
        for o in range(n_tp):
            out_ref[block * n_tp + o] = made


def small_total_kernel(n_tp, scalars, in_ref, *outs):
    total = sum_of(in_ref)
    local = in_ref[scalars[2]]
    for i in range(1, in_ref.shape[0] // n_tp):
        local = local + in_ref[i * n_tp + scalars[2]]
    for i in range(6):
        outs[i][...] = total[i : i + 1, :]
    outs[6][...] = local[6:7, :]
    size = outs[7].shape[1]
    outs[7][...] = jnp.concatenate([local[7:8, :size], local[7:8, size : 2 * size]], axis=0)


def after(value, *others):
    return lax.optimization_barrier((value, *others))[0]


def body(
    sizes,
    layer_input,
    cotangent,
    segment_ids,
    norm1_gain,
    norm1_bias,
    attend_weight,
    attend_bias,
    merge_weight,
    merge_bias,
    norm2_gain,
    norm2_bias,
    expand_weight,
    expand_bias,
    shrink_weight,
    shrink_bias,
):
    n_dp, n_ctx, n_tp = sizes
    group = n_dp * n_ctx
    seqs, q_len, wide = layer_input.shape
    assert seqs == 1
    block = wide // group
    width = attend_weight.shape[2]
    heads = width // HD
    hidden_width = expand_weight.shape[1]
    height = q_len // n_tp
    bias_block = expand_bias.shape[0]
    head_block = attend_bias.shape[1]
    tile = min(256, q_len)
    direct = (n_dp, n_ctx) == (2, 4) and block % 128 == 0
    direct = direct and bias_block == block and 2 * head_block <= block
    order = [0, 2, 4, 6, 1, 3, 5, 7] if direct else [0]
    ctx = lax.axis_index("ctx")
    tp = lax.axis_index("tp")
    me = lax.axis_index("dp") * n_ctx + ctx if direct else 0 * ctx
    plane = ("dp", "ctx")

    def plane_swap(value, offset):
        return lax.ppermute(value, plane, [(i, i ^ offset) for i in range(group)])

    def ctx_swap(value, offset):
        return lax.ppermute(value, "ctx", [(i, i ^ offset) for i in range(n_ctx)])

    def tp_swap(value, offset):
        return lax.ppermute(value, "tp", [(i, i ^ offset) for i in range(n_tp)])

    def with_cores(even):
        return even + [ctx_swap(v, 1) for v in even]

    def tp_gather(value):
        return [value] + [tp_swap(value, o) for o in range(1, n_tp)]

    def tp_relay(value):
        parts = [value, tp_swap(value, 1)]
        for step in (2 ** i for i in range(1, n_tp.bit_length() - 1)):
            far = tp_swap(value, step)
            parts += [far, tp_swap(far, 1)] + [tp_swap(value, o) for o in range(step + 2, 2 * step)]
        return parts

    def tp_exchange(parts):
        return [parts[0]] + [tp_swap(parts[o], o) for o in range(1, n_tp)]

    seg_all = segment_ids[0]
    seg_query = lax.dynamic_slice_in_dim(seg_all, ctx * q_len, q_len, 0)
    lows = jnp.sum(
        (seg_all[:, None] < seg_query[None, :]).astype(jnp.int32), axis=0, keepdims=True
    )
    place = jnp.stack([me, ctx, tp]).astype(jnp.int32)
    limits = jnp.concatenate([place, lows[0, ::tile]], axis=0)
    keep = jnp.broadcast_to((seg_query > 0).astype(BF16)[:, None], (q_len, 128))

    smalls = (
        norm1_gain,
        norm1_bias,
        merge_bias,
        norm2_gain,
        norm2_bias,
        shrink_bias,
        expand_bias,
    )
    if direct:
        (pack,) = call(
            pack_kernel,
            "pack",
            None,
            [jnp.swapaxes(attend_weight, 0, 1)]
            + [jnp.reshape(v, (1, block)) for v in smalls]
            + [attend_bias],
            [shape((block + 8, 3 * width), BF16)],
        )
        far = [plane_swap(pack, o) for o in order[1:4]]
        first = with_cores([after(v, limits, keep) for v in [pack] + far])
        merge_all = lax.all_gather(merge_weight, ("dp", "ctx", "tp"), axis=0)
        merge_all = jnp.reshape(merge_all, (group, n_tp, width, block))
        given = []
    else:

        def whole(value, axis):
            return lax.all_gather(value, plane, axis=axis, tiled=True)

        first = [jnp.reshape(whole(attend_weight, 0), (wide, 3 * width))]
        merge_all = whole(lax.all_gather(merge_weight, "tp", axis=0), 2)[None]
        dense_all = [jnp.concatenate([whole(expand_weight, 0), whole(shrink_weight.T, 0)], 0)]
        wide_rows = whole(jnp.stack(smalls[:6]), 1).astype(F32)
        given = [
            jnp.pad(wide_rows, ((0, 2), (0, 0))),
            whole(expand_bias, 0).astype(F32)[None],
            whole(attend_bias, 1).astype(F32),
        ]
    span = block if direct else wide

    normed1, query, pair, input_rows, wide_rows, expand_add, attend_add = call(
        functools.partial(project_kernel, order, span, head_block),
        "project",
        place,
        [layer_input[0], *first, *given],
        [
            shape((q_len, wide), BF16),
            shape((q_len, width), BF16),
            shape((q_len, 2 * width), BF16),
            shape((height, wide), BF16),
            shape((8, wide), F32),
            shape((1, hidden_width), F32),
            shape((2, width), F32),
        ],
        flops=6 * q_len * wide * width,
    )
    grad_rows = call(
        functools.partial(grad_order_kernel, order, n_tp),
        "order_grad",
        place,
        [after(cotangent[0], pair), keep],
        [shape((height, wide), BF16)] * n_tp,
    )
    ready = [grad_rows[0], limits]
    if direct:
        (dense_rows,) = call(
            turn_kernel,
            "turn",
            None,
            [after(expand_weight, pair), shrink_weight],
            [shape((2 * block, hidden_width), BF16)],
        )
        ready.append(dense_rows)
    near = [pair] + [ctx_swap(pair, o) for o in range(2, n_ctx, 2)]
    pairs = []
    for value in near:
        if pairs:
            value = after(value, *ready)
        pairs += [value, ctx_swap(value, 1)]
    if direct:
        dense_y = plane_swap(dense_rows, 4)
        dense_core = ctx_swap(dense_rows, 1)
        pairs[-1] = after(pairs[-1], dense_y, dense_core)
        dense_x, dense_xy = (plane_swap(after(dense_rows, near[1]), o) for o in (2, 6))
    out = call(
        functools.partial(attend_kernel, heads, tile, min(512, q_len), n_ctx, n_tp),
        "attention",
        limits,
        [lows, query, *pairs],
        [shape((height, width), BF16)] * n_tp + [shape((heads, q_len), F32)],
        attend_scratch(heads, tile, q_len, width),
        flops=4 * q_len * q_len * n_ctx * width,
    )
    mixed, lse = out[:n_tp], out[n_tp]
    mixed_rows = tp_exchange(mixed)
    hidden, normed2 = call(
        functools.partial(merge_kernel, n_tp, order),
        "merge",
        place,
        [input_rows, wide_rows, merge_all, *mixed_rows],
        [shape((height, wide), F32), shape((height, wide), BF16)],
        flops=2 * height * wide * wide,
    )

    if direct:
        dense_far = [after(v, normed2) for v in (dense_x, dense_y, dense_xy)]
        dense_all = [dense_rows, *dense_far, dense_core] + [ctx_swap(v, 1) for v in dense_far]
    normed_all = tp_relay(normed2)
    normed_all[2] = after(normed_all[2], normed_all[1])
    picks = [[o for o in range(n_tp) if o % 4 in (0, 2)], [o for o in range(n_tp) if o % 4 in (1, 3)]]
    acts, pres, parts, mlps = ([None] * n_tp for _ in range(4))
    sums = []
    for pick in picks:
        count = len(pick)
        if sums:
            normed_all[3] = after(normed_all[3], sums[0])
        out = call(
            functools.partial(dense_kernel, count),
            "dense",
            None,
            [expand_add]
            + [normed_all[o] for o in pick]
            + [grad_rows[o] for o in pick]
            + dense_all,
            [shape((height, hidden_width), BF16)] * (2 * count)
            + [shape((height, wide), BF16)] * (2 * count)
            + [shape((1, hidden_width), F32)],
            flops=8 * count * height * wide * hidden_width,
        )
        for i, o in enumerate(pick):
            acts[o], pres[o], parts[o], mlps[o] = (out[j * count + i] for j in range(4))
        sums.append(out[-1])
    grad_parts = tp_exchange(parts)
    dense_outer = None
    if direct:
        (dense_outer,) = call(
            functools.partial(outer_kernel, order, [(n_tp, n_tp)] * 2),
            "dense_outer",
            place,
            [*normed_all, *pres, *grad_rows, *acts],
            [shape((group, 3 * block, hidden_width), BF16)],
            flops=4 * wide * hidden_width * q_len,
        )
        grad_parts[2] = after(grad_parts[2], dense_outer)
    (grad_near,) = call(
        add_kernel, "add", None, [grad_parts[0], grad_parts[2]], [shape((height, wide), F32)]
    )
    grad_parts = [grad_near] + [grad_parts[o] for o in range(1, n_tp) if o != 2]
    out = call(
        functools.partial(hidden_back_kernel, len(grad_parts), n_tp, order),
        "hidden_back",
        place,
        [grad_rows[0], hidden, wide_rows, merge_all, *grad_parts, *mixed_rows],
        [
            shape((height, wide), F32),
            shape((height, wide), BF16),
            shape((4, wide), F32),
        ]
        + [shape((height, width), BF16)] * n_tp,
        [pltpu.VMEM((group, block, wide), BF16), pltpu.SemaphoreType.DMA((group,))]
        if direct
        else [],
        flops=2 * height * wide * wide,
        whole=dense_outer,
    )
    if direct:
        dense_outer = out[-1]
        out = out[:-1]
    hidden_grad, grad_attn, four, grad_mixed = out[0], out[1], out[2], tp_exchange(out[3:])
    mlps = tp_exchange([mlps[0]] + [after(v, hidden_grad) for v in mlps[1:]])

    out = call(
        functools.partial(attend_back_kernel, heads, tile, tile, n_ctx, n_tp),
        "attention_back",
        limits,
        [lows, lse, query, *pairs, *mixed, *grad_mixed],
        [shape((q_len, width), BF16)] + [shape((q_len, 2 * width), BF16)] * n_ctx,
        attend_back_scratch(heads, tile, tile, q_len, width),
        flops=10 * q_len * q_len * n_ctx * width,
    )
    grad_query, grad_pairs = out[0], out[1:]
    joined = []
    for o in reversed(range(0, n_ctx, 2)):
        if joined:
            other = after(ctx_swap(grad_pairs[o + 1], 1), joined[-1])
            (total,) = call(
                join_kernel, "join", None, [other, grad_pairs[o]], [shape(other.shape, BF16)]
            )
        else:
            other = ctx_swap(after(grad_pairs[o + 1], *mlps), 1)
            total, layer_part = call(
                functools.partial(join_layer_kernel, order),
                "join_layer",
                place,
                [other, grad_pairs[o], hidden, wide_rows, *mlps],
                [shape(other.shape, BF16), shape((height, wide), BF16)],
            )
        joined.append(total)
    joined = joined[::-1]
    layer_parts = tp_relay(layer_part)
    joined = [joined[0]] + [ctx_swap(v, 2 * i) for i, v in enumerate(joined) if i]
    joined[-1] = after(joined[-1], layer_parts[1], layer_parts[2])
    out = call(
        functools.partial(project_back_kernel, span, order, len(joined), n_tp),
        "project_back",
        place,
        [normed1, grad_query, *joined, *first],
        [shape((height, wide), BF16)] * n_tp
        + [
            shape((q_len, 2 * width), BF16),
            shape((2, width), F32),
            shape((len(order), span, 3 * width), BF16),
        ],
        flops=12 * q_len * wide * width,
    )
    normed1_parts, (grad_pair, attend_sums, attend_outer) = out[:n_tp], out[n_tp:]
    (two,) = call(
        functools.partial(first_sums_kernel, order),
        "first_sums",
        place,
        [layer_input[0], *normed1_parts],
        [shape((2, wide), F32)],
    )
    normed1_parts = tp_exchange(normed1_parts)

    def placed(parts, outs=()):
        return call(
            functools.partial(place_kernel, n_tp, height),
            "place",
            place,
            parts,
            [shape((q_len, wide), BF16), *outs],
        )

    (layer_output,) = placed(layer_parts)

    def scattered(value):
        flat = jnp.reshape(value, (-1, value.shape[-1]))
        return lax.psum_scatter(flat, plane, scatter_dimension=0, tiled=True)

    if direct:
        attend_part = scattered(attend_outer)
        out = call(
            dense_total_kernel,
            "dense_total",
            None,
            [after(scattered(dense_outer), grad_pair)],
            [shape((block, hidden_width), F32), shape((hidden_width, block), F32)]
            + [shape((block, width), BF16)] * n_tp,
        )
        grad_expand, grad_shrink, merge_parts = out[0], out[1], out[2:]
        normed1_parts[-1] = after(normed1_parts[-1], grad_expand, two, layer_output)
    else:
        merge_parts = []
    low = block * width // wide if direct else 0
    input_parts = call(
        functools.partial(input_kernel, order, n_tp),
        "input_back",
        place,
        [input_rows, hidden_grad, wide_rows, *normed1_parts, *merge_parts],
        [shape((height + low, wide), BF16)] * n_tp,
    )
    input_part = input_parts[0]
    input_parts = tp_exchange(input_parts)

    if direct:
        (grad_attend,) = call(
            attend_total_kernel,
            "attend_total",
            None,
            [attend_part],
            [shape((3, block, width), F32)],
        )
        (small,) = call(
            functools.partial(small_kernel, order, head_block, n_tp),
            "small",
            place,
            [two, four, attend_sums, *sums],
            [shape((group * n_tp, 8, block), F32)],
        )
        input_parts[-1] = after(input_parts[-1], grad_attend)
        input_grad, grad_merge = placed(input_parts, [shape((width, block), F32)])
        table = call(
            functools.partial(small_total_kernel, n_tp),
            "small_total",
            place,
            [
                after(
                    lax.all_to_all(after(small, input_part), ("dp", "ctx", "tp"), 0, 0), input_grad
                )
            ],
            [shape((1, block), F32)] * 7 + [shape((2, head_block), F32)],
        )
        rows = [jnp.reshape(v, (block,)) for v in table[:7]]
        expand_sum, attend_sum = rows[6], table[7]
        grad_attend = jnp.swapaxes(grad_attend, 0, 1)
    else:

        def cut(value, axis):
            return lax.psum_scatter(value, plane, scatter_dimension=axis, tiled=True)

        def outer_of(left, right):
            return cut(
                dot(jnp.concatenate(left), jnp.concatenate(right), 0, 0).astype(BF16), 0
            ).astype(F32)

        grad_expand = outer_of(normed_all, pres)
        grad_shrink = outer_of(grad_rows, acts).T
        grad_merge = outer_of([grad_attn], [jnp.concatenate(mixed_rows, axis=1)]).astype(BF16)
        grad_merge = [grad_merge[:, o * width : (o + 1) * width] for o in range(n_tp)]
        grad_merge = sum(v.astype(F32) for v in tp_exchange(grad_merge)).T
        grad_attend = jnp.reshape(cut(attend_outer[0], 0).astype(F32), (block, 3, width))
        (input_grad,) = placed(input_parts)
        table = lax.psum(cut(jnp.concatenate([two, four], axis=0), 1), "tp")
        rows = [table[i] for i in range(6)]
        expand_sum = cut(sum(sums)[0], 0)
        attend_sum = cut(attend_sums, 1)
    return (
        layer_output[None],
        input_grad[None],
        rows[0],
        rows[1],
        grad_attend,
        attend_sum,
        grad_merge,
        rows[2],
        rows[3],
        rows[4],
        grad_expand,
        expand_sum,
        grad_shrink,
        rows[5],
    )


def solution(mesh):
    sizes = (mesh.shape["dp"], mesh.shape["ctx"], mesh.shape["tp"])
    return jax.shard_map(
        functools.partial(body, sizes),
        mesh=mesh,
        in_specs=(
            P("dp", "ctx", None),
            P("dp", "ctx", None),
            P("dp", None),
            P(("dp", "ctx")),
            P(("dp", "ctx")),
            P(("dp", "ctx"), None, "tp"),
            P(None, ("tp", "dp", "ctx")),
            P("tp", ("dp", "ctx")),
            P(("dp", "ctx")),
            P(("dp", "ctx")),
            P(("dp", "ctx")),
            P(("dp", "ctx"), "tp"),
            P(("tp", "dp", "ctx")),
            P("tp", ("dp", "ctx")),
            P(("dp", "ctx")),
        ),
        out_specs=(
            P("dp", "ctx", None),
            P("dp", "ctx", None),
            P(("dp", "ctx")),
            P(("dp", "ctx")),
            P(("dp", "ctx"), None, "tp"),
            P(None, ("tp", "dp", "ctx")),
            P("tp", ("dp", "ctx")),
            P(("dp", "ctx")),
            P(("dp", "ctx")),
            P(("dp", "ctx")),
            P(("dp", "ctx"), "tp"),
            P(("tp", "dp", "ctx")),
            P("tp", ("dp", "ctx")),
            P(("dp", "ctx")),
        ),
        check_vma=False,
    )
```
